32 devices in a mesh: img: 16 (over z, x, core), row: 2 (over y).
Axes of the slice: x: 2, y: 2, z: 4, core: 2. Of those that a mesh axis runs over, the one named last changes fastest.
Arguments:
- llm_hidden: bfloat16 [8192, 6656], P('img', 'row'), may hold values from -96 to 96
- slot_start: int32 [16], P('img'), may hold values from 0 to 448
- image_group: int32 [16], replicated, may hold values from 0 to 15, each once
- timesteps: int32 [16], P('img'), may hold values from 0 to 999
- latents: float32 [16, 4, 16, 128], P('img', None, 'row'), may hold values from -6 to 6
- noise: float32 [16, 4, 16, 128], P('img', None, 'row'), may hold values from -6 to 6
- kv_weight: bfloat16 [6656, 640], P('row'), may hold values from -0.078125 to 0.078125
- in_weight: bfloat16 [3, 3, 320, 4], replicated, may hold values from -1 to 1
- res_weight: bfloat16 [3, 3, 320, 320], replicated, may hold values from -0.109375 to 0.109375
- query_weight: bfloat16 [320, 320], replicated, may hold values from -0.3125 to 0.3125
- out_weight: bfloat16 [320, 320], replicated, may hold values from -0.3125 to 0.3125
- cotangent: bfloat16 [16, 320, 16, 128], P('img', None, 'row'), may hold values from -6 to 6
Outputs:
- block_out: bfloat16 [16, 320, 16, 128], P('img', None, 'row')
- grad_hidden: bfloat16 [8192, 6656], P('img', 'row')
- grad_kv_weight: bfloat16 [6656, 640], P('row')
- grad_res_weight: bfloat16 [3, 3, 320, 320], replicated
- grad_query_weight: bfloat16 [320, 320], replicated
- grad_out_weight: bfloat16 [320, 320], replicated
The draws below stay inside these ranges and needn't reach their ends.
Inputs may be any that keep to these rules, and one draw needn't show every extreme that they name: `slot_start`: each image's 64 condition rows lie inside its own sequence of 512 tokens. `image_group`: every group denoises exactly one image.
All inputs are finite; a program needn't handle non-finite values.
Results may differ from the reference program's by a relative error of at most 0.035.
The reference program's roundings to bfloat16 on the way count: a program that leaves them out, or rounds other values in their place, can miss the bound.
Values may be sent and summed in bfloat16 or wider, within the bound.
No kernel may reach another device: no remote copies, remote signals or barrier semaphores. Data moves between devices by JAX's collectives and lax.ppermute only.
A program may use at most 128 MiB of HBM per device.

```python
import math
import jax
import jax.numpy as jnp
from jax import lax

COND = 6656
CHANNELS = 320
HEAD_DIM = 64
LAT_CH = 4
SLOTS = 64
WIDTH = 128
SEQ_DEV = 512
IMAGES = 16
TOKENS = 8192
HEIGHT = 16


def draw_llm_hidden(key, part):
    base_key = jax.random.fold_in(jax.random.fold_in(key, 11), 0)
    entries = jax.random.normal(base_key, (TOKENS, COND), jnp.float32)
    entries = jnp.clip(entries, -6.0, 6.0)
    return entries.astype(jnp.bfloat16)


def place_ends(array, own_key, smallest, top_value):
    extent = array.shape
    index_at = [jax.random.randint(jax.random.fold_in(own_key, axis), (), 0, extent[axis]) for axis in range(len(extent))]
    array = array.at[tuple(index_at)].set(smallest)
    longest = extent.index(max(extent))
    index_at[longest] = (index_at[longest] + 1) % extent[longest]
    return array.at[tuple(index_at)].set(top_value)


def strengthened(array, own_key, source, target, parts, factor):
    owner, partner = [(jnp.arange(array.shape[dim]) // (array.shape[dim] // parts)).reshape([-1 if axis == dim else 1 for axis in range(array.ndim)]) for dim in (source, target)]
    chosen = jax.random.permutation(own_key, parts)[partner]
    strong = (owner == chosen) | (owner == (partner + parts // 2) % parts)
    return jnp.where(strong, factor * array, array)


def level_of(key, extent, shards, smallest, largest):
    loudness, own = 1.0, jax.random.fold_in(key, 6)
    for position, parts in shards:
        draws = jnp.exp(jax.random.uniform(jax.random.fold_in(own, position), (parts,), jnp.float32, smallest / len(shards), largest / len(shards)))
        loudness = loudness * jnp.repeat(draws, extent[position] // parts).reshape([-1 if axis == position else 1 for axis in range(len(extent))])
    return loudness


def scatter_about(rng, extent, width, limit, shards=(), kind=jnp.bfloat16):
    result = width * jax.random.normal(rng, extent, jnp.float32)
    if shards:
        result = result * level_of(rng, extent, shards, -0.22, 0.18)
    return jnp.clip(result, -limit, limit).astype(kind)


def noise_with(rng, dims, deviation, limit, pieces, heavy, kind=jnp.bfloat16):
    array = deviation * jax.random.normal(rng, dims, jnp.float32)
    if pieces:
        array = array * level_of(rng, dims, pieces, -0.22, 0.18)
    return jnp.clip(strengthened(array, jax.random.fold_in(rng, 3), *heavy), -limit, limit).astype(kind)


def setup_inputs(seed: int = 0) -> dict:
    seeds = jax.random.split(jax.random.key(seed), 13)
    llm_hidden = draw_llm_hidden(jax.random.fold_in(seeds[12], 71), 0)
    slot_start = place_ends(jax.random.randint(seeds[1], (IMAGES,), 0, SEQ_DEV - SLOTS + 1), jax.random.fold_in(seeds[1], 1), 0, SEQ_DEV - SLOTS).astype(jnp.int32)
    image_group = jax.random.permutation(seeds[2], IMAGES).astype(jnp.int32)
    timesteps = place_ends(jax.random.randint(seeds[3], (IMAGES,), 0, 1000), jax.random.fold_in(seeds[3], 1), 0, 999).astype(jnp.int32)
    latents = scatter_about(seeds[4], (IMAGES, LAT_CH, HEIGHT, WIDTH), 1.0, 6.0, ((0, 16), (2, 2)), jnp.float32)
    noise = scatter_about(seeds[5], (IMAGES, LAT_CH, HEIGHT, WIDTH), 1.0, 6.0, ((0, 16), (2, 2)), jnp.float32)
    kv_weight = scatter_about(seeds[6], (COND, 2 * CHANNELS), COND ** -0.5, 0.078125, ((0, 2),))
    in_weight = scatter_about(seeds[7], (3, 3, CHANNELS, LAT_CH), (9 * LAT_CH) ** -0.5, 1.0)
    res_weight = scatter_about(seeds[8], (3, 3, CHANNELS, CHANNELS), (9 * CHANNELS) ** -0.5, 0.109375)
    query_weight = scatter_about(seeds[9], (CHANNELS, CHANNELS), CHANNELS ** -0.5, 0.3125)
    out_weight = scatter_about(seeds[10], (CHANNELS, CHANNELS), CHANNELS ** -0.5, 0.3125)
    cotangent = noise_with(seeds[11], (IMAGES, CHANNELS, HEIGHT, WIDTH), 1.0, 6.0, ((0, 16), (2, 2)), (0, 1, 16, 2.0))
    return {"llm_hidden": llm_hidden, "slot_start": slot_start, "image_group": image_group, "timesteps": timesteps, "latents": latents, "noise": noise, "kv_weight": kv_weight, "in_weight": in_weight, "res_weight": res_weight, "query_weight": query_weight, "out_weight": out_weight, "cotangent": cotangent}


def weighted_product(form, left, right):
    return jnp.einsum(form, left.astype(jnp.float32), right.astype(jnp.float32))

def noise_levels():
    plan = jnp.linspace(0.00085 ** 0.5, 0.012 ** 0.5, 1000, dtype=jnp.float32) ** 2
    return jnp.exp(jnp.cumsum(jnp.log(1.0 - plan)))

def noisy_input(latent, noise_one, timestep):
    levels = noise_levels()
    picked = jnp.sum(jnp.where(jnp.arange(levels.shape[0]) == timestep, levels, 0.0))
    return (jnp.sqrt(picked) * latent + jnp.sqrt(1.0 - picked) * noise_one).astype(jnp.bfloat16)

def time_shift(timestep, channel_total):
    half_count = channel_total // 2
    frequency = jnp.exp(-math.log(10000.0) * jnp.arange(half_count, dtype=jnp.float32) / half_count)
    angles = timestep.astype(jnp.float32) * frequency
    return jnp.concatenate([jnp.cos(angles), jnp.sin(angles)])

def pad_columns(field):
    return jnp.pad(field, ((0, 0), (0, 0), (1, 1)))

def convolve(padded, weight, row_count, col_count):
    running = jnp.zeros((weight.shape[2], row_count * col_count), jnp.float32)
    for row_tap in range(3):
        for col_tap in range(3):
            window = padded[:, row_tap:row_tap + row_count, col_tap:col_tap + col_count].reshape(padded.shape[0], row_count * col_count)
            running = running + jnp.dot(weight[row_tap, col_tap], window, preferred_element_type=jnp.float32)
    return running

def filter_grad(padded, upstream, row_count, col_count):
    tap_list = []
    for row_tap in range(3):
        for col_tap in range(3):
            window = padded[:, row_tap:row_tap + row_count, col_tap:col_tap + col_count].reshape(padded.shape[0], row_count * col_count)
            tap_list.append(lax.dot_general(upstream, window, (((1,), (1,)), ((), ())), preferred_element_type=jnp.float32))
    return jnp.stack(tap_list).reshape(3, 3, upstream.shape[0], padded.shape[0])

def block_pass(noisy, timestep, group_kv, upstream, in_weight, res_weight, query_weight, out_weight):
    channel_total = in_weight.shape[2]
    row_count, col_count = (noisy.shape[1], noisy.shape[2])
    latent_cell_count = row_count * col_count
    condition_slot_count = group_kv.shape[0]
    head_count = channel_total // HEAD_DIM
    logit_scale = HEAD_DIM ** (-0.5)
    noisy_pad = pad_columns(jnp.pad(noisy, ((0, 0), (1, 1), (0, 0))))
    first = convolve(noisy_pad, in_weight, row_count, col_count)
    hidden_act = jax.nn.silu(first + time_shift(timestep, channel_total)[:, None]).astype(jnp.bfloat16)
    act_pad = pad_columns(jnp.pad(hidden_act.reshape(channel_total, row_count, col_count), ((0, 0), (1, 1), (0, 0))))
    residual = (first + convolve(act_pad, res_weight, row_count, col_count)).astype(jnp.bfloat16)
    query = jnp.dot(query_weight, residual, preferred_element_type=jnp.float32).astype(jnp.bfloat16)
    query_per_head = query.reshape(head_count, HEAD_DIM, latent_cell_count)
    key_matrix = group_kv[:, :channel_total].reshape(condition_slot_count, head_count, HEAD_DIM)
    value_matrix = group_kv[:, channel_total:].reshape(condition_slot_count, head_count, HEAD_DIM)
    score_matrix = weighted_product('isf,tis->itf', query_per_head, key_matrix) * logit_scale
    softmax_full = jax.nn.softmax(score_matrix, axis=1)
    softmax_reduced_precision = softmax_full.astype(jnp.bfloat16)
    attention_output = weighted_product('cuo,ucb->cbo', softmax_reduced_precision, value_matrix).astype(jnp.bfloat16).reshape(channel_total, latent_cell_count)
    block_out = (residual.astype(jnp.float32) + jnp.dot(out_weight, attention_output, preferred_element_type=jnp.float32)).astype(jnp.bfloat16)
    upstream = upstream.reshape(channel_total, latent_cell_count)
    out_grad = lax.dot_general(upstream, attention_output, (((1,), (1,)), ((), ())), preferred_element_type=jnp.float32)
    grad_att = lax.dot_general(out_weight, upstream, (((0,), (0,)), ((), ())), preferred_element_type=jnp.float32).astype(jnp.bfloat16)
    head_gradient = grad_att.reshape(head_count, HEAD_DIM, latent_cell_count)
    probability_gradient = weighted_product('isf,tis->itf', head_gradient, value_matrix)
    score_gradient = (logit_scale * softmax_full * (probability_gradient - lax.optimization_barrier(jnp.sum(softmax_full * probability_gradient, axis=1, keepdims=True)))).astype(jnp.bfloat16)
    query_gradient = weighted_product('cuo,ucb->cbo', score_gradient, key_matrix).astype(jnp.bfloat16).reshape(channel_total, latent_cell_count)
    key_gradient = weighted_product('exv,ewv->xew', score_gradient, query_per_head).reshape(condition_slot_count, channel_total)
    value_gradient = weighted_product('exv,ewv->xew', softmax_reduced_precision, head_gradient).reshape(condition_slot_count, channel_total)
    grad_kv = jnp.concatenate([key_gradient, value_gradient], axis=1)
    query_grad = lax.dot_general(query_gradient, residual, (((1,), (1,)), ((), ())), preferred_element_type=jnp.float32)
    grad_resid = (upstream.astype(jnp.float32) + lax.dot_general(query_weight, query_gradient, (((0,), (0,)), ((), ())), preferred_element_type=jnp.float32)).astype(jnp.bfloat16)
    res_grad = filter_grad(act_pad, grad_resid, row_count, col_count)
    return (block_out.reshape(channel_total, row_count, col_count), grad_kv, res_grad, query_grad, out_grad)

def reference(llm_hidden, slot_start, image_group, timesteps, latents, noise, kv_weight, in_weight, res_weight, query_weight, out_weight, cotangent):
    image_count = slot_start.shape[0]
    seq_tokens = llm_hidden.shape[0] // image_count
    offsets = jnp.arange(image_count, dtype=jnp.int32) * seq_tokens + slot_start.astype(jnp.int32)

    def select_rows(first_row):
        return lax.dynamic_slice_in_dim(llm_hidden, first_row, SLOTS, 0)
    condition = jax.vmap(select_rows)(offsets)
    kv_rows = weighted_product('isf,fk->isk', condition, kv_weight).astype(jnp.bfloat16)
    group_kv = jnp.zeros_like(kv_rows).at[image_group].set(kv_rows)
    channel_total = in_weight.shape[2]
    zero_res = jnp.zeros((3, 3, channel_total, channel_total), jnp.float32)
    zero_square = jnp.zeros((channel_total, channel_total), jnp.float32)

    def per_group(running, scan_items):
        latent, noise_one, timestep, kv_one, upstream = scan_items
        noisy = noisy_input(latent, noise_one, timestep)
        block_out, grad_kv, res_grad, query_grad, out_grad = block_pass(noisy, timestep, kv_one, upstream, in_weight, res_weight, query_weight, out_weight)
        return ((running[0] + res_grad, running[1] + query_grad, running[2] + out_grad), (block_out, grad_kv.astype(jnp.bfloat16)))
    running, (block_outs, grad_groups) = lax.scan(per_group, (zero_res, zero_square, zero_square), (latents, noise, timesteps, group_kv, cotangent))
    grad_images = grad_groups[image_group]
    grad_condition = weighted_product('isk,fk->isf', grad_images, kv_weight).astype(jnp.bfloat16)
    positions = (offsets[:, None] + jnp.arange(SLOTS, dtype=jnp.int32)[None, :]).reshape(-1)
    grad_hidden = jnp.zeros_like(llm_hidden).at[positions].set(grad_condition.reshape(-1, llm_hidden.shape[1]))
    grad_kv_weight = (weighted_product('isf,isk->fk', condition, grad_images) * (image_count * SLOTS) ** (-0.5)).astype(jnp.bfloat16)
    weight_scale = (image_count * latents.shape[2] * latents.shape[3]) ** (-0.5)
    return (block_outs, grad_hidden, grad_kv_weight, (running[0] * weight_scale).astype(jnp.bfloat16), (running[1] * weight_scale).astype(jnp.bfloat16), (running[2] * weight_scale).astype(jnp.bfloat16))
```

```python
import math

import jax
import jax.numpy as jnp
from jax import lax
from jax.sharding import PartitionSpec as P

HEAD_DIM = 64
SLOTS = 64


def extended(cells, sides, width):
    for axis, dim in sides:
        count = lax.axis_size(axis)
        ends = count - 1
        head = lax.slice_in_dim(cells, 0, width, axis=dim)
        tail = lax.slice_in_dim(cells, cells.shape[dim] - width, cells.shape[dim], axis=dim)
        cells = jnp.concatenate(
            [
                lax.ppermute(tail, axis, [(i, (i + 1) % count) for i in range(ends)]),
                cells,
                lax.ppermute(head, axis, [((i + 1) % count, i) for i in range(ends)]),
            ],
            axis=dim,
        )
    return cells


def weighted_product(form, left, right):
    return jnp.einsum(form, left, right, preferred_element_type=jnp.float32)


def noise_levels():
    plan = jnp.linspace(0.00085**0.5, 0.012**0.5, 1000, dtype=jnp.float32) ** 2
    return jnp.exp(jnp.cumsum(jnp.log(1.0 - plan)))


def noisy_input(latent, noise_one, timestep):
    levels = noise_levels()
    picked = jnp.sum(jnp.where(jnp.arange(levels.shape[0]) == timestep, levels, 0.0))
    return (jnp.sqrt(picked) * latent + jnp.sqrt(1.0 - picked) * noise_one).astype(jnp.bfloat16)


def time_shift(timestep, channel_total):
    half_count = channel_total // 2
    frequency = jnp.exp(-math.log(10000.0) * jnp.arange(half_count, dtype=jnp.float32) / half_count)
    angles = timestep.astype(jnp.float32) * frequency
    return jnp.concatenate([jnp.cos(angles), jnp.sin(angles)])


def pad_columns(field):
    return jnp.pad(field, ((0, 0), (0, 0), (1, 1)))


def convolve(padded, weight, row_count, col_count):
    running = jnp.zeros((weight.shape[2], row_count * col_count), jnp.float32)
    for row_tap in range(3):
        for col_tap in range(3):
            window = padded[
                :, row_tap : row_tap + row_count, col_tap : col_tap + col_count
            ].reshape(padded.shape[0], row_count * col_count)
            running = running + jnp.dot(
                weight[row_tap, col_tap], window, preferred_element_type=jnp.float32
            )
    return running


def filter_grad(padded, upstream, row_count, col_count):
    tap_list = []
    for row_tap in range(3):
        for col_tap in range(3):
            window = padded[
                :, row_tap : row_tap + row_count, col_tap : col_tap + col_count
            ].reshape(padded.shape[0], row_count * col_count)
            tap_list.append(
                lax.dot_general(
                    upstream, window, (((1,), (1,)), ((), ())), preferred_element_type=jnp.float32
                )
            )
    return jnp.stack(tap_list).reshape(3, 3, upstream.shape[0], padded.shape[0])


def block_pass(
    noisy, timestep, group_kv, upstream, in_weight, res_weight, query_weight, out_weight
):
    channel_total = in_weight.shape[2]
    row_count, col_count = (noisy.shape[1], noisy.shape[2])
    latent_cell_count = row_count * col_count
    condition_slot_count = group_kv.shape[0]
    head_count = channel_total // HEAD_DIM
    logit_scale = HEAD_DIM ** (-0.5)
    noisy_pad = pad_columns(extended(noisy, (("row", 1),), 1))
    first = convolve(noisy_pad, in_weight, row_count, col_count)
    hidden_act = jax.nn.silu(first + time_shift(timestep, channel_total)[:, None]).astype(
        jnp.bfloat16
    )
    act_pad = pad_columns(
        extended(hidden_act.reshape(channel_total, row_count, col_count), (("row", 1),), 1)
    )
    residual = (first + convolve(act_pad, res_weight, row_count, col_count)).astype(jnp.bfloat16)
    query = jnp.dot(query_weight, residual, preferred_element_type=jnp.float32).astype(jnp.bfloat16)
    query_per_head = query.reshape(head_count, HEAD_DIM, latent_cell_count)
    key_matrix = group_kv[:, :channel_total].reshape(condition_slot_count, head_count, HEAD_DIM)
    value_matrix = group_kv[:, channel_total:].reshape(condition_slot_count, head_count, HEAD_DIM)
    score_matrix = weighted_product("isf,tis->itf", query_per_head, key_matrix) * logit_scale
    softmax_full = jax.nn.softmax(score_matrix, axis=1)
    softmax_reduced_precision = softmax_full.astype(jnp.bfloat16)
    attention_output = (
        weighted_product("cuo,ucb->cbo", softmax_reduced_precision, value_matrix)
        .astype(jnp.bfloat16)
        .reshape(channel_total, latent_cell_count)
    )
    block_out = (
        residual.astype(jnp.float32)
        + jnp.dot(out_weight, attention_output, preferred_element_type=jnp.float32)
    ).astype(jnp.bfloat16)
    upstream = upstream.reshape(channel_total, latent_cell_count)
    out_grad = lax.dot_general(
        upstream, attention_output, (((1,), (1,)), ((), ())), preferred_element_type=jnp.float32
    )
    grad_att = lax.dot_general(
        out_weight, upstream, (((0,), (0,)), ((), ())), preferred_element_type=jnp.float32
    ).astype(jnp.bfloat16)
    head_gradient = grad_att.reshape(head_count, HEAD_DIM, latent_cell_count)
    probability_gradient = weighted_product("isf,tis->itf", head_gradient, value_matrix)
    score_gradient = (
        logit_scale
        * softmax_full
        * (
            probability_gradient
            - jnp.sum(softmax_full * probability_gradient, axis=1, keepdims=True)
        )
    ).astype(jnp.bfloat16)
    query_gradient = (
        weighted_product("cuo,ucb->cbo", score_gradient, key_matrix)
        .astype(jnp.bfloat16)
        .reshape(channel_total, latent_cell_count)
    )
    key_gradient = weighted_product("exv,ewv->xew", score_gradient, query_per_head).reshape(
        condition_slot_count, channel_total
    )
    value_gradient = weighted_product(
        "exv,ewv->xew", softmax_reduced_precision, head_gradient
    ).reshape(condition_slot_count, channel_total)
    grad_kv = jnp.concatenate([key_gradient, value_gradient], axis=1)
    query_grad = lax.dot_general(
        query_gradient, residual, (((1,), (1,)), ((), ())), preferred_element_type=jnp.float32
    )
    grad_resid = (
        upstream.astype(jnp.float32)
        + lax.dot_general(
            query_weight,
            query_gradient,
            (((0,), (0,)), ((), ())),
            preferred_element_type=jnp.float32,
        )
    ).astype(jnp.bfloat16)
    res_grad = filter_grad(act_pad, grad_resid, row_count, col_count)
    return (
        block_out.reshape(channel_total, row_count, col_count),
        grad_kv,
        res_grad,
        query_grad,
        out_grad,
    )

GRID = ("img", "row")


def swap(block, mask):
    total = lax.axis_size("img") * lax.axis_size("row")
    return lax.ppermute(block, GRID, [(i, i ^ mask) for i in range(total)])


def place():
    rows = lax.axis_size("row")
    lines = lax.axis_size("img") // 4
    image = lax.axis_index("img")
    row = lax.axis_index("row")
    return {
        "core": (2, image % 2, lambda j: j * rows),
        "row": (rows, row, lambda j: j),
        "square": (2 * rows, (image // 2) % 2 * rows + row, lambda j: j // rows * 2 * rows + j % rows),
        "line": (lines, image // 4, lambda j: j * 4 * rows),
        "plane": (4, image % 4, lambda j: j * rows),
    }


def scatter_sum(pieces, whole, spot):
    count, own, mask = spot
    received = [
        swap(lax.dynamic_index_in_dim(pieces, own ^ j, 0, keepdims=False), mask(j))
        for j in range(count - 1, 0, -1)
    ]
    total = lax.dynamic_index_in_dim(whole, own, 0, keepdims=False)
    for one in received:
        total = total + one.astype(jnp.float32)
    return total


def gather_relative(block, spot):
    count, own, mask = spot
    far = {j: swap(block, mask(j)) for j in range(count - 1, 0, -1)}
    return [block] + [far[j] for j in range(1, count)]


def gather_ordered(block, spot, axis):
    count, own, mask = spot
    relative = jnp.stack(gather_relative(block, spot))
    ordered = [lax.dynamic_index_in_dim(relative, own ^ k, 0, keepdims=False) for k in range(count)]
    return jnp.concatenate(ordered, axis=axis)


def total_everywhere(part, scale, where):
    height, width = part.shape
    lines = where["line"][0]
    slot = -(-width // (128 * lines)) * 128
    part = jnp.pad(part, ((0, 0), (0, slot * lines - width)))
    width_all = slot * lines
    for key in ("core", "square"):
        count = where[key][0]
        whole = part.reshape(count, part.shape[0] // count, width_all)
        part = scatter_sum(whole.astype(jnp.bfloat16), whole, where[key])
    count, own, mask = where["line"]
    low = part.astype(jnp.bfloat16)
    received = [
        swap(lax.dynamic_slice_in_dim(low, (own ^ j) * slot, slot, 1), mask(j))
        for j in range(count - 1, 0, -1)
    ]
    total = lax.dynamic_slice_in_dim(part, own * slot, slot, 1)
    for one in received:
        total = total + one.astype(jnp.float32)
    result = (total * scale).astype(jnp.bfloat16)
    result = gather_ordered(result, where["line"], 1)
    result = gather_ordered(result, where["square"], 0)
    result = gather_ordered(result, where["core"], 0)
    return result[:, :width]


def shards(
    llm_hidden,
    slot_start,
    image_group,
    timesteps,
    latents,
    noise,
    kv_weight,
    in_weight,
    res_weight,
    query_weight,
    out_weight,
    cotangent,
):
    where = place()
    rows = lax.axis_size("row")
    images = lax.axis_size("img")
    lines = where["line"][0]
    own_index = lax.axis_index("img")
    core = where["core"][1]
    condition = lax.dynamic_slice_in_dim(llm_hidden, slot_start[0], SLOTS, 0)
    kv_part = jnp.dot(condition, kv_weight, preferred_element_type=jnp.float32)
    pair_width = kv_part.shape[1]
    band_rows = SLOTS // rows

    bands = kv_part.reshape(rows, band_rows, pair_width)
    kv_band = scatter_sum(bands, bands, where["row"]).astype(jnp.bfloat16)
    column = gather_relative(kv_band, where["line"])
    line_own, plane_own = where["line"][1], where["plane"][1]
    plane = []
    for k in range(4):
        target = line_own * 4 + (plane_own ^ k)
        chosen = jnp.zeros(kv_band.shape, jnp.float32)
        for j, block in enumerate(column):
            source = (line_own ^ j) * 4 + plane_own
            goes = lax.dynamic_index_in_dim(image_group, source, 0, keepdims=False) == target
            chosen = chosen + jnp.where(goes, block.astype(jnp.float32), 0.0)
        plane.append(chosen.astype(jnp.bfloat16))
    arrived = []
    for r in range(rows):
        total = jnp.zeros(kv_band.shape, jnp.float32)
        for k in range(4):
            one = plane[k] if k == 0 and r == 0 else swap(plane[k], k * rows + r)
            total = total + one.astype(jnp.float32)
        arrived.append(total.astype(jnp.bfloat16))
    arrived = jnp.stack(arrived)
    row_own = where["row"][1]
    group_kv = jnp.concatenate(
        [lax.dynamic_index_in_dim(arrived, row_own ^ r, 0, keepdims=False) for r in range(rows)]
    )

    half = condition.shape[1] // 2
    split = condition.reshape(SLOTS, 2, half)
    mine = lax.dynamic_index_in_dim(split, core, 1, keepdims=False)
    other = swap(lax.dynamic_index_in_dim(split, 1 - core, 1, keepdims=False), where["core"][2](1))
    spread = []
    for chunk in (mine, other):
        chunk = chunk[None]
        bit = lines // 2
        while bit:
            chunk = jnp.concatenate([chunk, swap(chunk, where["line"][2](bit))])
            bit //= 2
        chunk = jnp.concatenate([chunk, swap(chunk, where["plane"][2](2))])
        spread.append(chunk)
    order = [0]
    bit = lines // 2
    while bit:
        order = order + [j ^ bit for j in order]
        bit //= 2
    order = [j * 4 for j in order]
    order = order + [j ^ 2 for j in order]
    order = jnp.array(order + [j ^ 1 for j in order], jnp.int32)
    conditions = jnp.concatenate(spread).reshape(images * SLOTS, half)

    noisy = noisy_input(latents[0], noise[0], timesteps[0])
    block_out, grad_kv, res_grad, query_grad, out_grad = block_pass(
        noisy, timesteps[0], group_kv, cotangent[0], in_weight, res_weight, query_weight, out_weight
    )
    bands = grad_kv.reshape(rows, band_rows, pair_width)
    grad_band = scatter_sum(bands.astype(jnp.bfloat16), bands, where["row"]).astype(jnp.bfloat16)
    spots = jnp.stack(gather_relative(grad_band, where["line"]))
    spots = jnp.stack(gather_relative(spots, where["square"]))
    spots = jnp.stack(gather_relative(spots, where["core"]))
    spots = spots.reshape(2, 2, rows, lines, band_rows, pair_width)
    spots = jnp.concatenate(
        [lax.dynamic_index_in_dim(spots, row_own ^ r, 2, keepdims=False) for r in range(rows)], axis=3
    )
    groups = spots.transpose(2, 1, 0, 3, 4).reshape(images, SLOTS, pair_width)
    source_group = lax.dynamic_index_in_dim(image_group, own_index, 0, keepdims=False)
    grad_image = lax.dynamic_index_in_dim(groups, source_group ^ own_index, 0, keepdims=False)
    pairing = image_group[order ^ own_index] ^ own_index
    grad_images = groups[pairing].reshape(images * SLOTS, pair_width)

    grad_condition = lax.dot_general(
        grad_image, kv_weight, (((1,), (1,)), ((), ())), preferred_element_type=jnp.float32
    ).astype(jnp.bfloat16)
    grad_hidden = lax.dynamic_update_slice_in_dim(
        jnp.zeros_like(llm_hidden), grad_condition, slot_start[0], 0
    )
    kv_weight_half = (
        lax.dot_general(
            conditions, grad_images, (((0,), (0,)), ((), ())), preferred_element_type=jnp.float32
        )
        * (images * SLOTS) ** (-0.5)
    ).astype(jnp.bfloat16)
    grad_kv_weight = gather_ordered(kv_weight_half, where["core"], 0)
    weight_scale = (images * rows * latents.shape[2] * latents.shape[3]) ** (-0.5)
    channel_total = in_weight.shape[2]
    part = jnp.concatenate(
        [res_grad[a, b] for a in range(3) for b in range(3)] + [query_grad, out_grad], axis=1
    )
    totals = total_everywhere(part, weight_scale, where)
    taps = [totals[:, k * channel_total : (k + 1) * channel_total] for k in range(11)]
    return (
        block_out[None],
        grad_hidden,
        grad_kv_weight,
        jnp.stack(taps[:9]).reshape(3, 3, channel_total, channel_total),
        taps[9],
        taps[10],
    )


def solution(mesh):
    return jax.shard_map(
        shards,
        mesh=mesh,
        in_specs=(
            P("img", "row"),
            P("img"),
            P(),
            P("img"),
            P("img", None, "row", None),
            P("img", None, "row", None),
            P("row", None),
            P(),
            P(),
            P(),
            P(),
            P("img", None, "row", None),
        ),
        out_specs=(P("img", None, "row", None), P("img", "row"), P("row", None), P(), P(), P()),
        check_vma=False,
    )
```

```python
import functools
import math

import jax
import jax.numpy as jnp
from jax import lax
from jax.experimental import pallas as pl
from jax.experimental.pallas import tpu as pltpu
from jax.sharding import PartitionSpec as P

HEAD_DIM = 64
SLOTS = 64
GRID = ("img", "row")
F32 = jnp.float32
BF16 = jnp.bfloat16
VMEM = pl.BlockSpec(memory_space=pltpu.VMEM)
SMEM = pl.BlockSpec(memory_space=pltpu.SMEM)


def call(kernel, outs, ins, scratch=(), flops=0, scalars=0, name=None):
    outs = [jax.ShapeDtypeStruct(shape, kind) for shape, kind in outs]
    moved = sum(math.prod(x.shape) * x.dtype.itemsize for x in [*outs, *ins])
    return pl.pallas_call(
        kernel,
        out_shape=outs,
        in_specs=[SMEM] * scalars + [VMEM] * (len(ins) - scalars),
        out_specs=[VMEM] * len(outs),
        scratch_shapes=list(scratch),
        cost_estimate=pl.CostEstimate(flops=flops, bytes_accessed=moved, transcendentals=0),
        name=name,
    )(*ins)


def product(left, right, sides):
    return lax.dot_general(left, right, ((sides[:1], sides[1:]), ((), ())), preferred_element_type=F32)


def noise_levels():
    plan = jnp.linspace(0.00085**0.5, 0.012**0.5, 1000, dtype=jnp.float32) ** 2
    return jnp.exp(jnp.cumsum(jnp.log(1.0 - plan)))


def noisy_input(latent, noise_one, timestep):
    levels = noise_levels()
    picked = jnp.sum(jnp.where(jnp.arange(levels.shape[0]) == timestep, levels, 0.0))
    return (jnp.sqrt(picked) * latent + jnp.sqrt(1.0 - picked) * noise_one).astype(jnp.bfloat16)


def time_shift(timestep, channel_total):
    half_count = channel_total // 2
    frequency = jnp.exp(-math.log(10000.0) * jnp.arange(half_count, dtype=jnp.float32) / half_count)
    angles = timestep.astype(jnp.float32) * frequency
    return jnp.concatenate([jnp.cos(angles), jnp.sin(angles)])


def swap(block, mask):
    total = lax.axis_size("img") * lax.axis_size("row")
    return lax.ppermute(block, GRID, [(i, i ^ mask) for i in range(total)])


def place():
    rows = lax.axis_size("row")
    lines = lax.axis_size("img") // 4
    image = lax.axis_index("img")
    row = lax.axis_index("row")
    return {
        "core": (2, image % 2, lambda j: j * rows),
        "row": (rows, row, lambda j: j),
        "square": (2 * rows, (image // 2) % 2 * rows + row, lambda j: j // rows * 2 * rows + j % rows),
        "line": (lines, image // 4, lambda j: j * 4 * rows),
        "plane": (4, image % 4, lambda j: j * rows),
    }


def extended(cells, width):
    count = lax.axis_size("row")
    row = lax.axis_index("row")
    head = cells[:, :width]
    tail = cells[:, cells.shape[1] - width :]
    if count == 2:
        far = lax.ppermute(jnp.where(row == 0, tail, head), "row", [(0, 1), (1, 0)])
        above = jnp.where(row == 0, jnp.zeros_like(far), far)
        below = jnp.where(row == 0, far, jnp.zeros_like(far))
    else:
        above = lax.ppermute(tail, "row", [(i, i + 1) for i in range(count - 1)])
        below = lax.ppermute(head, "row", [(i + 1, i) for i in range(count - 1)])
    return jnp.concatenate([above, cells, below], axis=1)


def front_kernel(rows, cols, edges, patches, shift, in_weight, res_weight, query_weight, acts, hid, query):
    cells = rows * cols
    first = product(in_weight[...], patches[...], (1, 0))
    act = jax.nn.silu(first + shift[...])
    lane = lax.broadcasted_iota(jnp.int32, (act.shape[0], cols), 1)
    for r in range(rows + 2):
        band = act[:, r * cols : (r + 1) * cols]
        if r == 0:
            band = jnp.where(edges[0] == 1, band, 0.0)
        if r == rows + 1:
            band = jnp.where(edges[1] == 1, band, 0.0)
        spot = pl.ds(r * cols, cols)
        acts[1, :, spot] = band.astype(BF16)
        acts[0, :, spot] = jnp.where(lane == 0, 0.0, pltpu.roll(band, 1, 1)).astype(BF16)
        acts[2, :, spot] = jnp.where(lane == cols - 1, 0.0, pltpu.roll(band, cols - 1, 1)).astype(BF16)
    total = first[:, cols : cols + cells]
    for a in range(3):
        for b in range(3):
            total = total + product(res_weight[3 * a + b], acts[b, :, a * cols : a * cols + cells], (1, 0))
    low = total.astype(BF16)
    hid[...] = low
    query[...] = product(query_weight[...], low, (1, 0)).astype(BF16)


def attention_kernel(
    query, hid, upstream, pairs, query_weight, out_weight,
    block_out, grad_pairs, grad_hid, query_grad, out_grad, grad_att, attended, grad_query,
):
    channels = hid.shape[0]
    scale = HEAD_DIM**-0.5
    grad_att[...] = product(out_weight[...], upstream[...], (0, 0)).astype(BF16)
    for h in range(channels // HEAD_DIM):
        spot = slice(h * HEAD_DIM, (h + 1) * HEAD_DIM)
        keys = pairs[:, h * HEAD_DIM : (h + 1) * HEAD_DIM]
        vals = pairs[:, channels + h * HEAD_DIM : channels + (h + 1) * HEAD_DIM]
        one = query[spot, :]
        score = product(keys, one, (1, 0)) * scale
        grown = jnp.exp(score - jnp.max(score, axis=0, keepdims=True))
        probs = grown / jnp.sum(grown, axis=0, keepdims=True)
        low = probs.astype(BF16)
        attended[spot, :] = product(vals, low, (0, 0)).astype(BF16)
        back = grad_att[spot, :]
        grad_prob = product(vals, back, (1, 0))
        inner = jnp.sum(probs * grad_prob, axis=0, keepdims=True)
        grad_score = (scale * probs * (grad_prob - inner)).astype(BF16)
        grad_query[spot, :] = product(keys, grad_score, (0, 0)).astype(BF16)
        grad_pairs[:, h * HEAD_DIM : (h + 1) * HEAD_DIM] = product(grad_score, one, (1, 1))
        grad_pairs[:, channels + h * HEAD_DIM : channels + (h + 1) * HEAD_DIM] = product(low, back, (1, 1))
    block_out[...] = (
        hid[...].astype(F32) + product(out_weight[...], attended[...], (1, 0))
    ).astype(BF16)
    grad_hid[...] = (
        upstream[...].astype(F32) + product(query_weight[...], grad_query[...], (0, 0))
    ).astype(BF16)
    query_grad[...] = product(grad_query[...], hid[...], (1, 1))
    out_grad[...] = product(upstream[...], attended[...], (1, 1))


def filter_kernel(cols, spots, grad_hid, acts, query_grad, out_grad, kept, sent, whole, pair, wide):
    channels, cells = grad_hid.shape
    for t in range(0, 9, 2):
        taps = [t, t + 1] if t < 8 else [t]
        for k, tap in enumerate(taps):
            a, b = tap // 3, tap % 3
            pair[k * channels : (k + 1) * channels, :] = acts[b, :, a * cols : a * cols + cells]
        span = len(taps) * channels
        whole[:, t * channels : t * channels + span] = product(grad_hid[...], pair[:span, :], (1, 1))
    edge = 9 * channels
    base = edge // 128 * 128
    lead = edge - base
    wide[:, :channels] = query_grad[...]
    turned = pltpu.roll(wide[...], lead, 1) if lead else wide[...]
    lane = lax.broadcasted_iota(jnp.int32, (channels, 128), 1)
    whole[:, base : base + 128] = jnp.where(lane < lead, whole[:, base : base + 128], turned[:, :128])
    whole[:, base + 128 : edge + channels] = turned[:, 128 : lead + channels]
    whole[:, edge + channels : edge + 2 * channels] = out_grad[...]
    rest = whole.shape[1] - edge - 2 * channels
    if rest:
        whole[:, edge + 2 * channels :] = jnp.zeros((channels, rest), F32)
    half = channels // 2
    core = spots[0]
    kept[...] = whole[pl.ds(pl.multiple_of(core * half, 8), half), :]
    sent[...] = whole[pl.ds(pl.multiple_of((1 - core) * half, 8), half), :].astype(BF16)


def square_kernel(count, spots, kept, came, *refs):
    own, outs, held = refs[0], refs[1:count], refs[count]
    height = kept.shape[0] // count
    for q in range(count):
        held[q] = kept[q * height : (q + 1) * height, :] + came[q * height : (q + 1) * height, :].astype(F32)
    own[...] = held[spots[1]]
    for j in range(1, count):
        outs[j - 1][...] = held[spots[1] ^ j].astype(BF16)


def line_kernel(count, near, spots, *refs):
    total = refs[0][...]
    for one in refs[1:near]:
        total = total + one[...].astype(F32)
    own, outs, held = refs[near], refs[near + 1 : near + count], refs[near + count]
    slot = total.shape[1] // count
    for q in range(count):
        held[q] = total[:, q * slot : (q + 1) * slot]
    own[...] = held[spots[2]]
    for j in range(1, count):
        outs[j - 1][...] = held[spots[2] ^ j].astype(BF16)


def finish_kernel(scale, own, *refs):
    total = own[...]
    for one in refs[:-1]:
        total = total + one[...].astype(F32)
    refs[-1][...] = (total * scale).astype(BF16)


def widen_kernel(count, spots, *refs):
    parts, out, held = refs[:count], refs[count], refs[count + 1]
    slot = parts[0].shape[1]
    for j in range(count):
        held[spots[2] ^ j] = parts[j][...]
    for q in range(count):
        out[:, q * slot : (q + 1) * slot] = held[q]


def unpack_kernel(count, spots, *refs):
    parts = refs[: 2 * count]
    res, query, out, held, whole = refs[2 * count :]
    height = parts[0].shape[0]
    for c in range(2):
        for j in range(count):
            held[(spots[0] ^ c) * count + (spots[1] ^ j)] = parts[c * count + j][...]
    for q in range(2 * count):
        whole[q * height : (q + 1) * height, :] = held[q].astype(F32)
    channels = query.shape[0]
    for t in range(11):
        start = t * channels
        base = start // 128 * 128
        lead = start - base
        if lead:
            span = -(-(lead + channels) // 128) * 128
            piece = pltpu.roll(whole[:, base : base + span], span - lead, 1)[:, :channels]
        else:
            piece = whole[:, start : start + channels]
        piece = piece.astype(BF16)
        if t < 9:
            res[t] = piece
        elif t == 9:
            query[...] = piece
        else:
            out[...] = piece


def totals_everywhere(grad_hid, acts, query_grad, out_grad, cols, scale, where):
    channels, cells = grad_hid.shape
    squares, lines = where["square"][0], where["line"][0]
    spots = jnp.stack([where["core"][1], where["square"][1], where["line"][1]]).astype(jnp.int32)
    slot = -(-11 * channels // (128 * lines)) * 128
    width = slot * lines
    half, height = channels // 2, channels // 2 // squares
    kept, sent = call(
        functools.partial(filter_kernel, cols),
        [((half, width), F32), ((half, width), BF16)],
        [spots, grad_hid, acts, query_grad, out_grad],
        [
            pltpu.VMEM((channels, width), F32),
            pltpu.VMEM((2 * channels, cells), BF16),
            pltpu.VMEM((channels, -(-channels // 128) * 128), F32),
        ],
        flops=18 * channels * channels * cells,
        scalars=1,
        name="filter",
    )
    came = swap(sent, where["core"][2](1))
    own, *outs = call(
        functools.partial(square_kernel, squares),
        [((height, width), F32)] + [((height, width), BF16)] * (squares - 1),
        [spots, kept, came],
        [pltpu.VMEM((squares, height, width), F32)],
        scalars=1,
        name="square",
    )
    near = [swap(outs[j - 1], where["square"][2](j)) for j in range(squares - 1, 0, -1)]
    own, *outs = call(
        functools.partial(line_kernel, lines, squares),
        [((height, slot), F32)] + [((height, slot), BF16)] * (lines - 1),
        [spots, own, *near],
        [pltpu.VMEM((lines, height, slot), F32)],
        scalars=1,
        name="line",
    )
    near = [swap(outs[j - 1], where["line"][2](j)) for j in range(lines - 1, 0, -1)]
    (final,) = call(
        functools.partial(finish_kernel, scale), [((height, slot), BF16)], [own, *near], name="finish"
    )
    far = [swap(final, where["line"][2](j)) for j in range(lines - 1, 0, -1)][::-1]
    (wide,) = call(
        functools.partial(widen_kernel, lines),
        [((height, width), BF16)],
        [spots, final, *far],
        [pltpu.VMEM((lines, height, slot), BF16)],
        scalars=1,
        name="widen",
    )
    far = {j: swap(wide, where["square"][2](j)) for j in range(squares - 1, 0, -1)}
    mine = [wide] + [far[j] for j in range(1, squares)]
    other = [swap(one, where["core"][2](1)) for one in mine]
    res, query, out = call(
        functools.partial(unpack_kernel, squares),
        [((9, channels, channels), BF16), ((channels, channels), BF16), ((channels, channels), BF16)],
        [spots, *mine, *other],
        [pltpu.VMEM((2 * squares, height, width), BF16), pltpu.VMEM((channels, width), F32)],
        scalars=1,
        name="unpack",
    )
    return res.reshape(3, 3, channels, channels), query, out


def weight_kernel(scale, spots, pairing, mine, other, groups, big, send, held):
    count = groups.shape[0]

    @pl.when(pl.program_id(0) == 0)
    def _():
        for i in range(count):
            held[i * SLOTS : (i + 1) * SLOTS, :] = groups[pairing[i]]

    half = mine.shape[0]
    total = product(mine[...], held[:half, :], (0, 0)) + product(other[...], held[half:, :], (0, 0))
    low = (total * scale).astype(BF16)
    big[...] = low
    send[...] = low


def join_kernel(spots, came, big_in, big):
    big[...] = came[...]


def kv_weight_grad(mine, other, groups, pairing, scale, where):
    core = where["core"][1]
    rows, width = mine.shape
    pair_width = groups.shape[2]
    tile = 128 if width % 128 == 0 else width
    steps = width // tile
    spots = core.astype(jnp.int32)[None]
    big, send = pl.pallas_call(
        functools.partial(weight_kernel, scale),
        out_shape=[
            jax.ShapeDtypeStruct((2 * width, pair_width), BF16),
            jax.ShapeDtypeStruct((width, pair_width), BF16),
        ],
        grid_spec=pltpu.PrefetchScalarGridSpec(
            num_scalar_prefetch=2,
            grid=(steps,),
            in_specs=[
                pl.BlockSpec((rows, tile), lambda m, s, p: (0, m)),
                pl.BlockSpec((rows, tile), lambda m, s, p: (0, m)),
                pl.BlockSpec(groups.shape, lambda m, s, p: (0, 0, 0)),
            ],
            out_specs=[
                pl.BlockSpec((tile, pair_width), lambda m, s, p: (s[0] * steps + m, 0)),
                pl.BlockSpec((tile, pair_width), lambda m, s, p: (m, 0)),
            ],
            scratch_shapes=[pltpu.VMEM((2 * rows, pair_width), BF16)],
        ),
        cost_estimate=pl.CostEstimate(
            flops=4 * rows * width * pair_width,
            bytes_accessed=4 * rows * width + 6 * width * pair_width,
            transcendentals=0,
        ),
        name="kvgrad",
    )(spots, pairing, mine, other, groups)
    came = swap(send, where["core"][2](1))
    return pl.pallas_call(
        join_kernel,
        out_shape=jax.ShapeDtypeStruct((2 * width, pair_width), BF16),
        grid_spec=pltpu.PrefetchScalarGridSpec(
            num_scalar_prefetch=1,
            grid=(1,),
            in_specs=[
                pl.BlockSpec((width, pair_width), lambda m, s: (0, 0)),
                pl.BlockSpec(memory_space=pl.ANY),
            ],
            out_specs=pl.BlockSpec((width, pair_width), lambda m, s: (1 - s[0], 0)),
        ),
        input_output_aliases={2: 0},
        name="kvjoin",
    )(spots, came, big)


def hidden_kernel(start, image, weight, out):
    low = product(image[...], weight[...], (1, 1)).astype(BF16)
    tokens = out.shape[0]
    token = lax.broadcasted_iota(jnp.int32, (tokens, SLOTS), 0)
    slot = lax.broadcasted_iota(jnp.int32, (tokens, SLOTS), 1)
    chosen = jnp.where(token == slot + start[0], 1.0, 0.0).astype(BF16)
    out[...] = product(chosen, low, (1, 0)).astype(BF16)


def hidden_grad(start, grad_image, kv_weight, tokens):
    features, pair_width = kv_weight.shape
    tile = 256 if features % 256 == 0 else features
    return pl.pallas_call(
        hidden_kernel,
        out_shape=jax.ShapeDtypeStruct((tokens, features), BF16),
        grid_spec=pltpu.PrefetchScalarGridSpec(
            num_scalar_prefetch=1,
            grid=(features // tile,),
            in_specs=[
                pl.BlockSpec((SLOTS, pair_width), lambda m, s: (0, 0)),
                pl.BlockSpec((tile, pair_width), lambda m, s: (m, 0)),
            ],
            out_specs=pl.BlockSpec((tokens, tile), lambda m, s: (0, m)),
        ),
        cost_estimate=pl.CostEstimate(
            flops=2 * features * SLOTS * (pair_width + tokens),
            bytes_accessed=2 * features * (pair_width + tokens),
            transcendentals=0,
        ),
        name="hidden",
    )(start, grad_image, kv_weight)


def scatter_sum(pieces, whole, spot):
    count, own, mask = spot
    received = [
        swap(lax.dynamic_index_in_dim(pieces, own ^ j, 0, keepdims=False), mask(j))
        for j in range(count - 1, 0, -1)
    ]
    total = lax.dynamic_index_in_dim(whole, own, 0, keepdims=False)
    for one in received:
        total = total + one.astype(jnp.float32)
    return total


def gather_relative(block, spot):
    count, own, mask = spot
    far = {j: swap(block, mask(j)) for j in range(count - 1, 0, -1)}
    return [block] + [far[j] for j in range(1, count)]


def shards(
    llm_hidden,
    slot_start,
    image_group,
    timesteps,
    latents,
    noise,
    kv_weight,
    in_weight,
    res_weight,
    query_weight,
    out_weight,
    cotangent,
):
    where = place()
    rows = lax.axis_size("row")
    images = lax.axis_size("img")
    lines = where["line"][0]
    own_index = lax.axis_index("img")
    core = where["core"][1]
    row_own = where["row"][1]
    channels = in_weight.shape[2]
    row_count, col_count = latents.shape[2:]
    cells = row_count * col_count

    condition = lax.dynamic_slice_in_dim(llm_hidden, slot_start[0], SLOTS, 0)
    kv_part = jnp.dot(condition, kv_weight, preferred_element_type=jnp.float32)
    pair_width = kv_part.shape[1]
    band_rows = SLOTS // rows
    bands = kv_part.reshape(rows, band_rows, pair_width)
    kv_band = scatter_sum(bands, bands, where["row"]).astype(jnp.bfloat16)
    column = gather_relative(kv_band, where["line"])
    line_own, plane_own = where["line"][1], where["plane"][1]
    plane = []
    for k in range(4):
        target = line_own * 4 + (plane_own ^ k)
        chosen = jnp.zeros(kv_band.shape, jnp.float32)
        for j, block in enumerate(column):
            source = (line_own ^ j) * 4 + plane_own
            goes = lax.dynamic_index_in_dim(image_group, source, 0, keepdims=False) == target
            chosen = chosen + jnp.where(goes, block.astype(jnp.float32), 0.0)
        plane.append(chosen.astype(jnp.bfloat16))
    arrived = []
    for r in range(rows):
        total = jnp.zeros(kv_band.shape, jnp.float32)
        for k in range(4):
            one = plane[k] if k == 0 and r == 0 else swap(plane[k], k * rows + r)
            total = total + one.astype(jnp.float32)
        arrived.append(total.astype(jnp.bfloat16))
    arrived = jnp.stack(arrived)
    group_kv = jnp.concatenate(
        [lax.dynamic_index_in_dim(arrived, row_own ^ r, 0, keepdims=False) for r in range(rows)]
    )

    half = condition.shape[1] // 2
    split = condition.reshape(SLOTS, 2, half)
    mine = lax.dynamic_index_in_dim(split, core, 1, keepdims=False)
    other = swap(lax.dynamic_index_in_dim(split, 1 - core, 1, keepdims=False), where["core"][2](1))
    spread = []
    for chunk in (mine, other):
        bit = lines // 2
        while bit:
            chunk = jnp.concatenate([chunk, swap(chunk, where["line"][2](bit))])
            bit //= 2
        chunk = jnp.concatenate([chunk, swap(chunk, where["plane"][2](2))])
        spread.append(chunk)
    order = [0]
    bit = lines // 2
    while bit:
        order = order + [j ^ bit for j in order]
        bit //= 2
    order = [j * 4 for j in order]
    order = order + [j ^ 2 for j in order]
    order = jnp.array(order + [j ^ 1 for j in order], jnp.int32)

    noisy = extended(noisy_input(latents[0], noise[0], timesteps[0]), 2)
    padded = jnp.pad(noisy, ((0, 0), (0, 0), (1, 1)))
    patches = jnp.concatenate(
        [
            padded[:, a : a + row_count + 2, b : b + col_count].reshape(padded.shape[0], -1)
            for a in range(3)
            for b in range(3)
        ]
    )
    in_flat = in_weight.transpose(2, 0, 1, 3).reshape(channels, -1)
    edges = jnp.stack([row_own > 0, row_own < rows - 1]).astype(jnp.int32)
    acts, hid, query = call(
        functools.partial(front_kernel, row_count, col_count),
        [
            ((3, channels, cells + 2 * col_count), BF16),
            ((channels, cells), BF16),
            ((channels, cells), BF16),
        ],
        [
            edges,
            patches,
            time_shift(timesteps[0], channels)[:, None],
            in_flat,
            res_weight.reshape(9, channels, channels),
            query_weight,
        ],
        flops=20 * channels * channels * cells,
        scalars=1,
        name="front",
    )
    upstream = cotangent[0].reshape(channels, cells)
    block_out, grad_kv, grad_hid, query_grad, out_grad = call(
        attention_kernel,
        [
            ((channels, cells), BF16),
            ((SLOTS, pair_width), F32),
            ((channels, cells), BF16),
            ((channels, channels), F32),
            ((channels, channels), F32),
        ],
        [query, hid, upstream, group_kv, query_weight, out_weight],
        [pltpu.VMEM((channels, cells), BF16)] * 3,
        flops=10 * channels * channels * cells + 12 * channels * SLOTS * cells,
        name="attention",
    )
    bands = grad_kv.reshape(rows, band_rows, pair_width)
    grad_band = scatter_sum(bands.astype(jnp.bfloat16), bands, where["row"]).astype(jnp.bfloat16)
    spots = jnp.stack(gather_relative(grad_band, where["line"]))
    spots = jnp.stack(gather_relative(spots, where["square"]))
    spots = jnp.stack(gather_relative(spots, where["core"]))
    spots = spots.reshape(2, 2, rows, lines, band_rows, pair_width)
    spots = jnp.concatenate(
        [lax.dynamic_index_in_dim(spots, row_own ^ r, 2, keepdims=False) for r in range(rows)], axis=3
    )
    groups = spots.transpose(2, 1, 0, 3, 4).reshape(images, SLOTS, pair_width)
    source_group = lax.dynamic_index_in_dim(image_group, own_index, 0, keepdims=False)
    grad_image = lax.dynamic_index_in_dim(groups, source_group ^ own_index, 0, keepdims=False)
    pairing = image_group[order ^ own_index] ^ own_index

    grad_hidden = hidden_grad(slot_start, grad_image, kv_weight, llm_hidden.shape[0])
    grad_kv_weight = kv_weight_grad(
        spread[0], spread[1], groups, pairing, (images * SLOTS) ** (-0.5), where
    )
    weight_scale = (images * rows * cells) ** (-0.5)
    grad_res_weight, grad_query_weight, grad_out_weight = totals_everywhere(
        grad_hid, acts, query_grad, out_grad, col_count, weight_scale, where
    )
    return (
        block_out.reshape(1, channels, row_count, col_count),
        grad_hidden,
        grad_kv_weight,
        grad_res_weight,
        grad_query_weight,
        grad_out_weight,
    )


def solution(mesh):
    return jax.shard_map(
        shards,
        mesh=mesh,
        in_specs=(
            P("img", "row"),
            P("img"),
            P(),
            P("img"),
            P("img", None, "row", None),
            P("img", None, "row", None),
            P("row", None),
            P(),
            P(),
            P(),
            P(),
            P("img", None, "row", None),
        ),
        out_specs=(P("img", None, "row", None), P("img", "row"), P("row", None), P(), P(), P()),
        check_vma=False,
    )
```

```python
import functools
import math

import jax
import jax.numpy as jnp
from jax import lax
from jax.experimental import pallas as pl
from jax.experimental.pallas import tpu as pltpu
from jax.sharding import PartitionSpec as P

HEAD_DIM = 64
SLOTS = 64
GRID = ("img", "row")
F32 = jnp.float32
BF16 = jnp.bfloat16
VMEM = pl.BlockSpec(memory_space=pltpu.VMEM)
SMEM = pl.BlockSpec(memory_space=pltpu.SMEM)


def call(kernel, outs, ins, scratch=(), flops=0, scalars=0, name=None):
    outs = [jax.ShapeDtypeStruct(shape, kind) for shape, kind in outs]
    moved = sum(math.prod(x.shape) * x.dtype.itemsize for x in [*outs, *ins])
    return pl.pallas_call(
        kernel,
        out_shape=outs,
        in_specs=[SMEM] * scalars + [VMEM] * (len(ins) - scalars),
        out_specs=[VMEM] * len(outs),
        scratch_shapes=list(scratch),
        cost_estimate=pl.CostEstimate(flops=flops, bytes_accessed=moved, transcendentals=0),
        name=name,
    )(*ins)


def product(left, right, sides):
    return lax.dot_general(left, right, ((sides[:1], sides[1:]), ((), ())), preferred_element_type=F32)


def time_shift(timestep, channel_total):
    half_count = channel_total // 2
    frequency = jnp.exp(-math.log(10000.0) * jnp.arange(half_count, dtype=jnp.float32) / half_count)
    angles = timestep.astype(jnp.float32) * frequency
    return jnp.concatenate([jnp.cos(angles), jnp.sin(angles)])


def swap(block, mask):
    total = lax.axis_size("img") * lax.axis_size("row")
    return lax.ppermute(block, GRID, [(i, i ^ mask) for i in range(total)])


def after(value, *events):
    return lax.optimization_barrier((value, *events))[0]


def spots_of(spots, rows):
    image, row = spots[0], spots[1]
    return {
        "core": image & 1,
        "row": row,
        "square": ((image >> 1) & 1) * rows + row,
        "line": image >> 2,
        "plane": image & 3,
    }


def noisy_kernel(rows, spots, timestep, latents, noise, noisy, *edges):
    step = timestep[0]
    index = lax.broadcasted_iota(jnp.int32, (8, 128), 0) * 128 + lax.broadcasted_iota(
        jnp.int32, (8, 128), 1
    )
    low, high = 0.00085**0.5, 0.012**0.5
    beta = (low + index.astype(F32) * ((high - low) / 999.0)) ** 2
    logs = jnp.where(index <= step, jnp.log(1.0 - jnp.where(index < 1000, beta, 0.0)), 0.0)
    total = jnp.sum(jnp.sum(logs, axis=1, keepdims=True), axis=0, keepdims=True)
    level = jnp.exp(total)
    keep, mix = jnp.sqrt(level), jnp.sqrt(1.0 - level)
    height = latents.shape[2]
    for c in range(latents.shape[1]):
        value = (keep * latents[0, c] + mix * noise[0, c]).astype(BF16).astype(F32)
        noisy[c] = value
        head, tail = value[:2].astype(BF16), value[height - 2 :].astype(BF16)
        if rows == 2:
            edges[0][c] = jnp.where(spots[1] == 0, tail, head)
        else:
            edges[0][c] = tail
            edges[1][c] = head


def condition_kernel(rows, spots, start, hidden, weight, kept, *refs):
    sent, mine, away = refs[: rows - 1], refs[rows - 1], refs[rows]
    window, weights, cond, held, row_sem, sems = refs[rows + 1 :]
    here = spots_of(spots, rows)
    pieces = sems.shape[0]
    depth = weight.shape[0] // pieces
    span = window.shape[0]
    base = jnp.minimum((start[0] >> 4) << 4, hidden.shape[0] - span)
    load = pltpu.make_async_copy(hidden.at[pl.ds(pl.multiple_of(base, 16), span), :], window, row_sem)
    load.start()
    loads = [
        pltpu.make_async_copy(
            weight.at[k * depth : (k + 1) * depth, :], weights.at[k * depth : (k + 1) * depth, :], sems.at[k]
        )
        for k in range(pieces)
    ]
    for one in loads:
        one.start()
    load.wait()
    slot = lax.broadcasted_iota(jnp.int32, (SLOTS, span), 0)
    token = lax.broadcasted_iota(jnp.int32, (SLOTS, span), 1)
    chosen = jnp.where(token == slot + (start[0] - base), 1.0, 0.0).astype(BF16)
    cond[...] = product(chosen, window[...], (1, 0)).astype(BF16)
    half = cond.shape[1] // 2
    left, right = cond[:, :half], cond[:, half:]
    mine[...] = jnp.where(here["core"] == 0, left, right)
    away[...] = jnp.where(here["core"] == 0, right, left)
    total = None
    for k in range(pieces):
        loads[k].wait()
        one = product(cond[:, k * depth : (k + 1) * depth], weights[k * depth : (k + 1) * depth, :], (1, 0))
        total = one if total is None else total + one
    height = SLOTS // rows
    for r in range(rows):
        held[r] = total[r * height : (r + 1) * height]
    kept[...] = held[here["row"]]
    for j in range(1, rows):
        sent[j - 1][...] = held[here["row"] ^ j]


def select_kernel(rows, spots, group_of, *refs):
    lines = len(refs) - 4
    here = spots_of(spots, rows)
    for k in range(4):
        target = here["line"] * 4 + (here["plane"] ^ k)
        chosen = jnp.zeros(refs[0].shape, F32)
        for j in range(lines):
            goes = group_of[(here["line"] ^ j) * 4 + here["plane"]] == target
            chosen = chosen + jnp.where(goes, refs[j][...].astype(F32), 0.0)
        refs[lines + k][...] = chosen.astype(BF16)


def front_kernel(spots, noisy, *refs):
    rows_total = spots[2]
    far = refs[:-8]
    shift, in_weight, res_weight, query_weight, acts, hid, query, patches = refs[-8:]
    rows, cols = noisy.shape[1:]
    cells = rows * cols
    row = spots[1]
    inner, outer = row > 0, row < rows_total - 1
    above = jnp.where(inner, far[0][...].astype(F32), 0.0)
    below = jnp.where(outer, far[-1][...].astype(F32), 0.0)
    lane = lax.broadcasted_iota(jnp.int32, (noisy.shape[0], cols), 1)
    depth = noisy.shape[0]
    for r in range(rows + 4):
        if r < 2:
            line = above[:, r]
        elif r < rows + 2:
            line = noisy[:, r - 2]
        else:
            line = below[:, r - rows - 2]
        turned = [
            jnp.where(lane == 0, 0.0, pltpu.roll(line, 1, 1)),
            line,
            jnp.where(lane == cols - 1, 0.0, pltpu.roll(line, cols - 1, 1)),
        ]
        for a in range(3):
            if 0 <= r - a < rows + 2:
                for b in range(3):
                    k = 3 * a + b
                    patches[k * depth : (k + 1) * depth, (r - a) * cols : (r - a + 1) * cols] = turned[b]
    first = product(in_weight[...], patches[...].astype(BF16), (0, 0))
    act = jax.nn.silu(first + shift[...])
    lane = lax.broadcasted_iota(jnp.int32, (act.shape[0], cols), 1)
    for r in range(rows + 2):
        band = act[:, r * cols : (r + 1) * cols]
        if r == 0:
            band = jnp.where(inner, band, 0.0)
        if r == rows + 1:
            band = jnp.where(outer, band, 0.0)
        spot = slice(r * cols, (r + 1) * cols)
        acts[1, :, spot] = band.astype(BF16)
        acts[0, :, spot] = jnp.where(lane == 0, 0.0, pltpu.roll(band, 1, 1)).astype(BF16)
        acts[2, :, spot] = jnp.where(lane == cols - 1, 0.0, pltpu.roll(band, cols - 1, 1)).astype(BF16)
    total = first[:, cols : cols + cells]
    for a in range(3):
        for b in range(3):
            total = total + product(res_weight[3 * a + b], acts[b, :, a * cols : a * cols + cells], (1, 0))
    low = total.astype(BF16)
    hid[...] = low
    query[...] = product(query_weight[...], low, (1, 0)).astype(BF16)


def attention_kernel(rows, spots, query, hid, upstream, query_weight, out_weight, *refs):
    bands = refs[:rows]
    block_out, kept, grad_hid, query_grad, out_grad = refs[rows : rows + 5]
    sent = refs[rows + 5 : 2 * rows + 4]
    grad_att, attended, grad_query, held, pairs, grad_pairs = refs[2 * rows + 4 :]
    channels = hid.shape[0]
    here = spots_of(spots, rows)
    height = SLOTS // rows
    for j in range(rows):
        held[here["row"] ^ j] = bands[j][...]
    for r in range(rows):
        pairs[r * height : (r + 1) * height, :] = held[r]
    scale = HEAD_DIM**-0.5
    grad_att[...] = product(out_weight[...], upstream[...], (0, 0)).astype(BF16)
    for h in range(channels // HEAD_DIM):
        spot = slice(h * HEAD_DIM, (h + 1) * HEAD_DIM)
        keys = pairs[:, h * HEAD_DIM : (h + 1) * HEAD_DIM]
        vals = pairs[:, channels + h * HEAD_DIM : channels + (h + 1) * HEAD_DIM]
        one = query[spot, :]
        score = product(keys, one, (1, 0)) * scale
        grown = jnp.exp(score - jnp.max(score, axis=0, keepdims=True))
        probs = grown / jnp.sum(grown, axis=0, keepdims=True)
        low = probs.astype(BF16)
        attended[spot, :] = product(vals, low, (0, 0)).astype(BF16)
        back = grad_att[spot, :]
        grad_prob = product(vals, back, (1, 0))
        inner = jnp.sum(probs * grad_prob, axis=0, keepdims=True)
        grad_score = (scale * probs * (grad_prob - inner)).astype(BF16)
        grad_query[spot, :] = product(keys, grad_score, (0, 0)).astype(BF16)
        grad_pairs[:, h * HEAD_DIM : (h + 1) * HEAD_DIM] = product(grad_score, one, (1, 1))
        grad_pairs[:, channels + h * HEAD_DIM : channels + (h + 1) * HEAD_DIM] = product(low, back, (1, 1))
    kept[...] = grad_pairs[pl.ds(pl.multiple_of(here["row"] * height, 8), height), :]
    for j in range(1, rows):
        spot = pl.ds(pl.multiple_of((here["row"] ^ j) * height, 8), height)
        sent[j - 1][...] = grad_pairs[spot, :].astype(BF16)
    block_out[...] = (
        hid[...].astype(F32) + product(out_weight[...], attended[...], (1, 0))
    ).astype(BF16)
    grad_hid[...] = (
        upstream[...].astype(F32) + product(query_weight[...], grad_query[...], (0, 0))
    ).astype(BF16)
    query_grad[...] = product(grad_query[...], hid[...], (1, 1))
    out_grad[...] = product(upstream[...], attended[...], (1, 1))


def filter_kernel(rows, cols, spots, grad_hid, acts, query_grad, out_grad, kept, sent, whole, pair, wide):
    channels, cells = grad_hid.shape
    for t in range(0, 9, 2):
        taps = [t, t + 1] if t < 8 else [t]
        for k, tap in enumerate(taps):
            a, b = tap // 3, tap % 3
            pair[k * channels : (k + 1) * channels, :] = acts[b, :, a * cols : a * cols + cells]
        span = len(taps) * channels
        whole[:, t * channels : t * channels + span] = product(grad_hid[...], pair[:span, :], (1, 1))
    edge = 9 * channels
    base = edge // 128 * 128
    lead = edge - base
    wide[:, :channels] = query_grad[...]
    turned = pltpu.roll(wide[...], lead, 1) if lead else wide[...]
    lane = lax.broadcasted_iota(jnp.int32, (channels, 128), 1)
    whole[:, base : base + 128] = jnp.where(lane < lead, whole[:, base : base + 128], turned[:, :128])
    whole[:, base + 128 : edge + channels] = turned[:, 128 : lead + channels]
    whole[:, edge + channels : edge + 2 * channels] = out_grad[...]
    rest = whole.shape[1] - edge - 2 * channels
    if rest:
        whole[:, edge + 2 * channels :] = jnp.zeros((channels, rest), F32)
    half = channels // 2
    core = spots_of(spots, rows)["core"]
    kept[...] = whole[pl.ds(pl.multiple_of(core * half, 8), half), :]
    sent[...] = whole[pl.ds(pl.multiple_of((1 - core) * half, 8), half), :].astype(BF16)


def square_kernel(rows, spots, kept, came, *refs):
    count = 2 * rows
    here = spots_of(spots, rows)["square"]
    own, outs, held = refs[0], refs[1:count], refs[count]
    height = kept.shape[0] // count
    for q in range(count):
        held[q] = kept[q * height : (q + 1) * height, :] + came[q * height : (q + 1) * height, :].astype(F32)
    own[...] = held[here]
    for j in range(1, count):
        outs[j - 1][...] = held[here ^ j].astype(BF16)


def line_kernel(rows, count, near, spots, *refs):
    here = spots_of(spots, rows)["line"]
    total = refs[0][...]
    for one in refs[1:near]:
        total = total + one[...].astype(F32)
    own, outs, held = refs[near], refs[near + 1 : near + count], refs[near + count]
    slot = total.shape[1] // count
    for q in range(count):
        held[q] = total[:, q * slot : (q + 1) * slot]
    own[...] = held[here]
    for j in range(1, count):
        outs[j - 1][...] = held[here ^ j].astype(BF16)


def finish_kernel(scale, own, *refs):
    total = own[...]
    for one in refs[:-1]:
        total = total + one[...].astype(F32)
    refs[-1][...] = (total * scale).astype(BF16)


def widen_kernel(rows, count, spots, *refs):
    here = spots_of(spots, rows)["line"]
    parts, out, held = refs[:count], refs[count], refs[count + 1]
    slot = parts[0].shape[1]
    for j in range(count):
        held[here ^ j] = parts[j][...]
    for q in range(count):
        out[:, q * slot : (q + 1) * slot] = held[q]


def unpack_kernel(rows, spots, *refs):
    count = 2 * rows
    here = spots_of(spots, rows)
    parts = refs[: 2 * count]
    res, query, out, held, whole = refs[2 * count :]
    height = parts[0].shape[0]
    for c in range(2):
        for j in range(count):
            held[(here["core"] ^ c) * count + (here["square"] ^ j)] = parts[c * count + j][...]
    for q in range(2 * count):
        whole[q * height : (q + 1) * height, :] = held[q].astype(F32)
    channels = query.shape[0]
    for t in range(11):
        start = t * channels
        base = start // 128 * 128
        lead = start - base
        if lead:
            span = -(-(lead + channels) // 128) * 128
            piece = pltpu.roll(whole[:, base : base + span], span - lead, 1)[:, :channels]
        else:
            piece = whole[:, start : start + channels]
        piece = piece.astype(BF16)
        if t < 9:
            res[t] = piece
        elif t == 9:
            query[...] = piece
        else:
            out[...] = piece


def line_mask(j, rows):
    return j * 4 * rows


def square_mask(j, rows):
    return j // rows * 2 * rows + j % rows


def filter_step(spots, grad_hid, acts, query_grad, out_grad, cols, rows, lines):
    channels, cells = grad_hid.shape
    slot = -(-11 * channels // (128 * lines)) * 128
    width = slot * lines
    half = channels // 2
    return call(
        functools.partial(filter_kernel, rows, cols),
        [((half, width), F32), ((half, width), BF16)],
        [spots, grad_hid, acts, query_grad, out_grad],
        [
            pltpu.VMEM((channels, width), F32),
            pltpu.VMEM((2 * channels, cells), BF16),
            pltpu.VMEM((channels, -(-channels // 128) * 128), F32),
        ],
        flops=18 * channels * channels * cells,
        scalars=1,
        name="filter",
    )


def square_step(spots, kept, came, rows):
    squares = 2 * rows
    half, width = kept.shape
    height = half // squares
    return call(
        functools.partial(square_kernel, rows),
        [((height, width), F32)] + [((height, width), BF16)] * (squares - 1),
        [spots, kept, came],
        [pltpu.VMEM((squares, height, width), F32)],
        scalars=1,
        name="square",
    )


def line_step(spots, own, near, rows, lines):
    height, width = own.shape
    slot = width // lines
    return call(
        functools.partial(line_kernel, rows, lines, len(near) + 1),
        [((height, slot), F32)] + [((height, slot), BF16)] * (lines - 1),
        [spots, own, *near],
        [pltpu.VMEM((lines, height, slot), F32)],
        scalars=1,
        name="line",
    )


def widen_step(spots, final, far, rows):
    height, slot = final.shape
    lines = len(far) + 1
    return call(
        functools.partial(widen_kernel, rows, lines),
        [((height, slot * lines), BF16)],
        [spots, final, *far],
        [pltpu.VMEM((lines, height, slot), BF16)],
        scalars=1,
        name="widen",
    )[0]


def unpack_step(spots, mine, other, channels, rows):
    height, width = mine[0].shape
    squares = 2 * rows
    res, query, out = call(
        functools.partial(unpack_kernel, rows),
        [((9, channels, channels), BF16), ((channels, channels), BF16), ((channels, channels), BF16)],
        [spots, *mine, *other],
        [pltpu.VMEM((2 * squares, height, width), BF16), pltpu.VMEM((channels, width), F32)],
        scalars=1,
        name="unpack",
    )
    return res.reshape(3, 3, channels, channels), query, out


def gather_kernel(rows, lines, spots, group_of, *refs):
    count = 4 * rows
    parts = refs[:count]
    image_rows, all_rows, held = refs[count:]
    image, row = spots[0], spots[1]
    for k in range(count):
        for z in range(lines):
            held[k * lines + z] = parts[k][z]

    def spot(source, r):
        v = group_of[source] ^ image
        return (((v & 1) * 2 + ((v >> 1) & 1)) * rows + (row ^ r)) * lines + (v >> 2)

    height = image_rows.shape[1]
    for r in range(rows):
        image_rows[r] = held[spot(image, r)]
    for x in range(2):
        for z in range(lines):
            for c in range(2):
                p = (x * lines + z) * 2 + c
                for r in range(rows):
                    all_rows[p * rows + r] = held[spot(image ^ (z * 4 + x * 2 + c), r)]


def place_kernel(start, rows, blank, out, window, sem):
    span = window.shape[0]
    base = jnp.minimum((start[0] >> 4) << 4, out.shape[0] - span)
    token = lax.broadcasted_iota(jnp.int32, (span, SLOTS), 0)
    slot = lax.broadcasted_iota(jnp.int32, (span, SLOTS), 1)
    chosen = jnp.where(token == slot + (start[0] - base), 1.0, 0.0).astype(BF16)
    window[...] = product(chosen, rows[...], (1, 0)).astype(BF16)
    store = pltpu.make_async_copy(window, out.at[pl.ds(pl.multiple_of(base, 16), span), :], sem)
    store.start()
    store.wait()


def join_kernel(spots, own, came, out):
    width = own.shape[0]
    core = spots[0] & 1
    out[0:width, :] = jnp.where(core == 0, own[...], came[...])
    out[width : 2 * width, :] = jnp.where(core == 0, came[...], own[...])


def shards(
    llm_hidden,
    slot_start,
    image_group,
    timesteps,
    latents,
    noise,
    kv_weight,
    in_weight,
    res_weight,
    query_weight,
    out_weight,
    cotangent,
):
    rows = lax.axis_size("row")
    images = lax.axis_size("img")
    lines = images // 4
    channels = in_weight.shape[2]
    row_count, col_count = latents.shape[2:]
    cells = row_count * col_count
    tokens, features = llm_hidden.shape
    pair_width = kv_weight.shape[1]
    height = SLOTS // rows
    half = features // 2
    spots = jnp.stack([lax.axis_index("img"), lax.axis_index("row"), jnp.int32(rows)]).astype(jnp.int32)

    depth = latents.shape[1]
    noisy, *edges = call(
        functools.partial(noisy_kernel, rows),
        [((depth, row_count, col_count), F32)] + [((depth, 2, col_count), BF16)] * (1 if rows == 2 else 2),
        [spots, timesteps, latents, noise],
        scalars=2,
        name="noisy",
    )
    if rows == 2:
        far = [lax.ppermute(edges[0], "row", [(0, 1), (1, 0)])]
    else:
        far = [
            lax.ppermute(edges[0], "row", [(i, i + 1) for i in range(rows - 1)]),
            lax.ppermute(edges[1], "row", [(i + 1, i) for i in range(rows - 1)]),
        ]

    span = min(SLOTS + 16, tokens)
    pieces = 4 if features % 512 == 0 else 1
    kept, *rest = pl.pallas_call(
        functools.partial(condition_kernel, rows),
        out_shape=[jax.ShapeDtypeStruct((height, pair_width), F32)] * rows
        + [jax.ShapeDtypeStruct((SLOTS, half), BF16)] * 2,
        in_specs=[SMEM, SMEM, pl.BlockSpec(memory_space=pl.ANY), pl.BlockSpec(memory_space=pl.ANY)],
        out_specs=[VMEM] * (rows + 2),
        scratch_shapes=[
            pltpu.VMEM((span, features), BF16),
            pltpu.VMEM((features, pair_width), BF16),
            pltpu.VMEM((SLOTS, features), BF16),
            pltpu.VMEM((rows, height, pair_width), F32),
            pltpu.SemaphoreType.DMA,
            pltpu.SemaphoreType.DMA((pieces,)),
        ],
        cost_estimate=pl.CostEstimate(
            flops=2 * SLOTS * features * pair_width,
            bytes_accessed=2 * features * (pair_width + 3 * SLOTS),
            transcendentals=0,
        ),
        name="condition",
    )(spots, slot_start, llm_hidden, kv_weight)
    sent, mine, away = rest[: rows - 1], rest[rows - 1], rest[rows]

    band = kept
    for j in range(1, rows):
        band = band + swap(sent[j - 1], j)
    band = band.astype(BF16)
    column = [band] + [swap(band, line_mask(j, rows)) for j in range(1, lines)]
    plane = call(
        functools.partial(select_kernel, rows),
        [((height, pair_width), BF16)] * 4,
        [spots, image_group, *column],
        scalars=2,
        name="select",
    )
    band = plane[0].astype(F32)
    for k in range(1, 4):
        band = band + swap(plane[k], k * rows).astype(F32)
    band = band.astype(BF16)
    bands = [band] + [swap(band, j) for j in range(1, rows)]

    other = swap(away, rows)
    block = jnp.concatenate([mine, other])
    near = [block] + [swap(block, line_mask(j, rows)) for j in range(1, lines)]

    acts, hid, query = call(
        front_kernel,
        [
            ((3, channels, cells + 2 * col_count), BF16),
            ((channels, cells), BF16),
            ((channels, cells), BF16),
        ],
        [
            spots,
            noisy,
            *far,
            time_shift(timesteps[0], channels)[:, None],
            in_weight.transpose(0, 1, 3, 2).reshape(-1, channels),
            res_weight.reshape(9, channels, channels),
            query_weight,
        ],
        [pltpu.VMEM((9 * depth, cells + 2 * col_count), F32)],
        flops=20 * channels * channels * cells,
        scalars=1,
        name="front",
    )
    upstream = cotangent[0].reshape(channels, cells)
    block_out, kept, grad_hid, query_grad, out_grad, *sent = call(
        functools.partial(attention_kernel, rows),
        [
            ((channels, cells), BF16),
            ((height, pair_width), F32),
            ((channels, cells), BF16),
            ((channels, channels), F32),
            ((channels, channels), F32),
        ]
        + [((height, pair_width), BF16)] * (rows - 1),
        [spots, query, hid, upstream, query_weight, out_weight, *bands],
        [pltpu.VMEM((channels, cells), BF16)] * 3
        + [
            pltpu.VMEM((rows, height, pair_width), BF16),
            pltpu.VMEM((SLOTS, pair_width), BF16),
            pltpu.VMEM((SLOTS, pair_width), F32),
        ],
        flops=10 * channels * channels * cells + 12 * channels * SLOTS * cells,
        scalars=1,
        name="attention",
    )
    grad_band = kept
    for j in range(1, rows):
        grad_band = grad_band + swap(sent[j - 1], j).astype(F32)
    grad_band = grad_band.astype(BF16)
    kept, sent = filter_step(spots, grad_hid, acts, query_grad, out_grad, col_count, rows, lines)
    own, *outs = square_step(spots, kept, swap(sent, rows), rows)
    squares = 2 * rows
    came = [swap(outs[j - 1], square_mask(j, rows)) for j in range(1, squares)]
    own, *outs = line_step(spots, own, came, rows, lines)
    came = [swap(outs[j - 1], line_mask(j, rows)) for j in range(1, lines)]
    weight_scale = (images * rows * cells) ** (-0.5)
    (final,) = call(
        functools.partial(finish_kernel, weight_scale), [(own.shape, BF16)], [own, *came], name="finish"
    )
    came = [swap(final, line_mask(j, rows)) for j in range(1, lines)]
    wide = widen_step(spots, final, came, rows)
    mine_parts = [wide] + [swap(wide, square_mask(j, rows)) for j in range(1, squares)]
    other_parts = [swap(one, rows) for one in mine_parts]
    grad_res_weight, grad_query_weight, grad_out_weight = unpack_step(
        spots, mine_parts, other_parts, channels, rows
    )

    column = jnp.stack([grad_band] + [swap(grad_band, line_mask(j, rows)) for j in range(1, lines)])
    column = after(column, own)
    parts = [column] + [swap(column, square_mask(j, rows)) for j in range(1, squares)]
    parts = parts + [swap(one, rows) for one in parts]
    image_rows, all_rows = call(
        functools.partial(gather_kernel, rows, lines),
        [((rows, height, pair_width), BF16), ((images * rows, height, pair_width), BF16)],
        [spots, image_group, *parts],
        [pltpu.VMEM((4 * rows * lines, height, pair_width), BF16)],
        scalars=2,
        name="gather",
    )
    all_rows = all_rows.reshape(images * SLOTS, pair_width)
    near_half = images * SLOTS // 2
    near = near[: lines // 2] + [after(one, own) for one in near[lines // 2 :]]
    across = [swap(one, 2 * rows) for one in near]
    total = product(jnp.concatenate(near), all_rows[:near_half], (0, 0))
    total = total + product(jnp.concatenate(across), all_rows[near_half:], (0, 0))
    weight_half = (total * (images * SLOTS) ** (-0.5)).astype(BF16)
    (grad_kv_weight,) = call(
        join_kernel,
        [((features, pair_width), BF16)],
        [spots, weight_half, swap(weight_half, rows)],
        scalars=1,
        name="join",
    )
    grad_condition = product(image_rows.reshape(SLOTS, pair_width), kv_weight, (1, 1)).astype(BF16)
    grad_hidden = pl.pallas_call(
        place_kernel,
        out_shape=jax.ShapeDtypeStruct((tokens, features), BF16),
        in_specs=[SMEM, VMEM, pl.BlockSpec(memory_space=pl.ANY)],
        out_specs=pl.BlockSpec(memory_space=pl.ANY),
        scratch_shapes=[pltpu.VMEM((span, features), BF16), pltpu.SemaphoreType.DMA],
        input_output_aliases={2: 0},
        name="place",
    )(slot_start, grad_condition, jnp.zeros((tokens, features), BF16))
    return (
        block_out.reshape(1, channels, row_count, col_count),
        grad_hidden,
        grad_kv_weight,
        grad_res_weight,
        grad_query_weight,
        grad_out_weight,
    )


def solution(mesh):
    return jax.shard_map(
        shards,
        mesh=mesh,
        in_specs=(
            P("img", "row"),
            P("img"),
            P(),
            P("img"),
            P("img", None, "row", None),
            P("img", None, "row", None),
            P("row", None),
            P(),
            P(),
            P(),
            P(),
            P("img", None, "row", None),
        ),
        out_specs=(P("img", None, "row", None), P("img", "row"), P("row", None), P(), P(), P()),
        check_vma=False,
    )
```

```python
import functools
import math

import jax
import jax.numpy as jnp
from jax import lax
from jax.experimental import pallas as pl
from jax.experimental.pallas import tpu as pltpu
from jax.sharding import PartitionSpec as P


HEAD_DIM = 64
SLOTS = 64
GRID = ("img", "row")
F32 = jnp.float32
BF16 = jnp.bfloat16
VMEM = pl.BlockSpec(memory_space=pltpu.VMEM)
SMEM = pl.BlockSpec(memory_space=pltpu.SMEM)


LIMIT = 30 * 2**20


def near_core(array):
    return pltpu.with_memory_space_constraint(array, pltpu.VMEM)


def call(kernel, outs, ins, scratch=(), flops=0, scalars=0, leave=()):
    outs = [jax.ShapeDtypeStruct(shape, kind) for shape, kind in outs]
    moved = sum(math.prod(x.shape) * x.dtype.itemsize for x in [*outs, *ins])
    ins = [x if k < scalars else near_core(x) for k, x in enumerate(ins)]
    return pl.pallas_call(
        kernel,
        out_shape=[x if k in leave else pltpu.VMEM(x.shape, x.dtype) for k, x in enumerate(outs)],
        in_specs=[SMEM] * scalars + [VMEM] * (len(ins) - scalars),
        out_specs=[VMEM] * len(outs),
        scratch_shapes=list(scratch),
        cost_estimate=pl.CostEstimate(flops=flops, bytes_accessed=moved, transcendentals=0),
        compiler_params=pltpu.CompilerParams(vmem_limit_bytes=LIMIT),
    )(*ins)


def product(left, right, sides):
    return lax.dot_general(left, right, ((sides[:1], sides[1:]), ((), ())), preferred_element_type=F32)


def time_shift(timestep, channel_total):
    half_count = channel_total // 2
    frequency = jnp.exp(-math.log(10000.0) * jnp.arange(half_count, dtype=jnp.float32) / half_count)
    angles = timestep.astype(jnp.float32) * frequency
    return jnp.concatenate([jnp.cos(angles), jnp.sin(angles)])


def swap(block, mask):
    total = lax.axis_size("img") * lax.axis_size("row")
    return lax.ppermute(block, GRID, [(i, i ^ mask) for i in range(total)])


def spots_of(rows):
    image, row = lax.axis_index("img"), lax.axis_index("row")
    return {
        "image": image,
        "core": image & 1,
        "row": row,
        "square": ((image >> 1) & 1) * rows + row,
        "line": image >> 2,
        "plane": image & 3,
    }


def noisy_kernel(rows, timestep, latents, noise, noisy, *edges):
    step = timestep[0]
    index = lax.broadcasted_iota(jnp.int32, (8, 128), 0) * 128 + lax.broadcasted_iota(
        jnp.int32, (8, 128), 1
    )
    low, high = 0.00085**0.5, 0.012**0.5
    beta = (low + index.astype(F32) * ((high - low) / 999.0)) ** 2
    logs = jnp.where(index <= step, jnp.log(1.0 - jnp.where(index < 1000, beta, 0.0)), 0.0)
    total = jnp.sum(jnp.sum(logs, axis=1, keepdims=True), axis=0, keepdims=True)
    level = jnp.exp(total)
    keep, mix = jnp.sqrt(level), jnp.sqrt(1.0 - level)
    height = latents.shape[2]
    for c in range(latents.shape[1]):
        value = (keep * latents[0, c] + mix * noise[0, c]).astype(BF16).astype(F32)
        noisy[c] = value
        head, tail = value[:2].astype(BF16), value[height - 2 :].astype(BF16)
        if rows == 2:
            edges[0][c] = jnp.where(spots_of(rows)["row"] == 0, tail, head)
        else:
            edges[0][c] = tail
            edges[1][c] = head


def condition_kernel(rows, start, hidden, weight, kept, *refs):
    sent, mine, away = refs[: rows - 1], refs[rows - 1], refs[rows]
    window, weights, cond, held, row_sem, sems = refs[rows + 1 :]
    here = spots_of(rows)
    pieces = sems.shape[0]
    depth = weight.shape[0] // pieces
    span = window.shape[0]
    base = jnp.minimum((start[0] >> 4) << 4, hidden.shape[0] - span)
    load = pltpu.make_async_copy(hidden.at[pl.ds(pl.multiple_of(base, 16), span), :], window, row_sem)
    load.start()
    loads = [
        pltpu.make_async_copy(
            weight.at[k * depth : (k + 1) * depth, :], weights.at[k * depth : (k + 1) * depth, :], sems.at[k]
        )
        for k in range(pieces)
    ]
    for one in loads:
        one.start()
    load.wait()
    slot = lax.broadcasted_iota(jnp.int32, (SLOTS, span), 0)
    token = lax.broadcasted_iota(jnp.int32, (SLOTS, span), 1)
    chosen = jnp.where(token == slot + (start[0] - base), 1.0, 0.0).astype(BF16)
    cond[...] = product(chosen, window[...], (1, 0)).astype(BF16)
    half = cond.shape[1] // 2
    left, right = cond[:, :half], cond[:, half:]
    mine[...] = jnp.where(here["core"] == 0, left, right)
    away[...] = jnp.where(here["core"] == 0, right, left)
    total = None
    for k in range(pieces):
        loads[k].wait()
        one = product(cond[:, k * depth : (k + 1) * depth], weights[k * depth : (k + 1) * depth, :], (1, 0))
        total = one if total is None else total + one
    height = SLOTS // rows
    for r in range(rows):
        held[r] = total[r * height : (r + 1) * height]
    kept[...] = held[here["row"]]
    for j in range(1, rows):
        sent[j - 1][...] = held[here["row"] ^ j]


def select_kernel(rows, group_of, *refs):
    lines = len(refs) - 4
    here = spots_of(rows)
    for k in range(4):
        target = here["line"] * 4 + (here["plane"] ^ k)
        chosen = jnp.zeros(refs[0].shape, F32)
        for j in range(lines):
            goes = group_of[(here["line"] ^ j) * 4 + here["plane"]] == target
            chosen = chosen + jnp.where(goes, refs[j][...].astype(F32), 0.0)
        refs[lines + k][...] = chosen.astype(BF16)


def front_kernel(rows_total, noisy, *refs):
    far = refs[:-8]
    shift, in_weight, res_weight, query_weight, acts, hid, query, patches = refs[-8:]
    rows, cols = noisy.shape[1:]
    cells = rows * cols
    row = lax.axis_index("row")
    inner, outer = row > 0, row < rows_total - 1
    above = jnp.where(inner, far[0][...].astype(F32), 0.0)
    below = jnp.where(outer, far[-1][...].astype(F32), 0.0)
    lane = lax.broadcasted_iota(jnp.int32, (noisy.shape[0], cols), 1)
    depth = noisy.shape[0]
    for r in range(rows + 4):
        if r < 2:
            line = above[:, r]
        elif r < rows + 2:
            line = noisy[:, r - 2]
        else:
            line = below[:, r - rows - 2]
        turned = [
            jnp.where(lane == 0, 0.0, pltpu.roll(line, 1, 1)),
            line,
            jnp.where(lane == cols - 1, 0.0, pltpu.roll(line, cols - 1, 1)),
        ]
        for a in range(3):
            if 0 <= r - a < rows + 2:
                for b in range(3):
                    k = 3 * a + b
                    patches[k * depth : (k + 1) * depth, (r - a) * cols : (r - a + 1) * cols] = turned[b]
    first = product(in_weight[...], patches[...].astype(BF16), (0, 0))
    act = jax.nn.silu(first + shift[...])
    lane = lax.broadcasted_iota(jnp.int32, (act.shape[0], cols), 1)
    for r in range(rows + 2):
        band = act[:, r * cols : (r + 1) * cols]
        if r == 0:
            band = jnp.where(inner, band, 0.0)
        if r == rows + 1:
            band = jnp.where(outer, band, 0.0)
        spot = slice(r * cols, (r + 1) * cols)
        acts[1, :, spot] = band.astype(BF16)
        acts[0, :, spot] = jnp.where(lane == 0, 0.0, pltpu.roll(band, 1, 1)).astype(BF16)
        acts[2, :, spot] = jnp.where(lane == cols - 1, 0.0, pltpu.roll(band, cols - 1, 1)).astype(BF16)
    total = first[:, cols : cols + cells]
    for a in range(3):
        for b in range(3):
            total = total + product(res_weight[3 * a + b], acts[b, :, a * cols : a * cols + cells], (1, 0))
    low = total.astype(BF16)
    hid[...] = low
    query[...] = product(query_weight[...], low, (1, 0)).astype(BF16)


def attention_kernel(rows, query, hid, upstream, query_weight, out_weight, *refs):
    bands = refs[:rows]
    block_out, kept, grad_hid, query_grad, out_grad = refs[rows : rows + 5]
    sent = refs[rows + 5 : 2 * rows + 4]
    grad_att, attended, grad_query, held, pairs, grad_pairs = refs[2 * rows + 4 :]
    channels = hid.shape[0]
    here = spots_of(rows)
    height = SLOTS // rows
    for j in range(rows):
        held[here["row"] ^ j] = bands[j][...]
    for r in range(rows):
        pairs[r * height : (r + 1) * height, :] = held[r]
    scale = HEAD_DIM**-0.5
    grad_att[...] = product(out_weight[...], upstream[...], (0, 0)).astype(BF16)
    for h in range(channels // HEAD_DIM):
        spot = slice(h * HEAD_DIM, (h + 1) * HEAD_DIM)
        keys = pairs[:, h * HEAD_DIM : (h + 1) * HEAD_DIM]
        vals = pairs[:, channels + h * HEAD_DIM : channels + (h + 1) * HEAD_DIM]
        one = query[spot, :]
        score = product(keys, one, (1, 0)) * scale
        grown = jnp.exp(score - jnp.max(score, axis=0, keepdims=True))
        probs = grown / jnp.sum(grown, axis=0, keepdims=True)
        low = probs.astype(BF16)
        attended[spot, :] = product(vals, low, (0, 0)).astype(BF16)
        back = grad_att[spot, :]
        grad_prob = product(vals, back, (1, 0))
        inner = jnp.sum(probs * grad_prob, axis=0, keepdims=True)
        grad_score = (scale * probs * (grad_prob - inner)).astype(BF16)
        grad_query[spot, :] = product(keys, grad_score, (0, 0)).astype(BF16)
        grad_pairs[:, h * HEAD_DIM : (h + 1) * HEAD_DIM] = product(grad_score, one, (1, 1))
        grad_pairs[:, channels + h * HEAD_DIM : channels + (h + 1) * HEAD_DIM] = product(low, back, (1, 1))
    kept[...] = grad_pairs[pl.ds(pl.multiple_of(here["row"] * height, 8), height), :]
    for j in range(1, rows):
        spot = pl.ds(pl.multiple_of((here["row"] ^ j) * height, 8), height)
        sent[j - 1][...] = grad_pairs[spot, :].astype(BF16)
    block_out[...] = (
        hid[...].astype(F32) + product(out_weight[...], attended[...], (1, 0))
    ).astype(BF16)
    grad_hid[...] = (
        upstream[...].astype(F32) + product(query_weight[...], grad_query[...], (0, 0))
    ).astype(BF16)
    query_grad[...] = product(grad_query[...], hid[...], (1, 1))
    out_grad[...] = product(upstream[...], attended[...], (1, 1))


def filter_kernel(rows, cols, grad_hid, acts, query_grad, out_grad, kept, sent, whole, pair, wide):
    channels, cells = grad_hid.shape
    for t in range(0, 9, 2):
        taps = [t, t + 1] if t < 8 else [t]
        for k, tap in enumerate(taps):
            a, b = tap // 3, tap % 3
            pair[k * channels : (k + 1) * channels, :] = acts[b, :, a * cols : a * cols + cells]
        span = len(taps) * channels
        whole[:, t * channels : t * channels + span] = product(grad_hid[...], pair[:span, :], (1, 1))
    edge = 9 * channels
    base = edge // 128 * 128
    lead = edge - base
    wide[:, :channels] = query_grad[...]
    turned = pltpu.roll(wide[...], lead, 1) if lead else wide[...]
    lane = lax.broadcasted_iota(jnp.int32, (channels, 128), 1)
    whole[:, base : base + 128] = jnp.where(lane < lead, whole[:, base : base + 128], turned[:, :128])
    whole[:, base + 128 : edge + channels] = turned[:, 128 : lead + channels]
    whole[:, edge + channels : edge + 2 * channels] = out_grad[...]
    rest = whole.shape[1] - edge - 2 * channels
    if rest:
        whole[:, edge + 2 * channels :] = jnp.zeros((channels, rest), F32)
    half = channels // 2
    core = spots_of(rows)["core"]
    pieces, height = kept.shape[:2]
    for q in range(pieces):
        if height % 8 == 0:
            kept[q] = whole[pl.ds(pl.multiple_of(core * half + q * height, 8), height), :]
            away = whole[pl.ds(pl.multiple_of((1 - core) * half + q * height, 8), height), :]
        else:
            low = whole[q * height : (q + 1) * height, :]
            high = whole[half + q * height : half + (q + 1) * height, :]
            kept[q] = jnp.where(core == 0, low, high)
            away = jnp.where(core == 0, high, low)
        sent[q] = away.astype(BF16)


def square_kernel(rows, kept, came, own, *outs):
    here = spots_of(rows)["square"]
    own[...] = kept[here] + came[here].astype(F32)
    for j in range(1, 2 * rows):
        outs[j - 1][...] = (kept[here ^ j] + came[here ^ j].astype(F32)).astype(BF16)


def line_kernel(rows, count, near, *refs):
    here = spots_of(rows)["line"]
    total = refs[0][...]
    for one in refs[1:near]:
        total = total + one[...].astype(F32)
    own, outs, held = refs[near], refs[near + 1 : near + count], refs[near + count]
    slot = total.shape[1] // count
    held[...] = total
    own[...] = held[:, pl.ds(pl.multiple_of(here * slot, 128), slot)]
    for j in range(1, count):
        spot = pl.ds(pl.multiple_of((here ^ j) * slot, 128), slot)
        outs[j - 1][...] = held[:, spot].astype(BF16)


def unpack_kernel(rows, lines, *refs):
    count = 2 * rows
    here = spots_of(rows)
    parts = refs[: 2 * count]
    res, query, out, whole, *spare = refs[2 * count :]
    height = parts[0].shape[0]
    slot = parts[0].shape[1] // lines
    for c in range(2):
        for j in range(count):
            piece = parts[c * count + j][...].astype(F32)
            spot = (here["core"] ^ c) * count + (here["square"] ^ j)
            for z in range(lines):
                lanes = pl.ds(pl.multiple_of((here["line"] ^ z) * slot, 128), slot)
                one = piece[:, z * slot : (z + 1) * slot]
                if spare:
                    spare[0][spot, :, lanes] = one
                else:
                    whole[pl.ds(pl.multiple_of(spot * height, 8), height), lanes] = one
    if spare:
        for q in range(2 * count):
            whole[q * height : (q + 1) * height, :] = spare[0][q]
    channels = query.shape[0]
    for t in range(11):
        start = t * channels
        base = start // 128 * 128
        lead = start - base
        if lead:
            span = -(-(lead + channels) // 128) * 128
            piece = pltpu.roll(whole[:, base : base + span], span - lead, 1)[:, :channels]
        else:
            piece = whole[:, start : start + channels]
        piece = piece.astype(BF16)
        if t < 9:
            res[t] = piece
        elif t == 9:
            query[...] = piece
        else:
            out[...] = piece


def line_mask(j, rows):
    return j * 4 * rows


def square_mask(j, rows):
    return j // rows * 2 * rows + j % rows


def filter_step(grad_hid, acts, query_grad, out_grad, cols, rows, lines):
    channels, cells = grad_hid.shape
    slot = -(-11 * channels // (128 * lines)) * 128
    width = slot * lines
    half = channels // 2
    return call(
        functools.partial(filter_kernel, rows, cols),
        [((2 * rows, half // rows // 2, width), F32), ((2 * rows, half // rows // 2, width), BF16)],
        [grad_hid, acts, query_grad, out_grad],
        [
            pltpu.VMEM((channels, width), F32),
            pltpu.VMEM((2 * channels, cells), BF16),
            pltpu.VMEM((channels, -(-channels // 128) * 128), F32),
        ],
        flops=18 * channels * channels * cells,
    )


def square_step(kept, came, rows):
    squares, height, width = kept.shape
    return call(
        functools.partial(square_kernel, rows),
        [((height, width), F32)] + [((height, width), BF16)] * (squares - 1),
        [kept, came],
    )


def line_step(own, near, rows, lines):
    height, width = own.shape
    slot = width // lines
    return call(
        functools.partial(line_kernel, rows, lines, len(near) + 1),
        [((height, slot), F32)] + [((height, slot), BF16)] * (lines - 1),
        [own, *near],
        [pltpu.VMEM((height, width), F32)],
    )


def unpack_step(mine, other, channels, rows, lines):
    height = mine[0].shape[0]
    res, query, out = call(
        functools.partial(unpack_kernel, rows, lines),
        [((9, channels, channels), BF16), ((channels, channels), BF16), ((channels, channels), BF16)],
        [*mine, *other],
        [pltpu.VMEM((channels, mine[0].shape[1]), F32)]
        + [pltpu.VMEM((channels // height, height, mine[0].shape[1]), F32)] * (height % 8 > 0),
        leave=(0, 1, 2),
    )
    return res.reshape(3, 3, channels, channels), query, out


def gather_kernel(rows, lines, group_of, *refs):
    count = 4 * rows
    parts = refs[:count]
    image_rows, all_rows, held = refs[count:]
    image, row = lax.axis_index("img"), lax.axis_index("row")
    for k in range(count):
        for z in range(lines):
            held[k * lines + z] = parts[k][z]

    def spot(source, r):
        v = group_of[source] ^ image
        return (((v & 1) * 2 + ((v >> 1) & 1)) * rows + (row ^ r)) * lines + (v >> 2)

    for r in range(rows):
        image_rows[r] = held[spot(image, r)]
    for x in range(2):
        for z in range(lines):
            for c in range(2):
                p = (x * lines + z) * 2 + c
                for r in range(rows):
                    all_rows[p * rows + r] = held[spot(image ^ (z * 4 + x * 2 + c), r)]


def place_kernel(start, rows, blank, out, window, sem):
    span = window.shape[0]
    base = jnp.minimum((start[0] >> 4) << 4, out.shape[0] - span)
    token = lax.broadcasted_iota(jnp.int32, (span, SLOTS), 0)
    slot = lax.broadcasted_iota(jnp.int32, (span, SLOTS), 1)
    chosen = jnp.where(token == slot + (start[0] - base), 1.0, 0.0).astype(BF16)
    window[...] = product(chosen, rows[...], (1, 0)).astype(BF16)
    store = pltpu.make_async_copy(window, out.at[pl.ds(pl.multiple_of(base, 16), span), :], sem)
    store.start()
    store.wait()


def join_kernel(own, came, out, sems):
    width = own.shape[0]
    core = lax.axis_index("img") & 1
    count = sems.shape[1]
    depth = width // count
    stores = []
    for k in range(count):
        for side, one in enumerate((own, came)):
            start = (core if side == 0 else 1 - core) * width + k * depth
            target = out.at[pl.ds(pl.multiple_of(start, 8), depth), :]
            stores.append(pltpu.make_async_copy(one.at[k * depth : (k + 1) * depth, :], target, sems.at[side, k]))
    for one in stores:
        one.start()
    for one in stores:
        one.wait()


def blank_kernel(out, zeros, sems):
    zeros[...] = jnp.zeros(zeros.shape, zeros.dtype)
    depth = zeros.shape[0]
    count = out.shape[0] // depth
    stores = [
        pltpu.make_async_copy(zeros, out.at[k * depth : (k + 1) * depth, :], sems.at[k]) for k in range(count)
    ]
    for one in stores:
        one.start()
    for one in stores:
        one.wait()


def shards(
    llm_hidden,
    slot_start,
    image_group,
    timesteps,
    latents,
    noise,
    kv_weight,
    in_weight,
    res_weight,
    query_weight,
    out_weight,
    cotangent,
):
    rows = lax.axis_size("row")
    images = lax.axis_size("img")
    lines = images // 4
    channels = in_weight.shape[2]
    row_count, col_count = latents.shape[2:]
    cells = row_count * col_count
    tokens, features = llm_hidden.shape
    pair_width = kv_weight.shape[1]
    height = SLOTS // rows
    half = features // 2

    depth = latents.shape[1]
    noisy, *edges = call(
        functools.partial(noisy_kernel, rows),
        [((depth, row_count, col_count), F32)] + [((depth, 2, col_count), BF16)] * (1 if rows == 2 else 2),
        [timesteps, latents, noise],
        scalars=1,
    )
    if rows == 2:
        far = [lax.ppermute(edges[0], "row", [(0, 1), (1, 0)])]
    else:
        far = [
            lax.ppermute(edges[0], "row", [(i, i + 1) for i in range(rows - 1)]),
            lax.ppermute(edges[1], "row", [(i + 1, i) for i in range(rows - 1)]),
        ]

    span = min(SLOTS + 16, tokens)
    pieces = 4 if features % 512 == 0 else 1
    kept, *rest = pl.pallas_call(
        functools.partial(condition_kernel, rows),
        out_shape=[jax.ShapeDtypeStruct((height, pair_width), F32)] * rows
        + [jax.ShapeDtypeStruct((SLOTS, half), BF16)] * 2,
        in_specs=[SMEM, pl.BlockSpec(memory_space=pl.ANY), pl.BlockSpec(memory_space=pl.ANY)],
        out_specs=[VMEM] * (rows + 2),
        scratch_shapes=[
            pltpu.VMEM((span, features), BF16),
            pltpu.VMEM((features, pair_width), BF16),
            pltpu.VMEM((SLOTS, features), BF16),
            pltpu.VMEM((rows, height, pair_width), F32),
            pltpu.SemaphoreType.DMA,
            pltpu.SemaphoreType.DMA((pieces,)),
        ],
        cost_estimate=pl.CostEstimate(
            flops=2 * SLOTS * features * pair_width,
            bytes_accessed=2 * features * (pair_width + 3 * SLOTS),
            transcendentals=0,
        ),
        name="condition",
    )(slot_start, llm_hidden, kv_weight)
    sent, mine, away = rest[: rows - 1], rest[rows - 1], rest[rows]

    band = kept
    for j in range(1, rows):
        band = band + swap(sent[j - 1], j)
    band = band.astype(BF16)
    column = [band] + [swap(band, line_mask(j, rows)) for j in range(1, lines)]
    upstream = cotangent[0].reshape(channels, cells)
    shift = time_shift(timesteps[0], channels)[:, None]
    in_flat = in_weight.transpose(0, 1, 3, 2).reshape(-1, channels)
    column[0], upstream, shift, in_flat = lax.optimization_barrier((column[0], upstream, shift, in_flat))
    plane = call(
        functools.partial(select_kernel, rows), [((height, pair_width), BF16)] * 4, [image_group, *column], scalars=1
    )
    band = plane[0].astype(F32)
    for k in range(1, 4):
        band = band + swap(plane[k], k * rows).astype(F32)
    band = band.astype(BF16)
    bands = [band] + [swap(band, j) for j in range(1, rows)]

    other = swap(away, rows)
    block = jnp.concatenate([mine, other])
    near = [block] + [swap(block, line_mask(j, rows)) for j in range(1, lines)]

    acts, hid, query = call(
        functools.partial(front_kernel, rows),
        [
            ((3, channels, cells + 2 * col_count), BF16),
            ((channels, cells), BF16),
            ((channels, cells), BF16),
        ],
        [
            noisy,
            *far,
            shift,
            in_flat,
            res_weight.reshape(9, channels, channels),
            query_weight,
        ],
        [pltpu.VMEM((9 * depth, cells + 2 * col_count), F32)],
        flops=20 * channels * channels * cells,
    )
    block_out, kept, grad_hid, query_grad, out_grad, *sent = call(
        functools.partial(attention_kernel, rows),
        [
            ((channels, cells), BF16),
            ((height, pair_width), F32),
            ((channels, cells), BF16),
            ((channels, channels), F32),
            ((channels, channels), F32),
        ]
        + [((height, pair_width), BF16)] * (rows - 1),
        [query, hid, upstream, query_weight, out_weight, *bands],
        [pltpu.VMEM((channels, cells), BF16)] * 3
        + [
            pltpu.VMEM((rows, height, pair_width), BF16),
            pltpu.VMEM((SLOTS, pair_width), BF16),
            pltpu.VMEM((SLOTS, pair_width), F32),
        ],
        flops=10 * channels * channels * cells + 12 * channels * SLOTS * cells,
    )
    grad_band = kept
    for j in range(1, rows):
        grad_band = grad_band + swap(sent[j - 1], j).astype(F32)
    grad_band = grad_band.astype(BF16)
    kept, sent = filter_step(grad_hid, acts, query_grad, out_grad, col_count, rows, lines)
    own, *outs = square_step(kept, swap(sent, rows), rows)
    blank = pl.pallas_call(
        blank_kernel,
        out_shape=jax.ShapeDtypeStruct((tokens, features), BF16),
        out_specs=pl.BlockSpec(memory_space=pl.ANY),
        scratch_shapes=[
            pltpu.VMEM((tokens // 8, features), BF16),
            pltpu.SemaphoreType.DMA((8,)),
        ],
        name="blank",
    )()
    block_out = block_out.reshape(1, channels, row_count, col_count)
    own, block_out = lax.optimization_barrier((own, block_out))
    squares = 2 * rows
    came = [swap(outs[j - 1], square_mask(j, rows)) for j in range(1, squares)]
    own, *outs = line_step(own, came, rows, lines)
    came = [swap(outs[j - 1], line_mask(j, rows)) for j in range(1, lines)]
    weight_scale = (images * rows * cells) ** (-0.5)
    for one in came:
        own = own + one.astype(F32)
    final = (own * weight_scale).astype(BF16)
    far = [swap(final, line_mask(j, rows)) for j in range(1, lines)]

    column = jnp.stack([grad_band] + [swap(grad_band, line_mask(j, rows)) for j in range(1, lines)])
    parts = [column] + [swap(column, square_mask(j, rows)) for j in range(1, squares)]
    parts = parts + [swap(one, rows) for one in parts]
    image_rows, all_rows = call(
        functools.partial(gather_kernel, rows, lines),
        [((rows, height, pair_width), BF16), ((images * rows, height, pair_width), BF16)],
        [image_group, *parts],
        [pltpu.VMEM((4 * rows * lines, height, pair_width), BF16)],
        scalars=1,
    )
    all_rows = all_rows.reshape(images * SLOTS, pair_width)
    grad_condition = product(image_rows.reshape(SLOTS, pair_width), kv_weight, (1, 1)).astype(BF16)
    grad_hidden = pl.pallas_call(
        place_kernel,
        out_shape=jax.ShapeDtypeStruct((tokens, features), BF16),
        in_specs=[SMEM, VMEM, pl.BlockSpec(memory_space=pl.ANY)],
        out_specs=pl.BlockSpec(memory_space=pl.ANY),
        scratch_shapes=[pltpu.VMEM((span, features), BF16), pltpu.SemaphoreType.DMA],
        input_output_aliases={2: 0},
        name="place",
    )(slot_start, grad_condition, blank)
    wide = jnp.concatenate([final, *far], axis=1)
    parts = [wide] + [swap(wide, square_mask(j, rows)) for j in range(1, squares)]

    near_half = images * SLOTS // 2
    across = [swap(near[j], 2 * rows) for j in range(lines)]
    total = product(jnp.concatenate(near), all_rows[:near_half], (0, 0))
    total = total + product(jnp.concatenate(across), all_rows[near_half:], (0, 0))
    weight_half = (total * (images * SLOTS) ** (-0.5)).astype(BF16)
    came = swap(weight_half, rows)
    grad_kv_weight = pl.pallas_call(
        join_kernel,
        out_shape=jax.ShapeDtypeStruct((features, pair_width), BF16),
        in_specs=[VMEM, VMEM],
        out_specs=pl.BlockSpec(memory_space=pl.ANY),
        scratch_shapes=[pltpu.SemaphoreType.DMA((2, 4 if half % 64 == 0 else 1))],
        compiler_params=pltpu.CompilerParams(vmem_limit_bytes=LIMIT),
        name="join",
    )(near_core(weight_half), near_core(came))
    others = [swap(one, rows) for one in parts]
    grad_res_weight, grad_query_weight, grad_out_weight = unpack_step(
        parts, others, channels, rows, lines
    )
    return (
        block_out,
        grad_hidden,
        grad_kv_weight,
        grad_res_weight,
        grad_query_weight,
        grad_out_weight,
    )


def solution(mesh):
    return jax.shard_map(
        shards,
        mesh=mesh,
        in_specs=(
            P("img", "row"),
            P("img"),
            P(),
            P("img"),
            P("img", None, "row", None),
            P("img", None, "row", None),
            P("row", None),
            P(),
            P(),
            P(),
            P(),
            P("img", None, "row", None),
        ),
        out_specs=(P("img", None, "row", None), P("img", "row"), P("row", None), P(), P(), P()),
        check_vma=False,
    )
```

```python
import functools
import math

import jax
import jax.numpy as jnp
from jax import lax
from jax.experimental import pallas as pl
from jax.experimental.pallas import tpu as pltpu
from jax.sharding import PartitionSpec as P


HEAD_DIM = 64
SLOTS = 64
GRID = ("img", "row")
F32 = jnp.float32
BF16 = jnp.bfloat16
VMEM = pl.BlockSpec(memory_space=pltpu.VMEM)
SMEM = pl.BlockSpec(memory_space=pltpu.SMEM)


LIMIT = 20 * 2**20


def near_core(array):
    return pltpu.with_memory_space_constraint(array, pltpu.VMEM)


def call(kernel, outs, ins, scratch=(), flops=0, scalars=0, leave=()):
    outs = [jax.ShapeDtypeStruct(shape, kind) for shape, kind in outs]
    moved = sum(math.prod(x.shape) * x.dtype.itemsize for x in [*outs, *ins])
    ins = [x if k < scalars else near_core(x) for k, x in enumerate(ins)]
    return pl.pallas_call(
        kernel,
        out_shape=[x if k in leave else pltpu.VMEM(x.shape, x.dtype) for k, x in enumerate(outs)],
        in_specs=[SMEM] * scalars + [VMEM] * (len(ins) - scalars),
        out_specs=[VMEM] * len(outs),
        scratch_shapes=list(scratch),
        cost_estimate=pl.CostEstimate(flops=flops, bytes_accessed=moved, transcendentals=0),
        compiler_params=pltpu.CompilerParams(vmem_limit_bytes=LIMIT),
    )(*ins)


def product(left, right, sides):
    return lax.dot_general(left, right, ((sides[:1], sides[1:]), ((), ())), preferred_element_type=F32)


def time_shift(timestep, channel_total):
    half_count = channel_total // 2
    frequency = jnp.exp(-math.log(10000.0) * jnp.arange(half_count, dtype=jnp.float32) / half_count)
    angles = timestep.astype(jnp.float32) * frequency
    return jnp.concatenate([jnp.cos(angles), jnp.sin(angles)])


def swap(block, mask):
    total = lax.axis_size("img") * lax.axis_size("row")
    return lax.ppermute(block, GRID, [(i, i ^ mask) for i in range(total)])


def spots_of(rows):
    image, row = lax.axis_index("img"), lax.axis_index("row")
    return {
        "image": image,
        "core": image & 1,
        "row": row,
        "square": ((image >> 1) & 1) * rows + row,
        "line": image >> 2,
        "plane": image & 3,
    }


def noisy_kernel(rows, timestep, latents, noise, noisy, *edges):
    step = timestep[0]
    index = lax.broadcasted_iota(jnp.int32, (8, 128), 0) * 128 + lax.broadcasted_iota(
        jnp.int32, (8, 128), 1
    )
    low, high = 0.00085**0.5, 0.012**0.5
    beta = (low + index.astype(F32) * ((high - low) / 999.0)) ** 2
    logs = jnp.where(index <= step, jnp.log(1.0 - jnp.where(index < 1000, beta, 0.0)), 0.0)
    total = jnp.sum(jnp.sum(logs, axis=1, keepdims=True), axis=0, keepdims=True)
    level = jnp.exp(total)
    keep, mix = jnp.sqrt(level), jnp.sqrt(1.0 - level)
    height = latents.shape[2]
    for c in range(latents.shape[1]):
        value = (keep * latents[0, c] + mix * noise[0, c]).astype(BF16).astype(F32)
        noisy[c] = value
        head, tail = value[:2].astype(BF16), value[height - 2 :].astype(BF16)
        if rows == 2:
            edges[0][c] = jnp.where(spots_of(rows)["row"] == 0, tail, head)
        else:
            edges[0][c] = tail
            edges[1][c] = head


def condition_kernel(rows, start, hidden, weight, kept, *refs):
    sent, mine, away = refs[: rows - 1], refs[rows - 1], refs[rows]
    window, weights, cond, held, row_sem, sems = refs[rows + 1 :]
    here = spots_of(rows)
    pieces = sems.shape[0]
    depth = weight.shape[0] // pieces
    span = window.shape[0]
    base = jnp.minimum((start[0] >> 4) << 4, hidden.shape[0] - span)
    load = pltpu.make_async_copy(hidden.at[pl.ds(pl.multiple_of(base, 16), span), :], window, row_sem)
    load.start()
    loads = [
        pltpu.make_async_copy(
            weight.at[k * depth : (k + 1) * depth, :], weights.at[k * depth : (k + 1) * depth, :], sems.at[k]
        )
        for k in range(pieces)
    ]
    for one in loads:
        one.start()
    load.wait()
    slot = lax.broadcasted_iota(jnp.int32, (SLOTS, span), 0)
    token = lax.broadcasted_iota(jnp.int32, (SLOTS, span), 1)
    chosen = jnp.where(token == slot + (start[0] - base), 1.0, 0.0).astype(BF16)
    cond[...] = product(chosen, window[...], (1, 0)).astype(BF16)
    half = cond.shape[1] // 2
    left, right = cond[:, :half], cond[:, half:]
    mine[...] = jnp.where(here["core"] == 0, left, right)
    away[...] = jnp.where(here["core"] == 0, right, left)
    total = None
    for k in range(pieces):
        loads[k].wait()
        one = product(cond[:, k * depth : (k + 1) * depth], weights[k * depth : (k + 1) * depth, :], (1, 0))
        total = one if total is None else total + one
    height = SLOTS // rows
    for r in range(rows):
        held[r] = total[r * height : (r + 1) * height]
    kept[...] = held[here["row"]]
    for j in range(1, rows):
        sent[j - 1][...] = held[here["row"] ^ j]


def select_kernel(rows, group_of, *refs):
    lines = len(refs) - 4
    here = spots_of(rows)
    for k in range(4):
        target = here["line"] * 4 + (here["plane"] ^ k)
        chosen = jnp.zeros(refs[0].shape, F32)
        for j in range(lines):
            goes = group_of[(here["line"] ^ j) * 4 + here["plane"]] == target
            chosen = chosen + jnp.where(goes, refs[j][...].astype(F32), 0.0)
        refs[lines + k][...] = chosen.astype(BF16)


def front_kernel(rows_total, noisy, *refs):
    far = refs[:-8]
    shift, in_weight, res_weight, query_weight, acts, hid, query, patches = refs[-8:]
    rows, cols = noisy.shape[1:]
    cells = rows * cols
    row = lax.axis_index("row")
    inner, outer = row > 0, row < rows_total - 1
    above = jnp.where(inner, far[0][...].astype(F32), 0.0)
    below = jnp.where(outer, far[-1][...].astype(F32), 0.0)
    lane = lax.broadcasted_iota(jnp.int32, (noisy.shape[0], cols), 1)
    depth = noisy.shape[0]
    for r in range(rows + 4):
        if r < 2:
            line = above[:, r]
        elif r < rows + 2:
            line = noisy[:, r - 2]
        else:
            line = below[:, r - rows - 2]
        turned = [
            jnp.where(lane == 0, 0.0, pltpu.roll(line, 1, 1)),
            line,
            jnp.where(lane == cols - 1, 0.0, pltpu.roll(line, cols - 1, 1)),
        ]
        for a in range(3):
            if 0 <= r - a < rows + 2:
                for b in range(3):
                    k = 3 * a + b
                    patches[k * depth : (k + 1) * depth, (r - a) * cols : (r - a + 1) * cols] = turned[b]
    first = product(in_weight[...], patches[...].astype(BF16), (0, 0))
    act = jax.nn.silu(first + shift[...])
    lane = lax.broadcasted_iota(jnp.int32, (act.shape[0], cols), 1)
    for r in range(rows + 2):
        band = act[:, r * cols : (r + 1) * cols]
        if r == 0:
            band = jnp.where(inner, band, 0.0)
        if r == rows + 1:
            band = jnp.where(outer, band, 0.0)
        spot = slice(r * cols, (r + 1) * cols)
        acts[1, :, spot] = band.astype(BF16)
        acts[0, :, spot] = jnp.where(lane == 0, 0.0, pltpu.roll(band, 1, 1)).astype(BF16)
        acts[2, :, spot] = jnp.where(lane == cols - 1, 0.0, pltpu.roll(band, cols - 1, 1)).astype(BF16)
    total = first[:, cols : cols + cells]
    for a in range(3):
        for b in range(3):
            total = total + product(res_weight[3 * a + b], acts[b, :, a * cols : a * cols + cells], (1, 0))
    low = total.astype(BF16)
    hid[...] = low
    query[...] = product(query_weight[...], low, (1, 0)).astype(BF16)


def attention_kernel(rows, query, hid, upstream, query_weight, out_weight, *refs):
    bands = refs[:rows]
    block_out, kept, grad_hid, query_grad, out_grad = refs[rows : rows + 5]
    sent = refs[rows + 5 : 2 * rows + 4]
    grad_att, attended, grad_query, held, pairs, grad_pairs = refs[2 * rows + 4 :]
    channels = hid.shape[0]
    here = spots_of(rows)
    height = SLOTS // rows
    for j in range(rows):
        held[here["row"] ^ j] = bands[j][...]
    for r in range(rows):
        pairs[r * height : (r + 1) * height, :] = held[r]
    scale = HEAD_DIM**-0.5
    grad_att[...] = product(out_weight[...], upstream[...], (0, 0)).astype(BF16)
    for h in range(channels // HEAD_DIM):
        spot = slice(h * HEAD_DIM, (h + 1) * HEAD_DIM)
        keys = pairs[:, h * HEAD_DIM : (h + 1) * HEAD_DIM]
        vals = pairs[:, channels + h * HEAD_DIM : channels + (h + 1) * HEAD_DIM]
        one = query[spot, :]
        score = product(keys, one, (1, 0)) * scale
        grown = jnp.exp(score - jnp.max(score, axis=0, keepdims=True))
        probs = grown / jnp.sum(grown, axis=0, keepdims=True)
        low = probs.astype(BF16)
        attended[spot, :] = product(vals, low, (0, 0)).astype(BF16)
        back = grad_att[spot, :]
        grad_prob = product(vals, back, (1, 0))
        inner = jnp.sum(probs * grad_prob, axis=0, keepdims=True)
        grad_score = (scale * probs * (grad_prob - inner)).astype(BF16)
        grad_query[spot, :] = product(keys, grad_score, (0, 0)).astype(BF16)
        grad_pairs[:, h * HEAD_DIM : (h + 1) * HEAD_DIM] = product(grad_score, one, (1, 1))
        grad_pairs[:, channels + h * HEAD_DIM : channels + (h + 1) * HEAD_DIM] = product(low, back, (1, 1))
    kept[...] = grad_pairs[pl.ds(pl.multiple_of(here["row"] * height, 8), height), :]
    for j in range(1, rows):
        spot = pl.ds(pl.multiple_of((here["row"] ^ j) * height, 8), height)
        sent[j - 1][...] = grad_pairs[spot, :].astype(BF16)
    block_out[...] = (
        hid[...].astype(F32) + product(out_weight[...], attended[...], (1, 0))
    ).astype(BF16)
    grad_hid[...] = (
        upstream[...].astype(F32) + product(query_weight[...], grad_query[...], (0, 0))
    ).astype(BF16)
    query_grad[...] = product(grad_query[...], hid[...], (1, 1))
    out_grad[...] = product(upstream[...], attended[...], (1, 1))


def filter_kernel(rows, cols, grad_hid, acts, query_grad, out_grad, kept, sent, whole, pair, wide):
    channels, cells = grad_hid.shape
    for t in range(0, 9, 2):
        taps = [t, t + 1] if t < 8 else [t]
        for k, tap in enumerate(taps):
            a, b = tap // 3, tap % 3
            pair[k * channels : (k + 1) * channels, :] = acts[b, :, a * cols : a * cols + cells]
        span = len(taps) * channels
        whole[:, t * channels : t * channels + span] = product(grad_hid[...], pair[:span, :], (1, 1))
    edge = 9 * channels
    base = edge // 128 * 128
    lead = edge - base
    wide[:, :channels] = query_grad[...]
    turned = pltpu.roll(wide[...], lead, 1) if lead else wide[...]
    lane = lax.broadcasted_iota(jnp.int32, (channels, 128), 1)
    whole[:, base : base + 128] = jnp.where(lane < lead, whole[:, base : base + 128], turned[:, :128])
    whole[:, base + 128 : edge + channels] = turned[:, 128 : lead + channels]
    whole[:, edge + channels : edge + 2 * channels] = out_grad[...]
    rest = whole.shape[1] - edge - 2 * channels
    if rest:
        whole[:, edge + 2 * channels :] = jnp.zeros((channels, rest), F32)
    half = channels // 2
    core = spots_of(rows)["core"]
    pieces, height = kept.shape[:2]
    for q in range(pieces):
        if height % 8 == 0:
            kept[q] = whole[pl.ds(pl.multiple_of(core * half + q * height, 8), height), :]
            away = whole[pl.ds(pl.multiple_of((1 - core) * half + q * height, 8), height), :]
        else:
            low = whole[q * height : (q + 1) * height, :]
            high = whole[half + q * height : half + (q + 1) * height, :]
            kept[q] = jnp.where(core == 0, low, high)
            away = jnp.where(core == 0, high, low)
        sent[q] = away.astype(BF16)


def square_kernel(rows, kept, came, own, *outs):
    here = spots_of(rows)["square"]
    own[...] = kept[here] + came[here].astype(F32)
    for j in range(1, 2 * rows):
        outs[j - 1][...] = (kept[here ^ j] + came[here ^ j].astype(F32)).astype(BF16)


def line_kernel(rows, count, near, *refs):
    here = spots_of(rows)["line"]
    total = refs[0][...]
    for one in refs[1:near]:
        total = total + one[...].astype(F32)
    own, outs, held = refs[near], refs[near + 1 : near + count], refs[near + count]
    slot = total.shape[1] // count
    held[...] = total
    own[...] = held[:, pl.ds(pl.multiple_of(here * slot, 128), slot)]
    for j in range(1, count):
        spot = pl.ds(pl.multiple_of((here ^ j) * slot, 128), slot)
        outs[j - 1][...] = held[:, spot].astype(BF16)


def unpack_kernel(rows, lines, *refs):
    count = 2 * rows
    here = spots_of(rows)
    parts = refs[: 2 * count]
    res, query, out, whole, *spare = refs[2 * count :]
    height = parts[0].shape[0]
    slot = parts[0].shape[1] // lines
    for c in range(2):
        for j in range(count):
            piece = parts[c * count + j][...].astype(F32)
            spot = (here["core"] ^ c) * count + (here["square"] ^ j)
            for z in range(lines):
                lanes = pl.ds(pl.multiple_of((here["line"] ^ z) * slot, 128), slot)
                one = piece[:, z * slot : (z + 1) * slot]
                if spare:
                    spare[0][spot, :, lanes] = one
                else:
                    whole[pl.ds(pl.multiple_of(spot * height, 8), height), lanes] = one
    if spare:
        for q in range(2 * count):
            whole[q * height : (q + 1) * height, :] = spare[0][q]
    channels = query.shape[0]
    for t in range(11):
        start = t * channels
        base = start // 128 * 128
        lead = start - base
        if lead:
            span = -(-(lead + channels) // 128) * 128
            piece = pltpu.roll(whole[:, base : base + span], span - lead, 1)[:, :channels]
        else:
            piece = whole[:, start : start + channels]
        piece = piece.astype(BF16)
        if t < 9:
            res[t] = piece
        elif t == 9:
            query[...] = piece
        else:
            out[...] = piece


def line_mask(j, rows):
    return j * 4 * rows


def square_mask(j, rows):
    return j // rows * 2 * rows + j % rows


def filter_step(grad_hid, acts, query_grad, out_grad, cols, rows, lines):
    channels, cells = grad_hid.shape
    slot = -(-11 * channels // (128 * lines)) * 128
    width = slot * lines
    half = channels // 2
    return call(
        functools.partial(filter_kernel, rows, cols),
        [((2 * rows, half // rows // 2, width), F32), ((2 * rows, half // rows // 2, width), BF16)],
        [grad_hid, acts, query_grad, out_grad],
        [
            pltpu.VMEM((channels, width), F32),
            pltpu.VMEM((2 * channels, cells), BF16),
            pltpu.VMEM((channels, -(-channels // 128) * 128), F32),
        ],
        flops=18 * channels * channels * cells,
    )


def square_step(kept, came, rows):
    squares, height, width = kept.shape
    return call(
        functools.partial(square_kernel, rows),
        [((height, width), F32)] + [((height, width), BF16)] * (squares - 1),
        [kept, came],
    )


def line_step(own, near, rows, lines):
    height, width = own.shape
    slot = width // lines
    return call(
        functools.partial(line_kernel, rows, lines, len(near) + 1),
        [((height, slot), F32)] + [((height, slot), BF16)] * (lines - 1),
        [own, *near],
        [pltpu.VMEM((height, width), F32)],
    )


def unpack_step(mine, other, channels, rows, lines):
    height = mine[0].shape[0]
    res, query, out = call(
        functools.partial(unpack_kernel, rows, lines),
        [((9, channels, channels), BF16), ((channels, channels), BF16), ((channels, channels), BF16)],
        [*mine, *other],
        [pltpu.VMEM((channels, mine[0].shape[1]), F32)]
        + [pltpu.VMEM((channels // height, height, mine[0].shape[1]), F32)] * (height % 8 > 0),
        leave=(0, 1, 2),
    )
    return res.reshape(3, 3, channels, channels), query, out


def gather_kernel(rows, lines, group_of, *refs):
    count = 4 * rows
    parts = refs[:count]
    image_rows, all_rows, held = refs[count:]
    image, row = lax.axis_index("img"), lax.axis_index("row")
    for k in range(count):
        for z in range(lines):
            held[k * lines + z] = parts[k][z]

    def spot(source, r):
        v = group_of[source] ^ image
        return (((v & 1) * 2 + ((v >> 1) & 1)) * rows + (row ^ r)) * lines + (v >> 2)

    for r in range(rows):
        image_rows[r] = held[spot(image, r)]
    for x in range(2):
        for z in range(lines):
            for c in range(2):
                p = (x * lines + z) * 2 + c
                for r in range(rows):
                    all_rows[p * rows + r] = held[spot(image ^ (z * 4 + x * 2 + c), r)]


def place_kernel(start, image, weight, blank, out, window, sem):
    span = window.shape[0]
    base = jnp.minimum((start[0] >> 4) << 4, out.shape[0] - span)
    token = lax.broadcasted_iota(jnp.int32, (span, SLOTS), 0)
    slot = lax.broadcasted_iota(jnp.int32, (span, SLOTS), 1)
    chosen = jnp.where(token == slot + (start[0] - base), 1.0, 0.0).astype(BF16)
    rows = product(image[...], weight[...], (1, 1)).astype(BF16)
    window[...] = product(chosen, rows, (1, 0)).astype(BF16)
    store = pltpu.make_async_copy(window, out.at[pl.ds(pl.multiple_of(base, 16), span), :], sem)
    store.start()
    store.wait()


def join_kernel(flip, part, *refs):
    out, sems = refs[-2:]
    width = part.shape[0]
    core = (lax.axis_index("img") & 1) ^ flip
    count = sems.shape[0]
    depth = width // count
    stores = []
    for k in range(count):
        target = out.at[pl.ds(pl.multiple_of(core * width + k * depth, 8), depth), :]
        stores.append(pltpu.make_async_copy(part.at[k * depth : (k + 1) * depth, :], target, sems.at[k]))
    for one in stores:
        one.start()
    for one in stores:
        one.wait()


def join_step(flip, part, base):
    width, pair_width = part.shape
    spare = pl.BlockSpec(memory_space=pl.ANY)
    return pl.pallas_call(
        functools.partial(join_kernel, flip),
        out_shape=jax.ShapeDtypeStruct((2 * width, pair_width), BF16),
        in_specs=[VMEM] + [spare] * len(base),
        out_specs=spare,
        scratch_shapes=[pltpu.SemaphoreType.DMA((4 if width % 64 == 0 else 1,))],
        input_output_aliases={1: 0} if base else {},
        compiler_params=pltpu.CompilerParams(vmem_limit_bytes=LIMIT),
    )(near_core(part), *base)


def blank_kernel(out, zeros, sems):
    zeros[...] = jnp.zeros(zeros.shape, zeros.dtype)
    depth = zeros.shape[0]
    count = out.shape[0] // depth
    stores = [
        pltpu.make_async_copy(zeros, out.at[k * depth : (k + 1) * depth, :], sems.at[k]) for k in range(count)
    ]
    for one in stores:
        one.start()
    for one in stores:
        one.wait()


def shards(
    llm_hidden,
    slot_start,
    image_group,
    timesteps,
    latents,
    noise,
    kv_weight,
    in_weight,
    res_weight,
    query_weight,
    out_weight,
    cotangent,
):
    rows = lax.axis_size("row")
    images = lax.axis_size("img")
    lines = images // 4
    channels = in_weight.shape[2]
    row_count, col_count = latents.shape[2:]
    cells = row_count * col_count
    tokens, features = llm_hidden.shape
    pair_width = kv_weight.shape[1]
    height = SLOTS // rows
    half = features // 2

    depth = latents.shape[1]
    noisy, *edges = call(
        functools.partial(noisy_kernel, rows),
        [((depth, row_count, col_count), F32)] + [((depth, 2, col_count), BF16)] * (1 if rows == 2 else 2),
        [timesteps, latents, noise],
        scalars=1,
    )
    if rows == 2:
        far = [lax.ppermute(edges[0], "row", [(0, 1), (1, 0)])]
    else:
        far = [
            lax.ppermute(edges[0], "row", [(i, i + 1) for i in range(rows - 1)]),
            lax.ppermute(edges[1], "row", [(i + 1, i) for i in range(rows - 1)]),
        ]

    span = min(SLOTS + 16, tokens)
    pieces = 4 if features % 512 == 0 else 1
    kept, *rest = pl.pallas_call(
        functools.partial(condition_kernel, rows),
        out_shape=[jax.ShapeDtypeStruct((height, pair_width), F32)] * rows
        + [jax.ShapeDtypeStruct((SLOTS, half), BF16)] * 2,
        in_specs=[SMEM, pl.BlockSpec(memory_space=pl.ANY), pl.BlockSpec(memory_space=pl.ANY)],
        out_specs=[VMEM] * (rows + 2),
        scratch_shapes=[
            pltpu.VMEM((span, features), BF16),
            pltpu.VMEM((features, pair_width), BF16),
            pltpu.VMEM((SLOTS, features), BF16),
            pltpu.VMEM((rows, height, pair_width), F32),
            pltpu.SemaphoreType.DMA,
            pltpu.SemaphoreType.DMA((pieces,)),
        ],
        cost_estimate=pl.CostEstimate(
            flops=2 * SLOTS * features * pair_width,
            bytes_accessed=2 * features * (pair_width + 3 * SLOTS),
            transcendentals=0,
        ),
        name="condition",
    )(slot_start, llm_hidden, kv_weight)
    sent, mine, away = rest[: rows - 1], rest[rows - 1], rest[rows]

    band = kept
    for j in range(1, rows):
        band = band + swap(sent[j - 1], j)
    band = band.astype(BF16)
    column = [band] + [swap(band, line_mask(j, rows)) for j in range(1, lines)]
    upstream = cotangent[0].reshape(channels, cells)
    shift = time_shift(timesteps[0], channels)[:, None]
    in_flat = in_weight.transpose(0, 1, 3, 2).reshape(-1, channels)
    column[0], upstream, shift, in_flat = lax.optimization_barrier((column[0], upstream, shift, in_flat))
    plane = call(
        functools.partial(select_kernel, rows), [((height, pair_width), BF16)] * 4, [image_group, *column], scalars=1
    )
    band = plane[0].astype(F32)
    for k in range(1, 4):
        band = band + swap(plane[k], k * rows).astype(F32)
    band = band.astype(BF16)
    bands = [band] + [swap(band, j) for j in range(1, rows)]

    other = swap(away, rows)
    block = jnp.concatenate([mine, other])
    near = [block] + [swap(block, line_mask(j, rows)) for j in range(1, lines)]

    acts, hid, query = call(
        functools.partial(front_kernel, rows),
        [
            ((3, channels, cells + 2 * col_count), BF16),
            ((channels, cells), BF16),
            ((channels, cells), BF16),
        ],
        [
            noisy,
            *far,
            shift,
            in_flat,
            res_weight.reshape(9, channels, channels),
            query_weight,
        ],
        [pltpu.VMEM((9 * depth, cells + 2 * col_count), F32)],
        flops=20 * channels * channels * cells,
    )
    block_out, kept, grad_hid, query_grad, out_grad, *sent = call(
        functools.partial(attention_kernel, rows),
        [
            ((channels, cells), BF16),
            ((height, pair_width), F32),
            ((channels, cells), BF16),
            ((channels, channels), F32),
            ((channels, channels), F32),
        ]
        + [((height, pair_width), BF16)] * (rows - 1),
        [query, hid, upstream, query_weight, out_weight, *bands],
        [pltpu.VMEM((channels, cells), BF16)] * 3
        + [
            pltpu.VMEM((rows, height, pair_width), BF16),
            pltpu.VMEM((SLOTS, pair_width), BF16),
            pltpu.VMEM((SLOTS, pair_width), F32),
        ],
        flops=10 * channels * channels * cells + 12 * channels * SLOTS * cells,
    )
    grad_band = kept
    for j in range(1, rows):
        grad_band = grad_band + swap(sent[j - 1], j).astype(F32)
    grad_band = grad_band.astype(BF16)
    kept, sent = filter_step(grad_hid, acts, query_grad, out_grad, col_count, rows, lines)
    own, *outs = square_step(kept, swap(sent, rows), rows)
    blank = pl.pallas_call(
        blank_kernel,
        out_shape=jax.ShapeDtypeStruct((tokens, features), BF16),
        out_specs=pl.BlockSpec(memory_space=pl.ANY),
        scratch_shapes=[
            pltpu.VMEM((tokens // 8, features), BF16),
            pltpu.SemaphoreType.DMA((8,)),
        ],
        name="blank",
    )()
    block_out = block_out.reshape(1, channels, row_count, col_count)
    own, block_out = lax.optimization_barrier((own, block_out))
    squares = 2 * rows
    came = [swap(outs[j - 1], square_mask(j, rows)) for j in range(1, squares)]
    own, *outs = line_step(own, came, rows, lines)
    came = [swap(outs[j - 1], line_mask(j, rows)) for j in range(1, lines)]
    weight_scale = (images * rows * cells) ** (-0.5)
    for one in came:
        own = own + one.astype(F32)
    final = (own * weight_scale).astype(BF16)
    far = [swap(final, line_mask(j, rows)) for j in range(1, lines)]

    column = jnp.stack([grad_band] + [swap(grad_band, line_mask(j, rows)) for j in range(1, lines)])
    parts = [column] + [swap(column, square_mask(j, rows)) for j in range(1, squares)]
    parts = parts + [swap(one, rows) for one in parts]
    image_rows, all_rows = call(
        functools.partial(gather_kernel, rows, lines),
        [((rows, height, pair_width), BF16), ((images * rows, height, pair_width), BF16)],
        [image_group, *parts],
        [pltpu.VMEM((4 * rows * lines, height, pair_width), BF16)],
        scalars=1,
    )
    all_rows = all_rows.reshape(images * SLOTS, pair_width)
    grad_hidden = pl.pallas_call(
        place_kernel,
        out_shape=jax.ShapeDtypeStruct((tokens, features), BF16),
        in_specs=[SMEM, VMEM, VMEM, pl.BlockSpec(memory_space=pl.ANY)],
        out_specs=pl.BlockSpec(memory_space=pl.ANY),
        scratch_shapes=[pltpu.VMEM((span, features), BF16), pltpu.SemaphoreType.DMA],
        input_output_aliases={3: 0},
        compiler_params=pltpu.CompilerParams(vmem_limit_bytes=LIMIT),
        name="place",
    )(slot_start, near_core(image_rows.reshape(SLOTS, pair_width)), near_core(kv_weight), blank)
    wide = jnp.concatenate([final, *far], axis=1)
    parts = [wide] + [swap(wide, square_mask(j, rows)) for j in range(1, squares)]

    near_half = images * SLOTS // 2
    across = []
    for j in range(lines):
        if j % 2 and j > 1:
            across.append(swap(across[j - 1], line_mask(1, rows)))
        else:
            across.append(swap(near[j], 2 * rows))
    total = product(jnp.concatenate(near), all_rows[:near_half], (0, 0))
    total = total + product(jnp.concatenate(across), all_rows[near_half:], (0, 0))
    weight_half = (total * (images * SLOTS) ** (-0.5)).astype(BF16)
    came = swap(weight_half, rows)
    grad_kv_weight = join_step(0, weight_half, [])
    grad_kv_weight = join_step(1, came, [grad_kv_weight])
    others = [swap(one, rows) for one in parts]
    grad_res_weight, grad_query_weight, grad_out_weight = unpack_step(
        parts, others, channels, rows, lines
    )
    return (
        block_out,
        grad_hidden,
        grad_kv_weight,
        grad_res_weight,
        grad_query_weight,
        grad_out_weight,
    )


def solution(mesh):
    return jax.shard_map(
        shards,
        mesh=mesh,
        in_specs=(
            P("img", "row"),
            P("img"),
            P(),
            P("img"),
            P("img", None, "row", None),
            P("img", None, "row", None),
            P("row", None),
            P(),
            P(),
            P(),
            P(),
            P("img", None, "row", None),
        ),
        out_specs=(P("img", None, "row", None), P("img", "row"), P("row", None), P(), P(), P()),
        check_vma=False,
    )
```

```python
import functools
import math

import jax
import jax.numpy as jnp
from jax import lax
from jax.experimental import pallas as pl
from jax.experimental.pallas import tpu as pltpu
from jax.sharding import PartitionSpec as P


HEAD_DIM = 64
SLOTS = 64
GRID = ("img", "row")
F32 = jnp.float32
BF16 = jnp.bfloat16
VMEM = pl.BlockSpec(memory_space=pltpu.VMEM)
SMEM = pl.BlockSpec(memory_space=pltpu.SMEM)


LIMIT = 20 * 2**20


def near_core(array):
    return pltpu.with_memory_space_constraint(array, pltpu.VMEM)


def call(kernel, outs, ins, scratch=(), flops=0, scalars=0, leave=(), remote=0):
    outs = [jax.ShapeDtypeStruct(shape, kind) for shape, kind in outs]
    moved = sum(math.prod(x.shape) * x.dtype.itemsize for x in [*outs, *ins])
    near = len(ins) - scalars - remote
    ins = [near_core(x) if scalars <= k < scalars + near else x for k, x in enumerate(ins)]
    if remote:
        ins[-1] = pltpu.with_memory_space_constraint(ins[-1], pltpu.HBM)
    return pl.pallas_call(
        kernel,
        out_shape=[x if k in leave else pltpu.VMEM(x.shape, x.dtype) for k, x in enumerate(outs)],
        in_specs=[SMEM] * scalars + [VMEM] * near + [pl.BlockSpec(memory_space=pl.ANY)] * remote,
        out_specs=[VMEM] * len(outs),
        scratch_shapes=list(scratch),
        cost_estimate=pl.CostEstimate(flops=flops, bytes_accessed=moved, transcendentals=0),
        compiler_params=pltpu.CompilerParams(vmem_limit_bytes=LIMIT),
    )(*ins)


def product(left, right, sides):
    return lax.dot_general(left, right, ((sides[:1], sides[1:]), ((), ())), preferred_element_type=F32)


def time_shift(timestep, channel_total):
    half_count = channel_total // 2
    frequency = jnp.exp(-math.log(10000.0) * jnp.arange(half_count, dtype=jnp.float32) / half_count)
    angles = timestep.astype(jnp.float32) * frequency
    return jnp.concatenate([jnp.cos(angles), jnp.sin(angles)])


def swap(block, mask):
    total = lax.axis_size("img") * lax.axis_size("row")
    return lax.ppermute(block, GRID, [(i, i ^ mask) for i in range(total)])


def spots_of(rows):
    image, row = lax.axis_index("img"), lax.axis_index("row")
    return {
        "image": image,
        "core": image & 1,
        "row": row,
        "square": ((image >> 1) & 1) * rows + row,
        "line": image >> 2,
        "plane": image & 3,
    }


def noisy_kernel(rows, timestep, latents, noise, noisy, *edges):
    step = timestep[0]
    index = lax.broadcasted_iota(jnp.int32, (8, 128), 0) * 128 + lax.broadcasted_iota(
        jnp.int32, (8, 128), 1
    )
    low, high = 0.00085**0.5, 0.012**0.5
    beta = (low + index.astype(F32) * ((high - low) / 999.0)) ** 2
    logs = jnp.where(index <= step, jnp.log(1.0 - jnp.where(index < 1000, beta, 0.0)), 0.0)
    total = jnp.sum(jnp.sum(logs, axis=1, keepdims=True), axis=0, keepdims=True)
    level = jnp.exp(total)
    keep, mix = jnp.sqrt(level), jnp.sqrt(1.0 - level)
    height = latents.shape[2]
    for c in range(latents.shape[1]):
        value = (keep * latents[0, c] + mix * noise[0, c]).astype(BF16).astype(F32)
        noisy[c] = value
        head, tail = value[:2].astype(BF16), value[height - 2 :].astype(BF16)
        if rows == 2:
            edges[0][c] = jnp.where(spots_of(rows)["row"] == 0, tail, head)
        else:
            edges[0][c] = tail
            edges[1][c] = head


def condition_kernel(rows, start, hidden, weight, kept, *refs):
    sent, mine, away = refs[: rows - 1], refs[rows - 1], refs[rows]
    window, weights, cond, held, row_sem, sems = refs[rows + 1 :]
    here = spots_of(rows)
    pieces = sems.shape[0]
    depth = weight.shape[0] // pieces
    span = window.shape[0]
    base = jnp.minimum((start[0] >> 4) << 4, hidden.shape[0] - span)
    load = pltpu.make_async_copy(hidden.at[pl.ds(pl.multiple_of(base, 16), span), :], window, row_sem)
    load.start()
    loads = [
        pltpu.make_async_copy(
            weight.at[k * depth : (k + 1) * depth, :], weights.at[k * depth : (k + 1) * depth, :], sems.at[k]
        )
        for k in range(pieces)
    ]
    for one in loads:
        one.start()
    load.wait()
    slot = lax.broadcasted_iota(jnp.int32, (SLOTS, span), 0)
    token = lax.broadcasted_iota(jnp.int32, (SLOTS, span), 1)
    chosen = jnp.where(token == slot + (start[0] - base), 1.0, 0.0).astype(BF16)
    cond[...] = product(chosen, window[...], (1, 0)).astype(BF16)
    half = cond.shape[1] // 2
    left, right = cond[:, :half], cond[:, half:]
    mine[...] = jnp.where(here["core"] == 0, left, right)
    away[...] = jnp.where(here["core"] == 0, right, left)
    total = None
    for k in range(pieces):
        loads[k].wait()
        one = product(cond[:, k * depth : (k + 1) * depth], weights[k * depth : (k + 1) * depth, :], (1, 0))
        total = one if total is None else total + one
    height = SLOTS // rows
    for r in range(rows):
        held[r] = total[r * height : (r + 1) * height]
    kept[...] = held[here["row"]]
    for j in range(1, rows):
        sent[j - 1][...] = held[here["row"] ^ j]


def select_kernel(rows, group_of, *refs):
    lines = len(refs) - 4
    here = spots_of(rows)
    for k in range(4):
        target = here["line"] * 4 + (here["plane"] ^ k)
        chosen = jnp.zeros(refs[0].shape, F32)
        for j in range(lines):
            goes = group_of[(here["line"] ^ j) * 4 + here["plane"]] == target
            chosen = chosen + jnp.where(goes, refs[j][...].astype(F32), 0.0)
        refs[lines + k][...] = chosen.astype(BF16)


def front_kernel(rows_total, noisy, *refs):
    far = refs[:-12]
    shift, in_weight, query_weight, source, acts, hid, query = refs[-12:-5]
    patches, res_weight, ends, tails, sem = refs[-5:]
    load = pltpu.make_async_copy(source, res_weight, sem)
    load.start()
    rows, cols = noisy.shape[1:]
    cells = rows * cols
    row = lax.axis_index("row")
    inner, outer = row > 0, row < rows_total - 1
    above = jnp.where(inner, far[0][...].astype(F32), 0.0)
    below = jnp.where(outer, far[-1][...].astype(F32), 0.0)
    lane = lax.broadcasted_iota(jnp.int32, (noisy.shape[0], cols), 1)
    depth = noisy.shape[0]
    for r in range(rows + 4):
        if r < 2:
            line = above[:, r]
        elif r < rows + 2:
            line = noisy[:, r - 2]
        else:
            line = below[:, r - rows - 2]
        turned = [
            jnp.where(lane == 0, 0.0, pltpu.roll(line, 1, 1)),
            line,
            jnp.where(lane == cols - 1, 0.0, pltpu.roll(line, cols - 1, 1)),
        ]
        for a in range(3):
            if 0 <= r - a < rows + 2:
                for b in range(3):
                    k = 3 * a + b
                    patches[k * depth : (k + 1) * depth, (r - a) * cols : (r - a + 1) * cols] = turned[b]
    first = product(in_weight[...], patches[...].astype(BF16), (0, 0))
    act = jax.nn.silu(first + shift[...])
    lane = lax.broadcasted_iota(jnp.int32, (act.shape[0], cols), 1)
    for r in range(rows + 2):
        band = act[:, r * cols : (r + 1) * cols]
        if r == 0:
            band = jnp.where(inner, band, 0.0)
        if r == rows + 1:
            band = jnp.where(outer, band, 0.0)
        spot = slice(r * cols, (r + 1) * cols)
        acts[1, :, spot] = band.astype(BF16)
        acts[0, :, spot] = jnp.where(lane == 0, 0.0, pltpu.roll(band, 1, 1)).astype(BF16)
        acts[2, :, spot] = jnp.where(lane == cols - 1, 0.0, pltpu.roll(band, cols - 1, 1)).astype(BF16)
    total = first[:, cols : cols + cells]
    load.wait()
    channels = act.shape[0]
    main = channels // 256 * 256
    left = channels - main
    for k in range(9):
        a, b = k // 3, k % 3
        total = total + product(
            res_weight[k, :, :main], acts[b, :main, a * cols : a * cols + cells], (1, 0)
        )
        ends[:, k * left : (k + 1) * left] = res_weight[k, :, main:]
        tails[k * left : (k + 1) * left, :] = acts[b, main:, a * cols : a * cols + cells]
    total = total + product(ends[...], tails[...], (1, 0))
    low = total.astype(BF16)
    hid[...] = low
    query[...] = product(query_weight[...], low, (1, 0)).astype(BF16)


def attention_kernel(rows, query, hid, upstream, query_weight, out_weight, *refs):
    bands = refs[:rows]
    block_out, kept, grad_hid, query_grad, out_grad = refs[rows : rows + 5]
    sent = refs[rows + 5 : 2 * rows + 4]
    grad_att, attended, grad_query, held, pairs, grad_pairs, lows, grads = refs[2 * rows + 4 :]
    cells = hid.shape[1]
    chunk = 256 if cells % 256 == 0 else cells
    channels = hid.shape[0]
    here = spots_of(rows)
    height = SLOTS // rows
    for j in range(rows):
        held[here["row"] ^ j] = bands[j][...]
    for r in range(rows):
        pairs[r * height : (r + 1) * height, :] = held[r]
    scale = HEAD_DIM**-0.5
    grad_att[...] = product(out_weight[...], upstream[...], (0, 0)).astype(BF16)
    for h in range(channels // HEAD_DIM):
        spot = slice(h * HEAD_DIM, (h + 1) * HEAD_DIM)
        keys = pairs[:, h * HEAD_DIM : (h + 1) * HEAD_DIM]
        vals = pairs[:, channels + h * HEAD_DIM : channels + (h + 1) * HEAD_DIM]
        for k in range(0, cells, chunk):
            lanes = slice(k, k + chunk)
            score = product(keys, query[spot, lanes], (1, 0)) * scale
            grown = jnp.exp(score - jnp.max(score, axis=0, keepdims=True))
            probs = grown / jnp.sum(grown, axis=0, keepdims=True)
            low = probs.astype(BF16)
            lows[:, lanes] = low
            attended[spot, lanes] = product(vals, low, (0, 0)).astype(BF16)
            grad_prob = product(vals, grad_att[spot, lanes], (1, 0))
            inner = jnp.sum(probs * grad_prob, axis=0, keepdims=True)
            grad_score = (scale * probs * (grad_prob - inner)).astype(BF16)
            grads[:, lanes] = grad_score
            grad_query[spot, lanes] = product(keys, grad_score, (0, 0)).astype(BF16)
        grad_pairs[:, h * HEAD_DIM : (h + 1) * HEAD_DIM] = product(grads[...], query[spot, :], (1, 1))
        grad_pairs[:, channels + h * HEAD_DIM : channels + (h + 1) * HEAD_DIM] = product(
            lows[...], grad_att[spot, :], (1, 1)
        )
    kept[...] = grad_pairs[pl.ds(pl.multiple_of(here["row"] * height, 8), height), :]
    for j in range(1, rows):
        spot = pl.ds(pl.multiple_of((here["row"] ^ j) * height, 8), height)
        sent[j - 1][...] = grad_pairs[spot, :].astype(BF16)
    block_out[...] = (
        hid[...].astype(F32) + product(out_weight[...], attended[...], (1, 0))
    ).astype(BF16)
    grad_hid[...] = (
        upstream[...].astype(F32) + product(query_weight[...], grad_query[...], (0, 0))
    ).astype(BF16)
    query_grad[...] = product(grad_query[...], hid[...], (1, 1))
    out_grad[...] = product(upstream[...], attended[...], (1, 1))


def filter_kernel(rows, cols, grad_hid, acts, query_grad, out_grad, kept, sent, whole, pair, wide):
    channels, cells = grad_hid.shape
    for t in range(0, 9, 2):
        taps = [t, t + 1] if t < 8 else [t]
        for k, tap in enumerate(taps):
            a, b = tap // 3, tap % 3
            pair[k * channels : (k + 1) * channels, :] = acts[b, :, a * cols : a * cols + cells]
        span = len(taps) * channels
        whole[:, t * channels : t * channels + span] = product(grad_hid[...], pair[:span, :], (1, 1))
    edge = 9 * channels
    base = edge // 128 * 128
    lead = edge - base
    wide[:, :channels] = query_grad[...]
    turned = pltpu.roll(wide[...], lead, 1) if lead else wide[...]
    lane = lax.broadcasted_iota(jnp.int32, (channels, 128), 1)
    whole[:, base : base + 128] = jnp.where(lane < lead, whole[:, base : base + 128], turned[:, :128])
    whole[:, base + 128 : edge + channels] = turned[:, 128 : lead + channels]
    whole[:, edge + channels : edge + 2 * channels] = out_grad[...]
    rest = whole.shape[1] - edge - 2 * channels
    if rest:
        whole[:, edge + 2 * channels :] = jnp.zeros((channels, rest), F32)
    half = channels // 2
    core = spots_of(rows)["core"]
    pieces, height = kept.shape[:2]
    for q in range(pieces):
        if height % 8 == 0:
            kept[q] = whole[pl.ds(pl.multiple_of(core * half + q * height, 8), height), :]
            away = whole[pl.ds(pl.multiple_of((1 - core) * half + q * height, 8), height), :]
        else:
            low = whole[q * height : (q + 1) * height, :]
            high = whole[half + q * height : half + (q + 1) * height, :]
            kept[q] = jnp.where(core == 0, low, high)
            away = jnp.where(core == 0, high, low)
        sent[q] = away.astype(BF16)


def square_kernel(rows, kept, came, own, *outs):
    here = spots_of(rows)["square"]
    own[...] = kept[here] + came[here].astype(F32)
    for j in range(1, 2 * rows):
        outs[j - 1][...] = (kept[here ^ j] + came[here ^ j].astype(F32)).astype(BF16)


def line_kernel(rows, count, near, *refs):
    here = spots_of(rows)["line"]
    total = refs[0][...]
    for one in refs[1:near]:
        total = total + one[...].astype(F32)
    own, outs, held = refs[near], refs[near + 1 : near + count], refs[near + count]
    slot = total.shape[1] // count
    held[...] = total
    own[...] = held[:, pl.ds(pl.multiple_of(here * slot, 128), slot)]
    for j in range(1, count):
        spot = pl.ds(pl.multiple_of((here ^ j) * slot, 128), slot)
        outs[j - 1][...] = held[:, spot].astype(BF16)


def unpack_kernel(rows, lines, *refs):
    count = 2 * rows
    here = spots_of(rows)
    parts = refs[: 2 * count]
    res, query, out, whole, *spare = refs[2 * count :]
    height = parts[0].shape[0]
    slot = parts[0].shape[1] // lines
    for c in range(2):
        for j in range(count):
            piece = parts[c * count + j][...].astype(F32)
            spot = (here["core"] ^ c) * count + (here["square"] ^ j)
            for z in range(lines):
                lanes = pl.ds(pl.multiple_of((here["line"] ^ z) * slot, 128), slot)
                one = piece[:, z * slot : (z + 1) * slot]
                if spare:
                    spare[0][spot, :, lanes] = one
                else:
                    whole[pl.ds(pl.multiple_of(spot * height, 8), height), lanes] = one
    if spare:
        for q in range(2 * count):
            whole[q * height : (q + 1) * height, :] = spare[0][q]
    channels = query.shape[0]
    for t in range(11):
        start = t * channels
        base = start // 128 * 128
        lead = start - base
        if lead:
            span = -(-(lead + channels) // 128) * 128
            piece = pltpu.roll(whole[:, base : base + span], span - lead, 1)[:, :channels]
        else:
            piece = whole[:, start : start + channels]
        piece = piece.astype(BF16)
        if t < 9:
            res[t] = piece
        elif t == 9:
            query[...] = piece
        else:
            out[...] = piece


def line_mask(j, rows):
    return j * 4 * rows


def square_mask(j, rows):
    return j // rows * 2 * rows + j % rows


def filter_step(grad_hid, acts, query_grad, out_grad, cols, rows, lines):
    channels, cells = grad_hid.shape
    slot = -(-11 * channels // (128 * lines)) * 128
    width = slot * lines
    half = channels // 2
    return call(
        functools.partial(filter_kernel, rows, cols),
        [((2 * rows, half // rows // 2, width), F32), ((2 * rows, half // rows // 2, width), BF16)],
        [grad_hid, acts, query_grad, out_grad],
        [
            pltpu.VMEM((channels, width), F32),
            pltpu.VMEM((2 * channels, cells), BF16),
            pltpu.VMEM((channels, -(-channels // 128) * 128), F32),
        ],
        flops=18 * channels * channels * cells,
    )


def square_step(kept, came, rows):
    squares, height, width = kept.shape
    return call(
        functools.partial(square_kernel, rows),
        [((height, width), F32)] + [((height, width), BF16)] * (squares - 1),
        [kept, came],
    )


def line_step(own, near, rows, lines):
    height, width = own.shape
    slot = width // lines
    return call(
        functools.partial(line_kernel, rows, lines, len(near) + 1),
        [((height, slot), F32)] + [((height, slot), BF16)] * (lines - 1),
        [own, *near],
        [pltpu.VMEM((height, width), F32)],
    )


def unpack_step(mine, other, channels, rows, lines):
    height = mine[0].shape[0]
    res, query, out = call(
        functools.partial(unpack_kernel, rows, lines),
        [((9, channels, channels), BF16), ((channels, channels), BF16), ((channels, channels), BF16)],
        [*mine, *other],
        [pltpu.VMEM((channels, mine[0].shape[1]), F32)]
        + [pltpu.VMEM((channels // height, height, mine[0].shape[1]), F32)] * (height % 8 > 0),
        leave=(0, 1, 2),
    )
    return res.reshape(3, 3, channels, channels), query, out


def gather_kernel(rows, lines, group_of, *refs):
    count = 4 * rows
    parts = refs[:count]
    image_rows, all_rows, held = refs[count:]
    image, row = lax.axis_index("img"), lax.axis_index("row")
    for k in range(count):
        for z in range(lines):
            held[k * lines + z] = parts[k][z]

    def spot(source, r):
        v = group_of[source] ^ image
        return (((v & 1) * 2 + ((v >> 1) & 1)) * rows + (row ^ r)) * lines + (v >> 2)

    for r in range(rows):
        image_rows[r] = held[spot(image, r)]
    for x in range(2):
        for z in range(lines):
            for c in range(2):
                p = (x * lines + z) * 2 + c
                for r in range(rows):
                    all_rows[p * rows + r] = held[spot(image ^ (z * 4 + x * 2 + c), r)]


def place_kernel(start, image, weight, blank, out, window, sem):
    span = window.shape[0]
    base = jnp.minimum((start[0] >> 4) << 4, out.shape[0] - span)
    token = lax.broadcasted_iota(jnp.int32, (span, SLOTS), 0)
    slot = lax.broadcasted_iota(jnp.int32, (span, SLOTS), 1)
    chosen = jnp.where(token == slot + (start[0] - base), 1.0, 0.0).astype(BF16)
    rows = product(image[...], weight[...], (1, 1)).astype(BF16)
    window[...] = product(chosen, rows, (1, 0)).astype(BF16)
    store = pltpu.make_async_copy(window, out.at[pl.ds(pl.multiple_of(base, 16), span), :], sem)
    store.start()
    store.wait()


def join_kernel(flip, part, *refs):
    out, sems = refs[-2:]
    width = part.shape[0]
    core = (lax.axis_index("img") & 1) ^ flip
    count = sems.shape[0]
    depth = width // count
    stores = []
    for k in range(count):
        target = out.at[pl.ds(pl.multiple_of(core * width + k * depth, 8), depth), :]
        stores.append(pltpu.make_async_copy(part.at[k * depth : (k + 1) * depth, :], target, sems.at[k]))
    for one in stores:
        one.start()
    for one in stores:
        one.wait()


def join_step(flip, part, base):
    width, pair_width = part.shape
    spare = pl.BlockSpec(memory_space=pl.ANY)
    return pl.pallas_call(
        functools.partial(join_kernel, flip),
        out_shape=jax.ShapeDtypeStruct((2 * width, pair_width), BF16),
        in_specs=[VMEM] + [spare] * len(base),
        out_specs=spare,
        scratch_shapes=[pltpu.SemaphoreType.DMA((4 if width % 64 == 0 else 1,))],
        input_output_aliases={1: 0} if base else {},
        compiler_params=pltpu.CompilerParams(vmem_limit_bytes=LIMIT),
    )(near_core(part), *base)


def blank_kernel(out, zeros, sems):
    zeros[...] = jnp.zeros(zeros.shape, zeros.dtype)
    depth = zeros.shape[0]
    count = out.shape[0] // depth
    stores = [
        pltpu.make_async_copy(zeros, out.at[k * depth : (k + 1) * depth, :], sems.at[k]) for k in range(count)
    ]
    for one in stores:
        one.start()
    for one in stores:
        one.wait()


def shards(
    llm_hidden,
    slot_start,
    image_group,
    timesteps,
    latents,
    noise,
    kv_weight,
    in_weight,
    res_weight,
    query_weight,
    out_weight,
    cotangent,
):
    rows = lax.axis_size("row")
    images = lax.axis_size("img")
    lines = images // 4
    channels = in_weight.shape[2]
    row_count, col_count = latents.shape[2:]
    cells = row_count * col_count
    tokens, features = llm_hidden.shape
    pair_width = kv_weight.shape[1]
    height = SLOTS // rows
    half = features // 2

    depth = latents.shape[1]
    noisy, *edges = call(
        functools.partial(noisy_kernel, rows),
        [((depth, row_count, col_count), F32)] + [((depth, 2, col_count), BF16)] * (1 if rows == 2 else 2),
        [timesteps, latents, noise],
        scalars=1,
    )
    if rows == 2:
        far = [lax.ppermute(edges[0], "row", [(0, 1), (1, 0)])]
    else:
        far = [
            lax.ppermute(edges[0], "row", [(i, i + 1) for i in range(rows - 1)]),
            lax.ppermute(edges[1], "row", [(i + 1, i) for i in range(rows - 1)]),
        ]

    span = min(SLOTS + 16, tokens)
    pieces = 4 if features % 512 == 0 else 1
    kept, *rest = pl.pallas_call(
        functools.partial(condition_kernel, rows),
        out_shape=[jax.ShapeDtypeStruct((height, pair_width), F32)] * rows
        + [jax.ShapeDtypeStruct((SLOTS, half), BF16)] * 2,
        in_specs=[SMEM, pl.BlockSpec(memory_space=pl.ANY), pl.BlockSpec(memory_space=pl.ANY)],
        out_specs=[VMEM] * (rows + 2),
        scratch_shapes=[
            pltpu.VMEM((span, features), BF16),
            pltpu.VMEM((features, pair_width), BF16),
            pltpu.VMEM((SLOTS, features), BF16),
            pltpu.VMEM((rows, height, pair_width), F32),
            pltpu.SemaphoreType.DMA,
            pltpu.SemaphoreType.DMA((pieces,)),
        ],
        cost_estimate=pl.CostEstimate(
            flops=2 * SLOTS * features * pair_width,
            bytes_accessed=2 * features * (pair_width + 3 * SLOTS),
            transcendentals=0,
        ),
        name="condition",
    )(slot_start, llm_hidden, kv_weight)
    sent, mine, away = rest[: rows - 1], rest[rows - 1], rest[rows]

    band = kept
    for j in range(1, rows):
        band = band + swap(sent[j - 1], j)
    band = band.astype(BF16)
    column = [band] + [swap(band, line_mask(j, rows)) for j in range(1, lines)]
    upstream = cotangent[0].reshape(channels, cells)
    shift = time_shift(timesteps[0], channels)[:, None]
    in_flat = in_weight.transpose(0, 1, 3, 2).reshape(-1, channels)
    column[0], upstream, shift, in_flat = lax.optimization_barrier((column[0], upstream, shift, in_flat))
    plane = call(
        functools.partial(select_kernel, rows), [((height, pair_width), BF16)] * 4, [image_group, *column], scalars=1
    )
    band = plane[0].astype(F32)
    for k in range(1, 4):
        band = band + swap(plane[k], k * rows).astype(F32)
    band = band.astype(BF16)
    bands = [band] + [swap(band, j) for j in range(1, rows)]

    other = swap(away, rows)
    block = jnp.concatenate([mine, other])
    near = [block] + [swap(block, line_mask(j, rows)) for j in range(1, lines)]

    acts, hid, query = call(
        functools.partial(front_kernel, rows),
        [
            ((3, channels, cells + 2 * col_count), BF16),
            ((channels, cells), BF16),
            ((channels, cells), BF16),
        ],
        [
            noisy,
            *far,
            shift,
            in_flat,
            query_weight,
            res_weight.reshape(9, channels, channels),
        ],
        [
            pltpu.VMEM((9 * depth, cells + 2 * col_count), F32),
            pltpu.VMEM((9, channels, channels), BF16),
            pltpu.VMEM((channels, 9 * (channels % 256)), BF16),
            pltpu.VMEM((9 * (channels % 256), cells), BF16),
            pltpu.SemaphoreType.DMA,
        ],
        remote=1,
        flops=20 * channels * channels * cells,
    )
    block_out, kept, grad_hid, query_grad, out_grad, *sent = call(
        functools.partial(attention_kernel, rows),
        [
            ((channels, cells), BF16),
            ((height, pair_width), F32),
            ((channels, cells), BF16),
            ((channels, channels), F32),
            ((channels, channels), F32),
        ]
        + [((height, pair_width), BF16)] * (rows - 1),
        [query, hid, upstream, query_weight, out_weight, *bands],
        [pltpu.VMEM((channels, cells), BF16)] * 3
        + [
            pltpu.VMEM((rows, height, pair_width), BF16),
            pltpu.VMEM((SLOTS, pair_width), BF16),
            pltpu.VMEM((SLOTS, pair_width), F32),
            pltpu.VMEM((SLOTS, cells), BF16),
            pltpu.VMEM((SLOTS, cells), BF16),
        ],
        flops=10 * channels * channels * cells + 12 * channels * SLOTS * cells,
    )
    grad_band = kept
    for j in range(1, rows):
        grad_band = grad_band + swap(sent[j - 1], j).astype(F32)
    grad_band = grad_band.astype(BF16)
    kept, sent = filter_step(grad_hid, acts, query_grad, out_grad, col_count, rows, lines)
    own, *outs = square_step(kept, swap(sent, rows), rows)
    blank = pl.pallas_call(
        blank_kernel,
        out_shape=jax.ShapeDtypeStruct((tokens, features), BF16),
        out_specs=pl.BlockSpec(memory_space=pl.ANY),
        scratch_shapes=[
            pltpu.VMEM((tokens // 8, features), BF16),
            pltpu.SemaphoreType.DMA((8,)),
        ],
        name="blank",
    )()
    block_out = block_out.reshape(1, channels, row_count, col_count)
    own, block_out = lax.optimization_barrier((own, block_out))
    squares = 2 * rows
    came = [swap(outs[j - 1], square_mask(j, rows)) for j in range(1, squares)]
    own, *outs = line_step(own, came, rows, lines)
    came = [swap(outs[j - 1], line_mask(j, rows)) for j in range(1, lines)]
    weight_scale = (images * rows * cells) ** (-0.5)
    for one in came:
        own = own + one.astype(F32)
    final = (own * weight_scale).astype(BF16)
    far = [swap(final, line_mask(j, rows)) for j in range(1, lines)]

    column = jnp.stack([grad_band] + [swap(grad_band, line_mask(j, rows)) for j in range(1, lines)])
    parts = [column] + [swap(column, square_mask(j, rows)) for j in range(1, squares)]
    parts = parts + [swap(one, rows) for one in parts]
    image_rows, all_rows = call(
        functools.partial(gather_kernel, rows, lines),
        [((rows, height, pair_width), BF16), ((images * rows, height, pair_width), BF16)],
        [image_group, *parts],
        [pltpu.VMEM((4 * rows * lines, height, pair_width), BF16)],
        scalars=1,
    )
    all_rows = all_rows.reshape(images * SLOTS, pair_width)
    grad_hidden = pl.pallas_call(
        place_kernel,
        out_shape=jax.ShapeDtypeStruct((tokens, features), BF16),
        in_specs=[SMEM, VMEM, VMEM, pl.BlockSpec(memory_space=pl.ANY)],
        out_specs=pl.BlockSpec(memory_space=pl.ANY),
        scratch_shapes=[pltpu.VMEM((span, features), BF16), pltpu.SemaphoreType.DMA],
        input_output_aliases={3: 0},
        compiler_params=pltpu.CompilerParams(vmem_limit_bytes=LIMIT),
        name="place",
    )(slot_start, near_core(image_rows.reshape(SLOTS, pair_width)), near_core(kv_weight), blank)
    wide = jnp.concatenate([final, *far], axis=1)
    parts = [wide] + [swap(wide, square_mask(j, rows)) for j in range(1, squares)]

    near_half = images * SLOTS // 2
    across = []
    for j in range(lines):
        if j % 2 and j > 1:
            across.append(swap(across[j - 1], line_mask(1, rows)))
        else:
            across.append(swap(near[j], 2 * rows))
    total = product(jnp.concatenate(near), all_rows[:near_half], (0, 0))
    total = total + product(jnp.concatenate(across), all_rows[near_half:], (0, 0))
    weight_half = (total * (images * SLOTS) ** (-0.5)).astype(BF16)
    came = swap(weight_half, rows)
    grad_kv_weight = join_step(0, weight_half, [])
    grad_kv_weight = join_step(1, came, [grad_kv_weight])
    others = [swap(one, rows) for one in parts]
    grad_res_weight, grad_query_weight, grad_out_weight = unpack_step(
        parts, others, channels, rows, lines
    )
    return (
        block_out,
        grad_hidden,
        grad_kv_weight,
        grad_res_weight,
        grad_query_weight,
        grad_out_weight,
    )


def solution(mesh):
    return jax.shard_map(
        shards,
        mesh=mesh,
        in_specs=(
            P("img", "row"),
            P("img"),
            P(),
            P("img"),
            P("img", None, "row", None),
            P("img", None, "row", None),
            P("row", None),
            P(),
            P(),
            P(),
            P(),
            P("img", None, "row", None),
        ),
        out_specs=(P("img", None, "row", None), P("img", "row"), P("row", None), P(), P(), P()),
        check_vma=False,
    )
```

```python
import functools
import math

import jax
import jax.numpy as jnp
from jax import lax
from jax.experimental import pallas as pl
from jax.experimental.pallas import tpu as pltpu
from jax.sharding import PartitionSpec as P


HEAD_DIM = 64
SLOTS = 64
GRID = ("img", "row")
F32 = jnp.float32
BF16 = jnp.bfloat16
VMEM = pl.BlockSpec(memory_space=pltpu.VMEM)
SMEM = pl.BlockSpec(memory_space=pltpu.SMEM)


LIMIT = 20 * 2**20


def near_core(array):
    return pltpu.with_memory_space_constraint(array, pltpu.VMEM)


def call(kernel, outs, ins, scratch=(), flops=0, scalars=0, leave=(), remote=0):
    outs = [jax.ShapeDtypeStruct(shape, kind) for shape, kind in outs]
    moved = sum(math.prod(x.shape) * x.dtype.itemsize for x in [*outs, *ins])
    near = len(ins) - scalars - remote
    ins = [near_core(x) if scalars <= k < scalars + near else x for k, x in enumerate(ins)]
    if remote:
        ins[-1] = pltpu.with_memory_space_constraint(ins[-1], pltpu.HBM)
    return pl.pallas_call(
        kernel,
        out_shape=[x if k in leave else pltpu.VMEM(x.shape, x.dtype) for k, x in enumerate(outs)],
        in_specs=[SMEM] * scalars + [VMEM] * near + [pl.BlockSpec(memory_space=pl.ANY)] * remote,
        out_specs=[VMEM] * len(outs),
        scratch_shapes=list(scratch),
        cost_estimate=pl.CostEstimate(flops=flops, bytes_accessed=moved, transcendentals=0),
        compiler_params=pltpu.CompilerParams(vmem_limit_bytes=LIMIT),
    )(*ins)


def product(left, right, sides):
    return lax.dot_general(left, right, ((sides[:1], sides[1:]), ((), ())), preferred_element_type=F32)


def time_shift(timestep, channel_total):
    half_count = channel_total // 2
    frequency = jnp.exp(-math.log(10000.0) * jnp.arange(half_count, dtype=jnp.float32) / half_count)
    angles = timestep.astype(jnp.float32) * frequency
    return jnp.concatenate([jnp.cos(angles), jnp.sin(angles)])


def swap(block, mask):
    total = lax.axis_size("img") * lax.axis_size("row")
    return lax.ppermute(block, GRID, [(i, i ^ mask) for i in range(total)])


def spots_of(rows):
    image, row = lax.axis_index("img"), lax.axis_index("row")
    return {
        "image": image,
        "core": image & 1,
        "row": row,
        "square": ((image >> 1) & 1) * rows + row,
        "line": image >> 2,
        "plane": image & 3,
    }


def noisy_kernel(rows, timestep, latents, noise, noisy, *edges):
    step = timestep[0]
    index = lax.broadcasted_iota(jnp.int32, (8, 128), 0) * 128 + lax.broadcasted_iota(
        jnp.int32, (8, 128), 1
    )
    low, high = 0.00085**0.5, 0.012**0.5
    beta = (low + index.astype(F32) * ((high - low) / 999.0)) ** 2
    logs = jnp.where(index <= step, jnp.log(1.0 - jnp.where(index < 1000, beta, 0.0)), 0.0)
    total = jnp.sum(jnp.sum(logs, axis=1, keepdims=True), axis=0, keepdims=True)
    level = jnp.exp(total)
    keep, mix = jnp.sqrt(level), jnp.sqrt(1.0 - level)
    height = latents.shape[2]
    for c in range(latents.shape[1]):
        value = (keep * latents[0, c] + mix * noise[0, c]).astype(BF16).astype(F32)
        noisy[c] = value
        head, tail = value[:2].astype(BF16), value[height - 2 :].astype(BF16)
        if rows == 2:
            edges[0][c] = jnp.where(spots_of(rows)["row"] == 0, tail, head)
        else:
            edges[0][c] = tail
            edges[1][c] = head


def condition_kernel(rows, start, hidden, weight, kept, *refs):
    sent, mine, away = refs[: rows - 1], refs[rows - 1], refs[rows]
    window, weights, cond, held, row_sem, sems = refs[rows + 1 :]
    here = spots_of(rows)
    pieces = sems.shape[0]
    depth = weight.shape[0] // pieces
    span = window.shape[0]
    base = jnp.minimum((start[0] >> 4) << 4, hidden.shape[0] - span)
    load = pltpu.make_async_copy(hidden.at[pl.ds(pl.multiple_of(base, 16), span), :], window, row_sem)
    load.start()
    loads = [
        pltpu.make_async_copy(
            weight.at[k * depth : (k + 1) * depth, :], weights.at[k * depth : (k + 1) * depth, :], sems.at[k]
        )
        for k in range(pieces)
    ]
    for one in loads:
        one.start()
    load.wait()
    slot = lax.broadcasted_iota(jnp.int32, (SLOTS, span), 0)
    token = lax.broadcasted_iota(jnp.int32, (SLOTS, span), 1)
    chosen = jnp.where(token == slot + (start[0] - base), 1.0, 0.0).astype(BF16)
    cond[...] = product(chosen, window[...], (1, 0)).astype(BF16)
    half = cond.shape[1] // 2
    left, right = cond[:, :half], cond[:, half:]
    mine[...] = jnp.where(here["core"] == 0, left, right)
    away[...] = jnp.where(here["core"] == 0, right, left)
    total = None
    for k in range(pieces):
        loads[k].wait()
        one = product(cond[:, k * depth : (k + 1) * depth], weights[k * depth : (k + 1) * depth, :], (1, 0))
        total = one if total is None else total + one
    height = SLOTS // rows
    for r in range(rows):
        held[r] = total[r * height : (r + 1) * height]
    kept[...] = held[here["row"]]
    for j in range(1, rows):
        sent[j - 1][...] = held[here["row"] ^ j]


def select_kernel(rows, group_of, *refs):
    lines = len(refs) - 4
    here = spots_of(rows)
    for k in range(4):
        target = here["line"] * 4 + (here["plane"] ^ k)
        chosen = jnp.zeros(refs[0].shape, F32)
        for j in range(lines):
            goes = group_of[(here["line"] ^ j) * 4 + here["plane"]] == target
            chosen = chosen + jnp.where(goes, refs[j][...].astype(F32), 0.0)
        refs[lines + k][...] = chosen.astype(BF16)


def front_kernel(rows_total, noisy, *refs):
    far = refs[:-12]
    shift, in_weight, query_weight, source, acts, hid, query = refs[-12:-5]
    patches, res_weight, ends, tails, sem = refs[-5:]
    load = pltpu.make_async_copy(source, res_weight, sem)
    load.start()
    rows, cols = noisy.shape[1:]
    cells = rows * cols
    row = lax.axis_index("row")
    inner, outer = row > 0, row < rows_total - 1
    above = jnp.where(inner, far[0][...].astype(F32), 0.0)
    below = jnp.where(outer, far[-1][...].astype(F32), 0.0)
    lane = lax.broadcasted_iota(jnp.int32, (noisy.shape[0], cols), 1)
    depth = noisy.shape[0]
    for r in range(rows + 4):
        if r < 2:
            line = above[:, r]
        elif r < rows + 2:
            line = noisy[:, r - 2]
        else:
            line = below[:, r - rows - 2]
        turned = [
            jnp.where(lane == 0, 0.0, pltpu.roll(line, 1, 1)),
            line,
            jnp.where(lane == cols - 1, 0.0, pltpu.roll(line, cols - 1, 1)),
        ]
        for a in range(3):
            if 0 <= r - a < rows + 2:
                for b in range(3):
                    k = 3 * a + b
                    patches[k * depth : (k + 1) * depth, (r - a) * cols : (r - a + 1) * cols] = turned[b]
    first = product(in_weight[...], patches[...].astype(BF16), (0, 0))
    act = jax.nn.silu(first + shift[...])
    lane = lax.broadcasted_iota(jnp.int32, (act.shape[0], cols), 1)
    for r in range(rows + 2):
        band = act[:, r * cols : (r + 1) * cols]
        if r == 0:
            band = jnp.where(inner, band, 0.0)
        if r == rows + 1:
            band = jnp.where(outer, band, 0.0)
        spot = slice(r * cols, (r + 1) * cols)
        acts[1, :, spot] = band.astype(BF16)
        acts[0, :, spot] = jnp.where(lane == 0, 0.0, pltpu.roll(band, 1, 1)).astype(BF16)
        acts[2, :, spot] = jnp.where(lane == cols - 1, 0.0, pltpu.roll(band, cols - 1, 1)).astype(BF16)
    total = first[:, cols : cols + cells]
    load.wait()
    channels = act.shape[0]
    main = channels // 256 * 256
    left = channels - main
    for k in range(9):
        a, b = k // 3, k % 3
        total = total + product(
            res_weight[k, :, :main], acts[b, :main, a * cols : a * cols + cells], (1, 0)
        )
        ends[:, k * left : (k + 1) * left] = res_weight[k, :, main:]
        tails[k * left : (k + 1) * left, :] = acts[b, main:, a * cols : a * cols + cells]
    total = total + product(ends[...], tails[...], (1, 0))
    low = total.astype(BF16)
    hid[...] = low
    query[...] = product(query_weight[...], low, (1, 0)).astype(BF16)


def attention_kernel(rows, query, hid, upstream, query_weight, out_weight, *refs):
    bands = refs[:rows]
    block_out, kept, grad_hid, query_grad, out_grad = refs[rows : rows + 5]
    sent = refs[rows + 5 : 2 * rows + 4]
    grad_att, attended, grad_query, held, pairs, grad_pairs, lows, grads = refs[2 * rows + 4 :]
    cells = hid.shape[1]
    chunk = 256 if cells % 256 == 0 else cells
    channels = hid.shape[0]
    here = spots_of(rows)
    height = SLOTS // rows
    for j in range(rows):
        held[here["row"] ^ j] = bands[j][...]
    for r in range(rows):
        pairs[r * height : (r + 1) * height, :] = held[r]
    scale = HEAD_DIM**-0.5
    grad_att[...] = product(out_weight[...], upstream[...], (0, 0)).astype(BF16)
    for h in range(channels // HEAD_DIM):
        spot = slice(h * HEAD_DIM, (h + 1) * HEAD_DIM)
        keys = pairs[:, h * HEAD_DIM : (h + 1) * HEAD_DIM]
        vals = pairs[:, channels + h * HEAD_DIM : channels + (h + 1) * HEAD_DIM]
        for k in range(0, cells, chunk):
            lanes = slice(k, k + chunk)
            score = product(keys, query[spot, lanes], (1, 0)) * scale
            grown = jnp.exp(score - jnp.max(score, axis=0, keepdims=True))
            probs = grown / jnp.sum(grown, axis=0, keepdims=True)
            low = probs.astype(BF16)
            lows[:, lanes] = low
            attended[spot, lanes] = product(vals, low, (0, 0)).astype(BF16)
            grad_prob = product(vals, grad_att[spot, lanes], (1, 0))
            inner = jnp.sum(probs * grad_prob, axis=0, keepdims=True)
            grad_score = (scale * probs * (grad_prob - inner)).astype(BF16)
            grads[:, lanes] = grad_score
            grad_query[spot, lanes] = product(keys, grad_score, (0, 0)).astype(BF16)
        grad_pairs[:, h * HEAD_DIM : (h + 1) * HEAD_DIM] = product(grads[...], query[spot, :], (1, 1))
        grad_pairs[:, channels + h * HEAD_DIM : channels + (h + 1) * HEAD_DIM] = product(
            lows[...], grad_att[spot, :], (1, 1)
        )
    kept[...] = grad_pairs[pl.ds(pl.multiple_of(here["row"] * height, 8), height), :]
    for j in range(1, rows):
        spot = pl.ds(pl.multiple_of((here["row"] ^ j) * height, 8), height)
        sent[j - 1][...] = grad_pairs[spot, :].astype(BF16)
    block_out[...] = (
        hid[...].astype(F32) + product(out_weight[...], attended[...], (1, 0))
    ).astype(BF16)
    grad_hid[...] = (
        upstream[...].astype(F32) + product(query_weight[...], grad_query[...], (0, 0))
    ).astype(BF16)
    query_grad[...] = product(grad_query[...], hid[...], (1, 1))
    out_grad[...] = product(upstream[...], attended[...], (1, 1))


def filter_kernel(rows, cols, grad_hid, acts, query_grad, out_grad, kept, sent, whole, pair, wide):
    channels, cells = grad_hid.shape
    for k in range(9):
        a, b = k // 3, k % 3
        pair[k * channels : (k + 1) * channels, :] = acts[b, :, a * cols : a * cols + cells]
    for k in range(0, 9 * channels, 256):
        ends = min(k + 256, 9 * channels)
        whole[:, k:ends] = product(grad_hid[...], pair[k:ends, :], (1, 1))
    edge = 9 * channels
    base = edge // 128 * 128
    lead = edge - base
    wide[:, :channels] = query_grad[...]
    turned = pltpu.roll(wide[...], lead, 1) if lead else wide[...]
    lane = lax.broadcasted_iota(jnp.int32, (channels, 128), 1)
    whole[:, base : base + 128] = jnp.where(lane < lead, whole[:, base : base + 128], turned[:, :128])
    whole[:, base + 128 : edge + channels] = turned[:, 128 : lead + channels]
    whole[:, edge + channels : edge + 2 * channels] = out_grad[...]
    rest = whole.shape[1] - edge - 2 * channels
    if rest:
        whole[:, edge + 2 * channels :] = jnp.zeros((channels, rest), F32)
    half = channels // 2
    core = spots_of(rows)["core"]
    pieces, height = kept.shape[:2]
    for q in range(pieces):
        if height % 8 == 0:
            kept[q] = whole[pl.ds(pl.multiple_of(core * half + q * height, 8), height), :]
            away = whole[pl.ds(pl.multiple_of((1 - core) * half + q * height, 8), height), :]
        else:
            low = whole[q * height : (q + 1) * height, :]
            high = whole[half + q * height : half + (q + 1) * height, :]
            kept[q] = jnp.where(core == 0, low, high)
            away = jnp.where(core == 0, high, low)
        sent[q] = away.astype(BF16)


def square_kernel(rows, kept, came, own, *outs):
    here = spots_of(rows)["square"]
    own[...] = kept[here] + came[here].astype(F32)
    for j in range(1, 2 * rows):
        outs[j - 1][...] = (kept[here ^ j] + came[here ^ j].astype(F32)).astype(BF16)


def line_kernel(rows, count, near, *refs):
    here = spots_of(rows)["line"]
    total = refs[0][...]
    for one in refs[1:near]:
        total = total + one[...].astype(F32)
    own, outs, held = refs[near], refs[near + 1 : near + count], refs[near + count]
    slot = total.shape[1] // count
    held[...] = total
    own[...] = held[:, pl.ds(pl.multiple_of(here * slot, 128), slot)]
    for j in range(1, count):
        spot = pl.ds(pl.multiple_of((here ^ j) * slot, 128), slot)
        outs[j - 1][...] = held[:, spot].astype(BF16)


def unpack_kernel(rows, lines, *refs):
    count = 2 * rows
    here = spots_of(rows)
    parts = refs[: 2 * count]
    res, query, out, whole, *spare = refs[2 * count :]
    height = parts[0].shape[0]
    slot = parts[0].shape[1] // lines
    for c in range(2):
        for j in range(count):
            piece = parts[c * count + j][...].astype(F32)
            spot = (here["core"] ^ c) * count + (here["square"] ^ j)
            for z in range(lines):
                lanes = pl.ds(pl.multiple_of((here["line"] ^ z) * slot, 128), slot)
                one = piece[:, z * slot : (z + 1) * slot]
                if spare:
                    spare[0][spot, :, lanes] = one
                else:
                    whole[pl.ds(pl.multiple_of(spot * height, 8), height), lanes] = one
    if spare:
        for q in range(2 * count):
            whole[q * height : (q + 1) * height, :] = spare[0][q]
    channels = query.shape[0]
    for t in range(11):
        start = t * channels
        base = start // 128 * 128
        lead = start - base
        if lead:
            span = -(-(lead + channels) // 128) * 128
            piece = pltpu.roll(whole[:, base : base + span], span - lead, 1)[:, :channels]
        else:
            piece = whole[:, start : start + channels]
        piece = piece.astype(BF16)
        if t < 9:
            res[t] = piece
        elif t == 9:
            query[...] = piece
        else:
            out[...] = piece


def line_mask(j, rows):
    return j * 4 * rows


def square_mask(j, rows):
    return j // rows * 2 * rows + j % rows


def filter_step(grad_hid, acts, query_grad, out_grad, cols, rows, lines):
    channels, cells = grad_hid.shape
    slot = -(-11 * channels // (128 * lines)) * 128
    width = slot * lines
    half = channels // 2
    return call(
        functools.partial(filter_kernel, rows, cols),
        [((2 * rows, half // rows // 2, width), F32), ((2 * rows, half // rows // 2, width), BF16)],
        [grad_hid, acts, query_grad, out_grad],
        [
            pltpu.VMEM((channels, width), F32),
            pltpu.VMEM((9 * channels, cells), BF16),
            pltpu.VMEM((channels, -(-channels // 128) * 128), F32),
        ],
        flops=18 * channels * channels * cells,
    )


def square_step(kept, came, rows):
    squares, height, width = kept.shape
    return call(
        functools.partial(square_kernel, rows),
        [((height, width), F32)] + [((height, width), BF16)] * (squares - 1),
        [kept, came],
    )


def line_step(own, near, rows, lines):
    height, width = own.shape
    slot = width // lines
    return call(
        functools.partial(line_kernel, rows, lines, len(near) + 1),
        [((height, slot), F32)] + [((height, slot), BF16)] * (lines - 1),
        [own, *near],
        [pltpu.VMEM((height, width), F32)],
    )


def unpack_step(mine, other, channels, rows, lines):
    height = mine[0].shape[0]
    res, query, out = call(
        functools.partial(unpack_kernel, rows, lines),
        [((9, channels, channels), BF16), ((channels, channels), BF16), ((channels, channels), BF16)],
        [*mine, *other],
        [pltpu.VMEM((channels, mine[0].shape[1]), F32)]
        + [pltpu.VMEM((channels // height, height, mine[0].shape[1]), F32)] * (height % 8 > 0),
        leave=(0, 1, 2),
    )
    return res.reshape(3, 3, channels, channels), query, out


def gather_kernel(rows, lines, group_of, *refs):
    count = 4 * rows
    parts = refs[:count]
    image_rows, all_rows, held = refs[count:]
    image, row = lax.axis_index("img"), lax.axis_index("row")
    for k in range(count):
        for z in range(lines):
            held[k * lines + z] = parts[k][z]

    def spot(source, r):
        v = group_of[source] ^ image
        return (((v & 1) * 2 + ((v >> 1) & 1)) * rows + (row ^ r)) * lines + (v >> 2)

    for r in range(rows):
        image_rows[r] = held[spot(image, r)]
    for x in range(2):
        for z in range(lines):
            for c in range(2):
                p = (x * lines + z) * 2 + c
                for r in range(rows):
                    all_rows[p * rows + r] = held[spot(image ^ (z * 4 + x * 2 + c), r)]


def place_kernel(start, image, weight, blank, out, window, sem):
    span = window.shape[0]
    base = jnp.minimum((start[0] >> 4) << 4, out.shape[0] - span)
    token = lax.broadcasted_iota(jnp.int32, (span, SLOTS), 0)
    slot = lax.broadcasted_iota(jnp.int32, (span, SLOTS), 1)
    chosen = jnp.where(token == slot + (start[0] - base), 1.0, 0.0).astype(BF16)
    rows = product(image[...], weight[...], (1, 1)).astype(BF16)
    window[...] = product(chosen, rows, (1, 0)).astype(BF16)
    store = pltpu.make_async_copy(window, out.at[pl.ds(pl.multiple_of(base, 16), span), :], sem)
    store.start()
    store.wait()


def join_kernel(flip, part, *refs):
    out, sems = refs[-2:]
    width = part.shape[0]
    core = (lax.axis_index("img") & 1) ^ flip
    count = sems.shape[0]
    depth = width // count
    stores = []
    for k in range(count):
        target = out.at[pl.ds(pl.multiple_of(core * width + k * depth, 8), depth), :]
        stores.append(pltpu.make_async_copy(part.at[k * depth : (k + 1) * depth, :], target, sems.at[k]))
    for one in stores:
        one.start()
    for one in stores:
        one.wait()


def join_step(flip, part, base):
    width, pair_width = part.shape
    spare = pl.BlockSpec(memory_space=pl.ANY)
    return pl.pallas_call(
        functools.partial(join_kernel, flip),
        out_shape=jax.ShapeDtypeStruct((2 * width, pair_width), BF16),
        in_specs=[VMEM] + [spare] * len(base),
        out_specs=spare,
        scratch_shapes=[pltpu.SemaphoreType.DMA((4 if width % 64 == 0 else 1,))],
        input_output_aliases={1: 0} if base else {},
        compiler_params=pltpu.CompilerParams(vmem_limit_bytes=LIMIT),
    )(near_core(part), *base)


def blank_kernel(out, zeros, sems):
    zeros[...] = jnp.zeros(zeros.shape, zeros.dtype)
    depth = zeros.shape[0]
    count = out.shape[0] // depth
    stores = [
        pltpu.make_async_copy(zeros, out.at[k * depth : (k + 1) * depth, :], sems.at[k]) for k in range(count)
    ]
    for one in stores:
        one.start()
    for one in stores:
        one.wait()


def shards(
    llm_hidden,
    slot_start,
    image_group,
    timesteps,
    latents,
    noise,
    kv_weight,
    in_weight,
    res_weight,
    query_weight,
    out_weight,
    cotangent,
):
    rows = lax.axis_size("row")
    images = lax.axis_size("img")
    lines = images // 4
    channels = in_weight.shape[2]
    row_count, col_count = latents.shape[2:]
    cells = row_count * col_count
    tokens, features = llm_hidden.shape
    pair_width = kv_weight.shape[1]
    height = SLOTS // rows
    half = features // 2

    depth = latents.shape[1]
    noisy, *edges = call(
        functools.partial(noisy_kernel, rows),
        [((depth, row_count, col_count), F32)] + [((depth, 2, col_count), BF16)] * (1 if rows == 2 else 2),
        [timesteps, latents, noise],
        scalars=1,
    )
    if rows == 2:
        far = [lax.ppermute(edges[0], "row", [(0, 1), (1, 0)])]
    else:
        far = [
            lax.ppermute(edges[0], "row", [(i, i + 1) for i in range(rows - 1)]),
            lax.ppermute(edges[1], "row", [(i + 1, i) for i in range(rows - 1)]),
        ]

    span = min(SLOTS + 16, tokens)
    pieces = 4 if features % 512 == 0 else 1
    kept, *rest = pl.pallas_call(
        functools.partial(condition_kernel, rows),
        out_shape=[jax.ShapeDtypeStruct((height, pair_width), F32)] * rows
        + [jax.ShapeDtypeStruct((SLOTS, half), BF16)] * 2,
        in_specs=[SMEM, pl.BlockSpec(memory_space=pl.ANY), pl.BlockSpec(memory_space=pl.ANY)],
        out_specs=[VMEM] * (rows + 2),
        scratch_shapes=[
            pltpu.VMEM((span, features), BF16),
            pltpu.VMEM((features, pair_width), BF16),
            pltpu.VMEM((SLOTS, features), BF16),
            pltpu.VMEM((rows, height, pair_width), F32),
            pltpu.SemaphoreType.DMA,
            pltpu.SemaphoreType.DMA((pieces,)),
        ],
        cost_estimate=pl.CostEstimate(
            flops=2 * SLOTS * features * pair_width,
            bytes_accessed=2 * features * (pair_width + 3 * SLOTS),
            transcendentals=0,
        ),
        name="condition",
    )(slot_start, llm_hidden, kv_weight)
    sent, mine, away = rest[: rows - 1], rest[rows - 1], rest[rows]

    band = kept
    for j in range(1, rows):
        band = band + swap(sent[j - 1], j)
    band = band.astype(BF16)
    column = [band] + [swap(band, line_mask(j, rows)) for j in range(1, lines)]
    upstream = cotangent[0].reshape(channels, cells)
    shift = time_shift(timesteps[0], channels)[:, None]
    in_flat = in_weight.transpose(0, 1, 3, 2).reshape(-1, channels)
    column[0], upstream, shift, in_flat = lax.optimization_barrier((column[0], upstream, shift, in_flat))
    plane = call(
        functools.partial(select_kernel, rows), [((height, pair_width), BF16)] * 4, [image_group, *column], scalars=1
    )
    band = plane[0].astype(F32)
    for k in range(1, 4):
        band = band + swap(plane[k], k * rows).astype(F32)
    band = band.astype(BF16)
    bands = [band] + [swap(band, j) for j in range(1, rows)]

    other = swap(away, rows)
    block = jnp.concatenate([mine, other])
    near = [block] + [swap(block, line_mask(j, rows)) for j in range(1, lines)]

    acts, hid, query = call(
        functools.partial(front_kernel, rows),
        [
            ((3, channels, cells + 2 * col_count), BF16),
            ((channels, cells), BF16),
            ((channels, cells), BF16),
        ],
        [
            noisy,
            *far,
            shift,
            in_flat,
            query_weight,
            res_weight.reshape(9, channels, channels),
        ],
        [
            pltpu.VMEM((9 * depth, cells + 2 * col_count), F32),
            pltpu.VMEM((9, channels, channels), BF16),
            pltpu.VMEM((channels, 9 * (channels % 256)), BF16),
            pltpu.VMEM((9 * (channels % 256), cells), BF16),
            pltpu.SemaphoreType.DMA,
        ],
        remote=1,
        flops=20 * channels * channels * cells,
    )
    block_out, kept, grad_hid, query_grad, out_grad, *sent = call(
        functools.partial(attention_kernel, rows),
        [
            ((channels, cells), BF16),
            ((height, pair_width), F32),
            ((channels, cells), BF16),
            ((channels, channels), F32),
            ((channels, channels), F32),
        ]
        + [((height, pair_width), BF16)] * (rows - 1),
        [query, hid, upstream, query_weight, out_weight, *bands],
        [pltpu.VMEM((channels, cells), BF16)] * 3
        + [
            pltpu.VMEM((rows, height, pair_width), BF16),
            pltpu.VMEM((SLOTS, pair_width), BF16),
            pltpu.VMEM((SLOTS, pair_width), F32),
            pltpu.VMEM((SLOTS, cells), BF16),
            pltpu.VMEM((SLOTS, cells), BF16),
        ],
        flops=10 * channels * channels * cells + 12 * channels * SLOTS * cells,
    )
    grad_band = kept
    for j in range(1, rows):
        grad_band = grad_band + swap(sent[j - 1], j).astype(F32)
    grad_band = grad_band.astype(BF16)
    kept, sent = filter_step(grad_hid, acts, query_grad, out_grad, col_count, rows, lines)
    own, *outs = square_step(kept, swap(sent, rows), rows)
    blank = pl.pallas_call(
        blank_kernel,
        out_shape=jax.ShapeDtypeStruct((tokens, features), BF16),
        out_specs=pl.BlockSpec(memory_space=pl.ANY),
        scratch_shapes=[
            pltpu.VMEM((tokens // 8, features), BF16),
            pltpu.SemaphoreType.DMA((8,)),
        ],
        name="blank",
    )()
    block_out = block_out.reshape(1, channels, row_count, col_count)
    own, block_out = lax.optimization_barrier((own, block_out))
    squares = 2 * rows
    came = [swap(outs[j - 1], square_mask(j, rows)) for j in range(1, squares)]
    own, *outs = line_step(own, came, rows, lines)
    came = [swap(outs[j - 1], line_mask(j, rows)) for j in range(1, lines)]
    weight_scale = (images * rows * cells) ** (-0.5)
    for one in came:
        own = own + one.astype(F32)
    final = (own * weight_scale).astype(BF16)
    far = [swap(final, line_mask(j, rows)) for j in range(1, lines)]

    column = jnp.stack([grad_band] + [swap(grad_band, line_mask(j, rows)) for j in range(1, lines)])
    parts = [column] + [swap(column, square_mask(j, rows)) for j in range(1, squares)]
    parts = parts + [swap(one, rows) for one in parts]
    image_rows, all_rows = call(
        functools.partial(gather_kernel, rows, lines),
        [((rows, height, pair_width), BF16), ((images * rows, height, pair_width), BF16)],
        [image_group, *parts],
        [pltpu.VMEM((4 * rows * lines, height, pair_width), BF16)],
        scalars=1,
    )
    all_rows = all_rows.reshape(images * SLOTS, pair_width)
    grad_hidden = pl.pallas_call(
        place_kernel,
        out_shape=jax.ShapeDtypeStruct((tokens, features), BF16),
        in_specs=[SMEM, VMEM, VMEM, pl.BlockSpec(memory_space=pl.ANY)],
        out_specs=pl.BlockSpec(memory_space=pl.ANY),
        scratch_shapes=[pltpu.VMEM((span, features), BF16), pltpu.SemaphoreType.DMA],
        input_output_aliases={3: 0},
        compiler_params=pltpu.CompilerParams(vmem_limit_bytes=LIMIT),
        name="place",
    )(slot_start, near_core(image_rows.reshape(SLOTS, pair_width)), near_core(kv_weight), blank)
    wide = jnp.concatenate([final, *far], axis=1)
    parts = [wide] + [swap(wide, square_mask(j, rows)) for j in range(1, squares)]

    near_half = images * SLOTS // 2
    across = []
    for j in range(lines):
        if j % 2 and j > 1:
            across.append(swap(across[j - 1], line_mask(1, rows)))
        else:
            across.append(swap(near[j], 2 * rows))
    total = product(jnp.concatenate(near), all_rows[:near_half], (0, 0))
    total = total + product(jnp.concatenate(across), all_rows[near_half:], (0, 0))
    weight_half = (total * (images * SLOTS) ** (-0.5)).astype(BF16)
    came = swap(weight_half, rows)
    grad_kv_weight = join_step(0, weight_half, [])
    grad_kv_weight = join_step(1, came, [grad_kv_weight])
    others = [swap(one, rows) for one in parts]
    grad_res_weight, grad_query_weight, grad_out_weight = unpack_step(
        parts, others, channels, rows, lines
    )
    return (
        block_out,
        grad_hidden,
        grad_kv_weight,
        grad_res_weight,
        grad_query_weight,
        grad_out_weight,
    )


def solution(mesh):
    return jax.shard_map(
        shards,
        mesh=mesh,
        in_specs=(
            P("img", "row"),
            P("img"),
            P(),
            P("img"),
            P("img", None, "row", None),
            P("img", None, "row", None),
            P("row", None),
            P(),
            P(),
            P(),
            P(),
            P("img", None, "row", None),
        ),
        out_specs=(P("img", None, "row", None), P("img", "row"), P("row", None), P(), P(), P()),
        check_vma=False,
    )
```
